128 devices in a mesh: seq: 8 (over y, core), vocab: 16 (over x, z).
Axes of the slice: x: 4, y: 4, z: 4, core: 2. Of those that a mesh axis runs over, the one named last changes fastest.
Arguments:
- hidden: bfloat16 [2, 4096, 2048], P(None, 'seq'), may hold values from -6 to 6
- w_inner: bfloat16 [2, 2048, 2, 4096], P(None, None, None, 'vocab'), may hold values from -0.125 to 0.125
- w_state: bfloat16 [2, 2048, 2, 128], replicated, may hold values from -0.125 to 0.125
- w_step: bfloat16 [2, 2048, 64], P(None, None, 'vocab'), may hold values from -0.125 to 0.125
- step_bias: float32 [2, 64], P(None, 'vocab'), may hold values from -5 to -2
- rate: float32 [2, 64], P(None, 'vocab'), may hold values from 0.01 to 1.5
- skip_gain: float32 [2, 64], P(None, 'vocab'), may hold values from 0.5 to 1.5
- norm_gain: float32 [2, 4096], P(None, 'vocab'), may hold values from 0.1 to 1.9
- w_out: bfloat16 [2, 4096, 2048], P(None, 'vocab'), may hold values from -0.09375 to 0.09375
- final_gain: float32 [2, 2048], replicated, may hold values from 0.1 to 1.9
- head: bfloat16 [2, 2048, 26624], P(None, None, 'vocab'), as said below
- pool: bfloat16 [2, 16, 64, 64, 128], P(None, None, 'vocab'), may hold values from -3 to 3
- targets: int32 [4096], P('seq'), may hold values from 0 to 26623
- segment_ids: int32 [4096], P('seq'), may hold values from 0 to 3, never falling along the last dimension, each value on 1 to 2048 neighbouring positions
- flags: int32 [4], replicated, may hold values from 0 to 1, as said below
- pages: int32 [4], replicated, may hold values from 0 to 15
- live: int32 [16], P('seq'), may hold values 0 or 1
- owners: int32 [4], replicated, may hold values from 0 to 7
Outputs:
- token_diff: float32 [4096], P('seq')
- owned: float32 [8, 4], P('seq')
The draws below stay inside these ranges and needn't reach their ends.
Inputs may be any that keep to these rules, and one draw needn't show every extreme that they name: `segment_ids`: ids never fall along the positions, and every id from 0 to 3 occurs. `flags`: exactly one sequence has flag 0. `head`: each vocabulary column's entries are normal with a scale between 3 and 30 over the square root of 2048.
All inputs are finite; a program needn't handle non-finite values. No bound on the sum of `live` on one device may be relied on, other than what follows from the above.
Results may differ from the reference program's by a relative error of at most 0.029.
Values may be sent and summed in bfloat16 or wider, within the bound.
No kernel may reach another device: no remote copies, remote signals or barrier semaphores. Data moves between devices by JAX's collectives and lax.ppermute only.
A program may use at most 128 MiB of HBM per device.

```python
import math
import jax
import jax.numpy as jnp
import numpy as np
from jax import lax

D = 2048
HEADS = 64
HEAD_DIM = 64
INNER = 4096
STATE = 128
SPAN = 256
VOCAB = 26624
PAGES = 16
TOKENS = 4096
NSEQ = 4
MAXLEN = 2048
NBLK = 16
N_SEQ = 8
N_VOCAB = 16


def draw_head(key, part):
    normal_key = jax.random.fold_in(jax.random.fold_in(key, 11), 0)
    values = jax.random.normal(normal_key, (2, D, VOCAB), jnp.float32) * (3.0 / math.sqrt(D))
    return values.astype(jnp.bfloat16)


def draw_flags(key, part):
    fresh = jax.random.randint(jax.random.fold_in(key, 23), (), 0, NSEQ, jnp.int32)
    return (jnp.arange(NSEQ, dtype=jnp.int32) != fresh).astype(jnp.int32)


def with_ends(result, stream_key, least, high):
    longest = result.shape.index(max(result.shape))
    spots = []
    for shift in (0, 1):
        where = [jax.random.randint(jax.random.fold_in(stream_key, axis), (), 0, length) for axis, length in enumerate(result.shape)]
        where[longest] = (where[longest] + shift) % result.shape[longest]
        spots.append(tuple(where))
    return result.at[spots[0]].set(least).at[spots[1]].set(high)


def steps_of(stream_key, shape, cuts, least, top_value):
    level, own = 1.0, jax.random.fold_in(stream_key, 6)
    for axis_at, blocks in cuts:
        draws = jnp.exp(jax.random.uniform(jax.random.fold_in(own, axis_at), (blocks,), jnp.float32, least / len(cuts), top_value / len(cuts)))
        level = level * jnp.repeat(draws, shape[axis_at] // blocks).reshape([-1 if axis == axis_at else 1 for axis in range(len(shape))])
    return level


def rank_bounds(number_of, lean):
    loads = [(1 << 20) // math.isqrt(standing ** lean) + 1 for standing in range(1, number_of + 1)]
    width = 1 + sum(loads) // (1 << 30)
    return np.cumsum(np.array([max(1, weight // width) for weight in loads]))


def ranked_ids(stream_key, dims, count, lean):
    grid = rank_bounds(count, lean)
    lot = jax.random.randint(jax.random.fold_in(stream_key, 1), dims, 0, int(grid[count - 1]))
    standing = jnp.searchsorted(jnp.asarray(grid, jnp.int32), lot, side="right")
    return jax.random.permutation(jax.random.fold_in(stream_key, 2), count)[standing].astype(jnp.int32)


def length_profile(number_of, total, most, slope):
    loads = [(1 << 20) // math.isqrt(standing ** slope) + 1 for standing in range(2, number_of + 1)]
    rest, counts = total - most - (number_of - 1), [1] * (number_of - 1)
    while rest > 0:
        movable = [i for i in range(number_of - 1) if counts[i] < most]
        whole, remaining = sum([loads[i] for i in movable]), rest
        for i in movable:
            addition = min(most - counts[i], max(1, remaining * loads[i] // whole), rest)
            counts[i] = counts[i] + addition
            rest = rest - addition
    return np.array([most] + counts)


def ragged_sizes(key, number_of, total, bound, skew):
    if number_of == 2:
        one = jax.random.randint(key, (), max(1, total - bound), min(bound, total - 1) + 1)
        return jnp.stack([one, total - one])
    tallies = jnp.asarray(length_profile(number_of, total, bound, skew), jnp.int32)
    pairs = (number_of - 1) // 2
    giver, receiver = tallies[1:1 + 2 * pairs:2], tallies[2:2 + 2 * pairs:2]
    room = jnp.minimum(giver - 1, bound - receiver)
    moved = jax.random.randint(jax.random.fold_in(key, 1), (pairs,), 0, 1 << 20) % (room + 1)
    tallies = tallies.at[1:1 + 2 * pairs:2].set(giver - moved).at[2:2 + 2 * pairs:2].set(receiver + moved)
    return tallies[jax.random.permutation(jax.random.fold_in(key, 2), number_of)]


def normal_values(rng, dims, deviation, reach, cuts=(), kind=jnp.bfloat16):
    values = jax.random.normal(rng, dims, jnp.float32) * deviation
    if len(cuts) > 0:
        values = steps_of(rng, dims, cuts, -0.22, 0.18) * values
    return jnp.clip(values, min=-reach, max=reach).astype(kind)


def setup_inputs(seed: int = 0) -> dict:
    keys = jax.random.split(jax.random.key(seed), 19)
    return {
        "hidden": normal_values(keys[0], (2, TOKENS, D), 1.0, 6.0, ((1, 8),)),
        "w_inner": normal_values(keys[1], (2, D, 2, INNER), D ** -0.5, 0.125, ((3, 16),)),
        "w_state": normal_values(keys[2], (2, D, 2, STATE), D ** -0.5, 0.125),
        "w_step": normal_values(keys[3], (2, D, HEADS), D ** -0.5, 0.125, ((2, 16),)),
        "step_bias": jnp.clip(-5.0 + 3.0 * jax.random.uniform(keys[4], (2, HEADS), jnp.float32) ** steps_of(keys[4], (2, HEADS), ((1, 16),), -0.2, 0.2), -5.0, -2.0),
        "rate": jnp.clip(jnp.exp(math.log(1.5) - 5.0106353 * jax.random.uniform(keys[5], (2, HEADS), jnp.float32) ** steps_of(keys[5], (2, HEADS), ((1, 16),), -0.2, 0.2)), 0.01, 1.5),
        "skip_gain": jnp.clip(0.5 + 1.0 * jax.random.uniform(keys[6], (2, HEADS), jnp.float32) ** steps_of(keys[6], (2, HEADS), ((1, 16),), -0.2, 0.2), 0.5, 1.5),
        "norm_gain": jnp.clip(1.0 + 0.18 * jax.random.normal(keys[7], (2, INNER), jnp.float32), 0.1, 1.9),
        "w_out": normal_values(keys[8], (2, INNER, D), INNER ** -0.5, 0.09375, ((1, 16),)),
        "final_gain": jnp.clip(1.0 + 0.18 * jax.random.normal(keys[9], (2, D), jnp.float32), 0.1, 1.9),
        "head": draw_head(jax.random.fold_in(keys[18], 71), 0),
        "pool": normal_values(keys[11], (2, PAGES, HEADS, HEAD_DIM, STATE), 0.5, 3.0, ((2, 16),)),
        "targets": with_ends(ranked_ids(keys[12], (TOKENS,), VOCAB, 2), jax.random.fold_in(keys[12], 3), 0, VOCAB - 1).astype(jnp.int32),
        "segment_ids": jnp.searchsorted(jnp.cumsum(ragged_sizes(keys[13], NSEQ, TOKENS, MAXLEN, 0)), jnp.arange(TOKENS), side="right").astype(jnp.int32),
        "flags": draw_flags(jax.random.fold_in(keys[18], 71), 0),
        "pages": with_ends(jax.random.randint(keys[15], (NSEQ,), 0, PAGES), jax.random.fold_in(keys[15], 1), 0, PAGES - 1).astype(jnp.int32),
        "live": with_ends((jax.random.randint(keys[16], (NBLK,), 0, 4) < 3).astype(jnp.int32), jax.random.fold_in(keys[16], 1), 0, 1),
        "owners": with_ends(jax.random.randint(keys[17], (NSEQ,), 0, N_SEQ), jax.random.fold_in(keys[17], 1), 0, N_SEQ - 1).astype(jnp.int32),
    }


NORM_EPS = 1e-05
HIGH = lax.Precision.HIGHEST

def block_step(carried, pieces):
    values_in, input_map, output_map, log_decay, step_size, onehot, segment = pieces
    length = values_in.shape[0]
    running = jnp.cumsum(log_decay, axis=0)
    seg_decay = jnp.dot(onehot.T, log_decay, precision=HIGH)
    upto_end = jnp.cumsum(seg_decay, axis=0)
    before = upto_end - seg_decay
    end_rows = jnp.dot(onehot, upto_end, precision=HIGH)
    start_rows = jnp.dot(onehot, before, precision=HIGH)
    places = jnp.arange(length, dtype=jnp.int32)
    allowed = (places[:, None] >= places[None, :]) & (segment[:, None] == segment[None, :])
    log_gap = running.T[:, :, None] - running.T[:, None, :]
    decay_kernel = jnp.exp(jnp.where(allowed[None], log_gap, -jnp.inf))
    scores = jnp.dot(output_map, input_map.T, precision=HIGH)
    weights = decay_kernel * scores[None] * step_size.T[:, None, :]
    mixer_out = jnp.einsum('hts,shp->thp', weights, values_in, precision=HIGH)
    from_state = jnp.einsum('tn,jhpn->tjhp', output_map, carried, precision=HIGH)
    picked = lax.optimization_barrier(jnp.sum(onehot[:, :, None, None] * from_state, axis=1))
    mixer_out = mixer_out + picked * jnp.exp(running - start_rows)[:, :, None]
    retain = jnp.exp(end_rows - running) * step_size
    spread = onehot[:, :, None, None] * (retain[:, None, :, None] * values_in[:, None, :, :])
    added_state = jnp.einsum('tjhp,tn->jhpn', spread, input_map, precision=HIGH)
    carried = jnp.exp(seg_decay)[:, :, None, None] * carried + added_state
    return (carried, mixer_out)

def scan_blocks(values_in, input_map, output_map, log_decay, step_size, onehot, segment, init_state, length):
    turns = values_in.shape[0] // length

    def to_blocks(array):
        return array.reshape((turns, length) + array.shape[1:])
    pieces = tuple((to_blocks(array) for array in (values_in, input_map, output_map, log_decay, step_size, onehot, segment)))
    end_state, outputs = lax.scan(block_step, init_state, pieces)
    return (outputs.reshape(values_in.shape), end_state)

def reference(hidden, w_inner, w_state, w_step, step_bias, rate, skip_gain, norm_gain, w_out, final_gain, head, pool, targets, segment_ids, flags, pages, live, owners):
    seg_onehot = (segment_ids[:, None] == jnp.arange(NSEQ, dtype=jnp.int32)[None, :]).astype(jnp.float32)
    live_rows = jnp.repeat(live.astype(jnp.float32), SPAN)
    group_width = INNER // N_VOCAB
    scores_list = []
    for which_model in range(2):
        tokens_in = hidden[which_model]
        inner_proj = jnp.dot(tokens_in, w_inner[which_model].reshape(D, 2 * INNER), preferred_element_type=jnp.float32)
        gate_in = inner_proj[:, :INNER]
        values_bf = jax.nn.silu(inner_proj[:, INNER:]).astype(jnp.bfloat16)
        values_in = lax.optimization_barrier(values_bf).astype(jnp.float32).reshape(TOKENS, HEADS, HEAD_DIM)
        state_bf = jax.nn.silu(jnp.dot(tokens_in, w_state[which_model].reshape(D, 2 * STATE), preferred_element_type=jnp.float32)).astype(jnp.bfloat16)
        state_proj = lax.optimization_barrier(state_bf).astype(jnp.float32)
        step_size = jax.nn.softplus(jnp.dot(tokens_in, w_step[which_model], preferred_element_type=jnp.float32) + step_bias[which_model][None, :])
        log_decay = -step_size * rate[which_model][None, :]
        init_state = pool[which_model][pages].astype(jnp.float32) * flags.astype(jnp.float32)[:, None, None, None]
        mixer_out, end_state = scan_blocks(values_in, state_proj[:, :STATE], state_proj[:, STATE:], log_decay, step_size, seg_onehot, segment_ids, init_state, SPAN)
        mixer_out = mixer_out + skip_gain[which_model][None, :, None] * values_in
        gated_rows = mixer_out.reshape(TOKENS, INNER) * jax.nn.silu(gate_in)
        mean_square = lax.optimization_barrier(jnp.mean(gated_rows * gated_rows, axis=1, keepdims=True))
        mixed_rows = (gated_rows * lax.rsqrt(mean_square + NORM_EPS) * norm_gain[which_model][None, :]).astype(jnp.bfloat16)
        weights_out = w_out[which_model]

        def add_group(running, group_index):
            part_rows = lax.dynamic_slice_in_dim(mixed_rows, group_index * group_width, group_width, 1)
            part_weights = lax.dynamic_slice_in_dim(weights_out, group_index * group_width, group_width, 0)
            rounded = lax.optimization_barrier(jnp.dot(part_rows, part_weights, preferred_element_type=jnp.float32).astype(jnp.bfloat16))
            return (running + rounded.astype(jnp.float32), None)
        out_sum, unused = lax.scan(add_group, jnp.zeros((TOKENS, D), jnp.float32), jnp.arange(N_VOCAB, dtype=jnp.int32))
        residual = tokens_in.astype(jnp.float32) + out_sum
        normed = (residual * lax.rsqrt(lax.optimization_barrier(jnp.mean(residual * residual, axis=1, keepdims=True)) + NORM_EPS) * final_gain[which_model][None, :]).astype(jnp.bfloat16)
        head_model = head[which_model]

        def block_score(pieces):
            row_block, target_block = pieces
            logits = jnp.dot(row_block, head_model, preferred_element_type=jnp.float32)
            row_top = lax.optimization_barrier(jnp.max(logits, axis=1))
            row_total = lax.optimization_barrier(jnp.sum(jnp.exp(logits - row_top[:, None]), axis=1))
            chosen = jnp.take_along_axis(logits, target_block[:, None], axis=1)[:, 0]
            return chosen - row_top - jnp.log(row_total)
        scored = lax.map(block_score, (normed.reshape(NBLK, SPAN, D), targets.reshape(NBLK, SPAN)))
        scores_list.append(scored.reshape(TOKENS))
    token_diff = live_rows * (scores_list[0] - scores_list[1])
    per_sequence = jnp.dot(seg_onehot.T, token_diff, precision=HIGH)
    owner_onehot = (owners[None, :] == jnp.arange(N_SEQ, dtype=jnp.int32)[:, None]).astype(jnp.float32)
    owned = owner_onehot * per_sequence[None, :]
    return (token_diff, owned)
```

```python
import functools

import jax
import jax.numpy as jnp
from jax import lax
from jax.experimental import pallas as pl
from jax.experimental.pallas import tpu as pltpu
from jax.sharding import Mesh
from jax.sharding import PartitionSpec as P

NORM_EPS = 1e-05
SPAN = 256
REACH = 4
SEQ = ("y", "core")
VOC = ("x", "z")
F32 = jnp.float32
BF16 = jnp.bfloat16
LOW = -1e30


def silu(v):
    return v / (1.0 + jnp.exp(-v))


def contract(a, b, dims):
    return lax.dot_general(a, b, (dims, ((), ())), preferred_element_type=F32)


def mix_kernel(val_ref, st_ref, stp_ref, bias_ref, rate_ref, skip_ref, seg_ref, y_ref, c_ref, e_ref, pay_ref):
    rows, inner = y_ref.shape
    heads = stp_ref.shape[0]
    wide = inner // heads
    state = c_ref.shape[1]
    seg = seg_ref[...]
    raw = stp_ref[...] + bias_ref[...]
    dt = jnp.maximum(raw, 0.0) + jnp.log1p(jnp.exp(-jnp.abs(raw)))
    la = -dt * rate_ref[...]
    lane = lax.broadcasted_iota(jnp.int32, la.shape, 1)
    run = la
    step = 1
    while step < rows:
        run = run + jnp.where(lane >= step, pltpu.roll(run, step, 1), 0.0)
        step *= 2
    last = jnp.max(seg, axis=1, keepdims=True)
    base = jnp.zeros_like(la)
    for j in range(4):
        base_j = jnp.sum(jnp.where(seg < j, la, 0.0), axis=1, keepdims=True)
        base = jnp.where(seg == j, base_j, base)
    total = jnp.sum(la, axis=1, keepdims=True)
    grow = jnp.exp(run - base)
    keep = jnp.where(seg == last, jnp.exp(jnp.minimum(total - run, 0.0)) * dt, 0.0)
    tail = jnp.exp(jnp.sum(jnp.where(seg == last, la, 0.0), axis=1, keepdims=True))
    cols = jnp.transpose(jnp.concatenate([run, keep], axis=0))
    segf = jnp.broadcast_to(seg.astype(F32), (heads, rows))
    ecol = jnp.transpose(jnp.concatenate([grow, segf], axis=0))
    e_ref[...] = ecol
    values = silu(val_ref[...]).astype(BF16)
    in_map = silu(st_ref[0]).astype(BF16)
    out_map = silu(st_ref[1]).astype(BF16)
    c_ref[...] = out_map
    vf = values.astype(F32)
    kept = jnp.concatenate(
        [vf[:, h * wide : (h + 1) * wide] * cols[:, heads + h : heads + h + 1] for h in range(heads)], axis=1
    ).astype(BF16)
    added = contract(kept, in_map, ((0,), (0,)))
    pay_ref[0:inner, :] = added.astype(BF16)
    high = tail.astype(BF16).astype(F32)
    low = tail - high
    meta = jnp.concatenate(
        [
            jnp.broadcast_to(high, (heads, state)),
            jnp.broadcast_to(low, (heads, state)),
            jnp.broadcast_to(last.astype(F32) + 1.0, (8, state)),
        ],
        axis=0,
    )
    pay_ref[inner : inner + 16, :] = meta.astype(BF16)
    blocks = rows // SPAN
    for i in range(blocks):
        t0 = i * SPAN
        acc = [vf[t0 : t0 + SPAN, h * wide : (h + 1) * wide] * skip_ref[h : h + 1, :] for h in range(heads)]
        for j in range(i + 1):
            s0 = j * SPAN
            scores = contract(out_map[t0 : t0 + SPAN], in_map[s0 : s0 + SPAN], ((1,), (1,)))
            same = ecol[t0 : t0 + SPAN, heads : heads + 1] == segf[0:1, s0 : s0 + SPAN]
            if i == j:
                same = same & (
                    lax.broadcasted_iota(jnp.int32, (SPAN, SPAN), 0)
                    >= lax.broadcasted_iota(jnp.int32, (SPAN, SPAN), 1)
                )
            for h in range(heads):
                gap = cols[t0 : t0 + SPAN, h : h + 1] - run[h : h + 1, s0 : s0 + SPAN]
                weight = jnp.exp(jnp.where(same, gap, LOW)) * (scores * dt[h : h + 1, s0 : s0 + SPAN])
                acc[h] = acc[h] + contract(
                    weight.astype(BF16), values[s0 : s0 + SPAN, h * wide : (h + 1) * wide], ((1,), (0,))
                )
        y_ref[t0 : t0 + SPAN, :] = jnp.concatenate(acc, axis=1)


def mix_local(val, st, stp, bias, rate, skip, seg):
    rows, inner = val.shape
    state = st.shape[2]
    return pl.pallas_call(
        mix_kernel,
        out_shape=(
            jax.ShapeDtypeStruct((rows, inner), F32),
            jax.ShapeDtypeStruct((rows, state), BF16),
            jax.ShapeDtypeStruct((rows, 8), F32),
            jax.ShapeDtypeStruct((inner + 16, state), BF16),
        ),
        cost_estimate=pl.CostEstimate(flops=3 * 10**9, bytes_accessed=3 * 10**6, transcendentals=10**6),
        name="mix_local",
    )(val, st, stp, bias, rate, skip, seg)


def gate_kernel(
    pages_ref, flags_ref, y_ref, gate_ref, c_ref, e_ref, r1_ref, r2_ref, r3_ref, r4_ref,
    p0_ref, p1_ref, p2_ref, p3_ref, gain_ref, w_ref, out_ref,
):
    rows, inner = y_ref.shape
    heads = p0_ref.shape[0]
    wide = inner // heads
    state = c_ref.shape[1]
    width = w_ref.shape[1]
    e_col = e_ref[...]
    seg_col = e_col[:, heads : heads + 1]
    seg_first = e_col[0:1, heads : heads + 1]
    init = [
        p.reshape(inner, state)[...].astype(F32) * flags_ref[j].astype(F32)
        for j, p in enumerate((p0_ref, p1_ref, p2_ref, p3_ref))
    ]
    through = jnp.ones((heads, state), F32)
    parts = [jnp.zeros((wide, state), F32) for _ in range(heads)]
    for r in (r1_ref, r2_ref, r3_ref, r4_ref):
        meta = r[inner : inner + 16, :].astype(F32)
        hit = meta[8:9, :] == seg_first + 1.0
        piece = r[0:inner, :].astype(F32)
        weight = jnp.where(hit, through, 0.0)
        for h in range(heads):
            parts[h] = parts[h] + weight[h : h + 1, :] * piece[h * wide : (h + 1) * wide, :]
        through = jnp.where(hit, through * (meta[0:heads] + meta[heads : 2 * heads]), through)
    prior = jnp.concatenate(parts, axis=0)
    through = jnp.concatenate([jnp.broadcast_to(through[h : h + 1, :], (wide, state)) for h in range(heads)], axis=0)
    out_map = c_ref[...]
    picked = jnp.zeros((rows, inner), F32)
    for j in range(4):
        start = jnp.where(seg_first == float(j), prior + through * init[j], init[j])
        high = start.astype(BF16)
        low = (start - high.astype(F32)).astype(BF16)
        from_state = contract(out_map, high, ((1,), (1,))) + contract(out_map, low, ((1,), (1,)))
        picked = jnp.where(seg_col == float(j), from_state, picked)
    spread = jnp.concatenate([jnp.broadcast_to(e_col[:, h : h + 1], (rows, wide)) for h in range(heads)], axis=1)
    gated = (y_ref[...] + picked * spread) * silu(gate_ref[...])
    square = jnp.sum(gated * gated, axis=1, keepdims=True)
    mixed = (gated * gain_ref[...]).astype(BF16)
    out_ref[:, 0:width] = contract(mixed, w_ref[...], ((1,), (0,))).astype(BF16)
    high = square.astype(BF16).astype(F32)
    mid = (square - high).astype(BF16).astype(F32)
    low = square - high - mid
    lane = lax.broadcasted_iota(jnp.int32, (rows, 128), 1)
    extra = jnp.where(lane == 0, high, jnp.where(lane == 1, mid, jnp.where(lane == 2, low, 0.0)))
    out_ref[:, width : width + 128] = extra.astype(BF16)


def gate_out(m, pages, flags, y, gate, c, e, recv, pool, gain, w_out):
    rows, inner = y.shape
    heads = pool.shape[2]
    state = c.shape[1]
    width = w_out.shape[2]
    whole = lambda a: pl.BlockSpec(a.shape, lambda g, pg, fl: (0,) * a.ndim)
    page = lambda j: pl.BlockSpec(
        (None, None, heads, pool.shape[3], state), lambda g, pg, fl: (m, pg[j], 0, 0, 0)
    )
    return pl.pallas_call(
        gate_kernel,
        grid_spec=pltpu.PrefetchScalarGridSpec(
            num_scalar_prefetch=2,
            grid=(1,),
            in_specs=[whole(y), whole(gate), whole(c), whole(e)]
            + [whole(r) for r in recv]
            + [page(j) for j in range(4)]
            + [
                pl.BlockSpec((1, inner), lambda g, pg, fl: (0, 0)),
                pl.BlockSpec((None, inner, width), lambda g, pg, fl: (m, 0, 0)),
            ],
            out_specs=pl.BlockSpec((rows, width + 128), lambda g, pg, fl: (0, 0)),
        ),
        out_shape=jax.ShapeDtypeStruct((rows, width + 128), BF16),
        cost_estimate=pl.CostEstimate(flops=3 * 10**9, bytes_accessed=6 * 10**6, transcendentals=10**5),
        name="gate_out",
    )(pages, flags, y, gate, c, e, *recv, pool, pool, pool, pool, gain, w_out)


def norm_kernel(units, part_ref, hid_ref, gain_ref, out_ref):
    width = hid_ref.shape[1]
    total = jnp.sum(part_ref[...].astype(F32), axis=0)
    square = total[:, width : width + 1] + total[:, width + 1 : width + 2] + total[:, width + 2 : width + 3]
    res = hid_ref[...].astype(F32) + total[:, 0:width] * lax.rsqrt(square / units + NORM_EPS)
    mean = jnp.sum(res * res, axis=1, keepdims=True) / width
    normed = (res * lax.rsqrt(mean + NORM_EPS) * gain_ref[...]).astype(BF16)
    out_ref[...] = jnp.broadcast_to(normed[None], out_ref.shape)


def final_norm(part, hid, gain, units):
    return pl.pallas_call(
        functools.partial(norm_kernel, float(units)),
        out_shape=jax.ShapeDtypeStruct((part.shape[0],) + hid.shape, BF16),
        cost_estimate=pl.CostEstimate(flops=10**7, bytes_accessed=4 * 10**6, transcendentals=100),
        name="final_norm",
    )(part, hid, gain)


def head_kernel(x_ref, w_ref, tgt_ref, out_ref):
    logits = contract(x_ref[...], w_ref[...], ((1,), (0,)))
    top = jnp.max(logits, axis=1, keepdims=True)
    total = jnp.sum(jnp.exp(logits - top), axis=1, keepdims=True)
    lse = top + jnp.log(total)
    at = lax.broadcasted_iota(jnp.int32, logits.shape, 1)
    chosen = jnp.sum(jnp.where(at == tgt_ref[...], logits, 0.0), axis=1, keepdims=True)
    lane = lax.broadcasted_iota(jnp.int32, (logits.shape[0], 8), 1)
    out_ref[...] = jnp.transpose(jnp.where(lane == 0, lse, jnp.where(lane == 1, chosen, 0.0)))


def head_stats(m, x, head, tgt, tile=256):
    rows, depth = x.shape
    vocab = head.shape[2]
    return pl.pallas_call(
        head_kernel,
        grid=(rows // tile,),
        in_specs=[
            pl.BlockSpec((tile, depth), lambda i: (i, 0)),
            pl.BlockSpec((None, depth, vocab), lambda i: (m, 0, 0)),
            pl.BlockSpec((tile, 1), lambda i: (i, 0)),
        ],
        out_specs=pl.BlockSpec((8, tile), lambda i: (0, i)),
        out_shape=jax.ShapeDtypeStruct((8, rows), F32),
        cost_estimate=pl.CostEstimate(
            flops=2 * rows * depth * vocab, bytes_accessed=2 * depth * vocab, transcendentals=rows * vocab
        ),
        name="head_stats",
    )(x, head, tgt)


def diff_kernel(s0_ref, s1_ref, live_ref, seg_ref, diff_ref, sums_ref):
    scores = []
    for ref in (s0_ref, s1_ref):
        part = ref[...]
        lse = part[:, 0, :]
        top = jnp.max(lse, axis=0, keepdims=True)
        total = top + jnp.log(jnp.sum(jnp.exp(lse - top), axis=0, keepdims=True))
        scores.append(jnp.sum(part[:, 1, :], axis=0, keepdims=True) - total)
    rows = seg_ref.shape[1]
    alive = jnp.where(
        lax.broadcasted_iota(jnp.int32, (1, rows), 1) < SPAN, live_ref[0].astype(F32), live_ref[1].astype(F32)
    )
    diff = alive * (scores[0] - scores[1])
    diff_ref[...] = diff
    which = lax.broadcasted_iota(jnp.int32, (8, rows), 0)
    sums = jnp.sum(jnp.where(which == seg_ref[...], diff, 0.0), axis=1, keepdims=True)
    sums_ref[...] = jnp.broadcast_to(sums, sums_ref.shape)


def token_diffs(s0, s1, live, seg):
    rows = seg.shape[1]
    vm = pl.BlockSpec(memory_space=pltpu.VMEM)
    return pl.pallas_call(
        diff_kernel,
        in_specs=[vm, vm, pl.BlockSpec(memory_space=pltpu.SMEM), vm],
        out_shape=(jax.ShapeDtypeStruct((1, rows), F32), jax.ShapeDtypeStruct((8, 128), F32)),
        name="token_diffs",
    )(s0, s1, live, seg)


def to_all(value, axes):
    count = lax.axis_size(axes)
    return lax.all_to_all(jnp.broadcast_to(value[None], (count,) + value.shape), axes, 0, 0)


def per_device(
    hidden, w_inner, w_state, w_step, step_bias, rate, skip_gain, norm_gain, w_out, final_gain, head, pool,
    targets, segment_ids, flags, pages, live, owners,
):
    rows = targets.shape[0]
    depth = hidden.shape[2]
    inner = w_inner.shape[3]
    group = lax.axis_size(VOC)
    devices = lax.axis_size(SEQ)
    place = lax.axis_index(VOC)
    share = rows // group
    seg = segment_ids.reshape(1, rows)
    tgt = (targets - place * head.shape[2]).reshape(rows, 1)
    stats = []
    for m in range(2):
        tokens = hidden[m]
        proj = jnp.einsum("td,dgi->gti", tokens, w_inner[m], preferred_element_type=F32)
        st = jnp.einsum("td,dgn->gtn", tokens, w_state[m], preferred_element_type=F32)
        stp = jnp.einsum("td,dh->ht", tokens, w_step[m], preferred_element_type=F32)
        wide = inner // rate.shape[1]
        y, c, e, pay = mix_local(
            proj[1], st, stp, step_bias[m][:, None], rate[m][:, None],
            jnp.broadcast_to(skip_gain[m][:, None], (rate.shape[1], wide)), seg,
        )
        recv = [lax.ppermute(pay, SEQ, [(i, i + k) for i in range(devices - k)]) for k in range(1, REACH + 1)]
        part = gate_out(m, pages, flags, y, proj[0], c, e, recv, pool, norm_gain[m][None], w_out)
        part = lax.all_to_all(part.reshape(group, share, depth + 128), VOC, 0, 0)
        mine = lax.dynamic_slice_in_dim(tokens, place * share, share, 0)
        normed = final_norm(part, mine, final_gain[m][None], inner * group)
        normed = lax.all_to_all(normed, VOC, 0, 0).reshape(rows, depth)
        stats.append(to_all(head_stats(m, normed, head, tgt), VOC))
    diff, sums = token_diffs(stats[0], stats[1], live, seg)
    sums = jnp.sum(to_all(sums, SEQ)[:, 0:4, 0], axis=0)
    owned = jnp.where(owners == lax.axis_index(SEQ), sums, 0.0)
    return diff.reshape(rows), owned[None]


def solution(mesh):
    seq, vocab = mesh.devices.shape
    fine = Mesh(mesh.devices.reshape(seq // 2, 2, 4, vocab // 4), ("y", "core", "x", "z"))
    placed = (
        P(None, SEQ, None),
        P(None, None, None, VOC),
        P(),
        P(None, None, VOC),
        P(None, VOC),
        P(None, VOC),
        P(None, VOC),
        P(None, VOC),
        P(None, VOC, None),
        P(),
        P(None, None, VOC),
        P(None, None, VOC, None, None),
        P(SEQ),
        P(SEQ),
        P(),
        P(),
        P(SEQ),
        P(),
    )
    return jax.shard_map(
        per_device, mesh=fine, in_specs=placed, out_specs=(P(SEQ), P(SEQ, None)), check_vma=False
    )
```

```python
import functools

import jax
import jax.numpy as jnp
from jax import lax
from jax.experimental import pallas as pl
from jax.experimental.pallas import tpu as pltpu
from jax.sharding import Mesh
from jax.sharding import PartitionSpec as P

NORM_EPS = 1e-05
SPAN = 256
REACH = 4
SEQ = ("y", "core")
VOC = ("x", "z")
F32 = jnp.float32
BF16 = jnp.bfloat16
LOW = -1e30


def silu(v):
    return v / (1.0 + jnp.exp(-v))


def contract(a, b, dims):
    return lax.dot_general(a, b, (dims, ((), ())), preferred_element_type=F32)


def as_column(row):
    count = row.shape[1]
    spread = jnp.broadcast_to(row, (count, count))
    eye = lax.broadcasted_iota(jnp.int32, spread.shape, 0) == lax.broadcasted_iota(jnp.int32, spread.shape, 1)
    return jnp.sum(jnp.where(eye, spread, 0.0), axis=1, keepdims=True)


def mix_kernel(
    m, tok_ref, wi_ref, ws_ref, wp_ref, bias_ref, rate_ref, skip_ref, seg_ref,
    y_ref, gate_ref, c_ref, e_ref, pay_ref, val_ref, st_ref, stp_ref,
):
    k = pl.program_id(0)
    inner = y_ref.shape[1]

    @pl.when(k == 0)
    def _():
        gate_ref[...] = jnp.zeros_like(gate_ref)
        val_ref[...] = jnp.zeros_like(val_ref)
        st_ref[...] = jnp.zeros_like(st_ref)
        stp_ref[...] = jnp.zeros_like(stp_ref)

    tokens = tok_ref[...]
    gate_ref[...] += contract(tokens, wi_ref[:, 0:inner], ((1,), (0,)))
    val_ref[...] += contract(tokens, wi_ref[:, inner:], ((1,), (0,)))
    st_ref[...] += contract(tokens, ws_ref[...], ((1,), (0,)))
    stp_ref[...] += contract(tokens, wp_ref[...], ((1,), (1,)))

    @pl.when(k == pl.num_programs(0) - 1)
    def _():
        scan_rows(
            m, bias_ref, rate_ref, skip_ref, seg_ref, y_ref, c_ref, e_ref, pay_ref, val_ref, st_ref, stp_ref
        )


def scan_rows(m, bias_ref, rate_ref, skip_ref, seg_ref, y_ref, c_ref, e_ref, pay_ref, val_ref, st_ref, stp_ref):
    rows, inner = y_ref.shape
    heads = bias_ref.shape[1]
    wide = inner // heads
    state = c_ref.shape[1]
    seg = seg_ref[...]
    raw = jnp.transpose(stp_ref[...])[0:heads, :] + as_column(bias_ref[m : m + 1, :])
    dt = jnp.maximum(raw, 0.0) + jnp.log1p(jnp.exp(-jnp.abs(raw)))
    la = -dt * as_column(rate_ref[m : m + 1, :])
    skip = as_column(skip_ref[m : m + 1, :])
    lane = lax.broadcasted_iota(jnp.int32, la.shape, 1)
    run = la
    step = 1
    while step < rows:
        run = run + jnp.where(lane >= step, pltpu.roll(run, step, 1), 0.0)
        step *= 2
    last = jnp.max(seg, axis=1, keepdims=True)
    base = jnp.zeros_like(la)
    for j in range(4):
        base_j = jnp.sum(jnp.where(seg < j, la, 0.0), axis=1, keepdims=True)
        base = jnp.where(seg == j, base_j, base)
    total = jnp.sum(la, axis=1, keepdims=True)
    grow = jnp.exp(run - base)
    keep = jnp.where(seg == last, jnp.exp(jnp.minimum(total - run, 0.0)) * dt, 0.0)
    tail = jnp.exp(jnp.sum(jnp.where(seg == last, la, 0.0), axis=1, keepdims=True))
    cols = jnp.transpose(jnp.concatenate([run, keep], axis=0))
    segf = jnp.broadcast_to(seg.astype(F32), (heads, rows))
    ecol = jnp.transpose(jnp.concatenate([grow, segf], axis=0))
    e_ref[...] = ecol
    values = silu(val_ref[...]).astype(BF16)
    in_map = silu(st_ref[:, 0:state]).astype(BF16)
    out_map = silu(st_ref[:, state:]).astype(BF16)
    c_ref[...] = out_map
    vf = values.astype(F32)
    kept = jnp.concatenate(
        [vf[:, h * wide : (h + 1) * wide] * cols[:, heads + h : heads + h + 1] for h in range(heads)], axis=1
    ).astype(BF16)
    added = contract(kept, in_map, ((0,), (0,)))
    pay_ref[0:inner, :] = added.astype(BF16)
    high = tail.astype(BF16).astype(F32)
    low = tail - high
    meta = jnp.concatenate(
        [
            jnp.broadcast_to(high, (heads, state)),
            jnp.broadcast_to(low, (heads, state)),
            jnp.broadcast_to(last.astype(F32) + 1.0, (8, state)),
        ],
        axis=0,
    )
    pay_ref[inner : inner + 16, :] = meta.astype(BF16)
    blocks = rows // SPAN
    for i in range(blocks):
        t0 = i * SPAN
        acc = [vf[t0 : t0 + SPAN, h * wide : (h + 1) * wide] * skip[h : h + 1, :] for h in range(heads)]
        for j in range(i + 1):
            s0 = j * SPAN
            scores = contract(out_map[t0 : t0 + SPAN], in_map[s0 : s0 + SPAN], ((1,), (1,)))
            same = ecol[t0 : t0 + SPAN, heads : heads + 1] == segf[0:1, s0 : s0 + SPAN]
            if i == j:
                same = same & (
                    lax.broadcasted_iota(jnp.int32, (SPAN, SPAN), 0)
                    >= lax.broadcasted_iota(jnp.int32, (SPAN, SPAN), 1)
                )
            for h in range(heads):
                gap = cols[t0 : t0 + SPAN, h : h + 1] - run[h : h + 1, s0 : s0 + SPAN]
                weight = jnp.exp(jnp.where(same, gap, LOW)) * (scores * dt[h : h + 1, s0 : s0 + SPAN])
                acc[h] = acc[h] + contract(
                    weight.astype(BF16), values[s0 : s0 + SPAN, h * wide : (h + 1) * wide], ((1,), (0,))
                )
        y_ref[t0 : t0 + SPAN, :] = jnp.concatenate(acc, axis=1)


def mix_local(m, hidden, w_inner, w_state, w_step, bias, rate, skip, seg, chunks=4):
    rows, depth = hidden.shape[1:]
    inner = w_inner.shape[2] // 2
    state = w_state.shape[2] // 2
    heads = bias.shape[1]
    deep = depth // chunks
    whole = lambda a: pl.BlockSpec(a.shape, lambda k: (0,) * a.ndim)
    const = lambda shape: pl.BlockSpec(shape, lambda k: (0, 0))
    shapes = ((rows, inner), F32), ((rows, inner), F32), ((rows, state), BF16), ((rows, 2 * heads), F32), (
        (inner + 16, state), BF16)
    return pl.pallas_call(
        functools.partial(mix_kernel, m),
        grid=(chunks,),
        in_specs=[
            pl.BlockSpec((None, rows, deep), lambda k: (m, 0, k)),
            pl.BlockSpec((None, deep, 2 * inner), lambda k: (m, k, 0)),
            pl.BlockSpec((None, deep, 2 * state), lambda k: (m, k, 0)),
            pl.BlockSpec((None, heads, deep), lambda k: (m, 0, k)),
            whole(bias), whole(rate), whole(skip), whole(seg),
        ],
        out_specs=[const(shape) for shape, _ in shapes],
        out_shape=[jax.ShapeDtypeStruct(shape, kind) for shape, kind in shapes],
        scratch_shapes=[
            pltpu.VMEM((rows, inner), F32), pltpu.VMEM((rows, 2 * state), F32), pltpu.VMEM((rows, heads), F32)
        ],
        cost_estimate=pl.CostEstimate(flops=5 * 10**9, bytes_accessed=8 * 10**6, transcendentals=10**6),
        name="mix_local",
    )(hidden, w_inner, w_state, w_step, bias, rate, skip, seg)


def gate_kernel(
    m, pages_ref, flags_ref, y_ref, gate_ref, c_ref, e_ref, r1_ref, r2_ref, r3_ref, r4_ref,
    p0_ref, p1_ref, p2_ref, p3_ref, gain_ref, w_ref, out_ref,
):
    rows, inner = y_ref.shape
    heads = p0_ref.shape[0]
    wide = inner // heads
    state = c_ref.shape[1]
    width = w_ref.shape[1]
    e_col = e_ref[...]
    seg_col = e_col[:, heads : heads + 1]
    seg_first = e_col[0:1, heads : heads + 1]
    init = [
        p.reshape(inner, state)[...].astype(F32) * flags_ref[j].astype(F32)
        for j, p in enumerate((p0_ref, p1_ref, p2_ref, p3_ref))
    ]
    through = jnp.ones((heads, state), F32)
    parts = [jnp.zeros((wide, state), F32) for _ in range(heads)]
    for r in (r1_ref, r2_ref, r3_ref, r4_ref):
        meta = r[inner : inner + 16, :].astype(F32)
        hit = meta[8:9, :] == seg_first + 1.0
        piece = r[0:inner, :].astype(F32)
        weight = jnp.where(hit, through, 0.0)
        for h in range(heads):
            parts[h] = parts[h] + weight[h : h + 1, :] * piece[h * wide : (h + 1) * wide, :]
        through = jnp.where(hit, through * (meta[0:heads] + meta[heads : 2 * heads]), through)
    prior = jnp.concatenate(parts, axis=0)
    through = jnp.concatenate([jnp.broadcast_to(through[h : h + 1, :], (wide, state)) for h in range(heads)], axis=0)
    out_map = c_ref[...]
    picked = jnp.zeros((rows, inner), F32)
    for j in range(4):
        start = jnp.where(seg_first == float(j), prior + through * init[j], init[j])
        high = start.astype(BF16)
        low = (start - high.astype(F32)).astype(BF16)
        from_state = contract(out_map, high, ((1,), (1,))) + contract(out_map, low, ((1,), (1,)))
        picked = jnp.where(seg_col == float(j), from_state, picked)
    spread = jnp.concatenate([jnp.broadcast_to(e_col[:, h : h + 1], (rows, wide)) for h in range(heads)], axis=1)
    gated = (y_ref[...] + picked * spread) * silu(gate_ref[...])
    square = jnp.sum(gated * gated, axis=1, keepdims=True)
    mixed = (gated * gain_ref[m : m + 1, :]).astype(BF16)
    out_ref[:, 0:width] = contract(mixed, w_ref[...], ((1,), (0,))).astype(BF16)
    high = square.astype(BF16).astype(F32)
    mid = (square - high).astype(BF16).astype(F32)
    low = square - high - mid
    lane = lax.broadcasted_iota(jnp.int32, (rows, 128), 1)
    extra = jnp.where(lane == 0, high, jnp.where(lane == 1, mid, jnp.where(lane == 2, low, 0.0)))
    out_ref[:, width : width + 128] = extra.astype(BF16)


def gate_out(m, pages, flags, y, gate, c, e, recv, pool, gain, w_out):
    rows, inner = y.shape
    heads = pool.shape[2]
    state = c.shape[1]
    width = w_out.shape[2]
    whole = lambda a: pl.BlockSpec(a.shape, lambda g, pg, fl: (0,) * a.ndim)
    page = lambda j: pl.BlockSpec(
        (None, None, heads, pool.shape[3], state), lambda g, pg, fl: (m, pg[j], 0, 0, 0)
    )
    return pl.pallas_call(
        functools.partial(gate_kernel, m),
        grid_spec=pltpu.PrefetchScalarGridSpec(
            num_scalar_prefetch=2,
            grid=(1,),
            in_specs=[whole(y), whole(gate), whole(c), whole(e)]
            + [whole(r) for r in recv]
            + [page(j) for j in range(4)]
            + [
                whole(gain),
                pl.BlockSpec((None, inner, width), lambda g, pg, fl: (m, 0, 0)),
            ],
            out_specs=pl.BlockSpec((rows, width + 128), lambda g, pg, fl: (0, 0)),
        ),
        out_shape=jax.ShapeDtypeStruct((rows, width + 128), BF16),
        cost_estimate=pl.CostEstimate(flops=3 * 10**9, bytes_accessed=6 * 10**6, transcendentals=10**5),
        name="gate_out",
    )(pages, flags, y, gate, c, e, *recv, pool, pool, pool, pool, gain, w_out)


def norm_kernel(m, units, place_ref, part_ref, hid_ref, gain_ref, out_ref):
    width = hid_ref.shape[1]
    total = jnp.sum(part_ref[...].astype(F32), axis=0)
    square = total[:, width : width + 1] + total[:, width + 1 : width + 2] + total[:, width + 2 : width + 3]
    res = hid_ref[...].astype(F32) + total[:, 0:width] * lax.rsqrt(square / units + NORM_EPS)
    mean = jnp.sum(res * res, axis=1, keepdims=True) / width
    normed = (res * lax.rsqrt(mean + NORM_EPS) * gain_ref[m : m + 1, :]).astype(BF16)
    out_ref[...] = jnp.broadcast_to(normed[None], out_ref.shape)


def final_norm(m, place, part, hidden, gain, units):
    group, share, _ = part.shape
    depth = hidden.shape[2]
    return pl.pallas_call(
        functools.partial(norm_kernel, m, float(units)),
        grid_spec=pltpu.PrefetchScalarGridSpec(
            num_scalar_prefetch=1,
            grid=(1,),
            in_specs=[
                pl.BlockSpec(part.shape, lambda g, at: (0, 0, 0)),
                pl.BlockSpec((None, share, depth), lambda g, at: (m, at[0], 0)),
                pl.BlockSpec(gain.shape, lambda g, at: (0, 0)),
            ],
            out_specs=pl.BlockSpec((group, share, depth), lambda g, at: (0, 0, 0)),
        ),
        out_shape=jax.ShapeDtypeStruct((group, share, depth), BF16),
        cost_estimate=pl.CostEstimate(flops=10**7, bytes_accessed=4 * 10**6, transcendentals=100),
        name="final_norm",
    )(place, part, hidden, gain)


def head_kernel(place_ref, x_ref, w_ref, tgt_ref, out_ref):
    tile = x_ref.shape[0]
    vocab = w_ref.shape[1]
    i = pl.program_id(0)
    logits = contract(x_ref[...], w_ref[...], ((1,), (0,)))
    top = jnp.max(logits, axis=1, keepdims=True)
    total = jnp.sum(jnp.exp(logits - top), axis=1, keepdims=True)
    lse = top + jnp.log(total)
    target = (tgt_ref[...] - place_ref[0] * vocab).astype(F32)
    target = jnp.transpose(jnp.broadcast_to(target, (8, tile)))[:, 0:1]
    at = lax.broadcasted_iota(jnp.int32, logits.shape, 1).astype(F32)
    chosen = jnp.sum(jnp.where(at == target, logits, 0.0), axis=1, keepdims=True)
    lane = lax.broadcasted_iota(jnp.int32, (tile, 8), 1)
    flat = jnp.transpose(jnp.where(lane == 0, lse, jnp.where(lane == 1, chosen, 0.0)))
    count = tile // 128
    for n in range(count):
        for which in range(2):
            piece = flat[which : which + 1, n * 128 : (n + 1) * 128]
            out_ref[:, pl.ds(which * 4 + i * count + n, 1), :] = jnp.broadcast_to(
                piece[None], (out_ref.shape[0], 1, 128)
            )


def head_stats(m, place, x, head, tgt, group, tile=256):
    rows, depth = x.shape
    vocab = head.shape[2]
    return pl.pallas_call(
        head_kernel,
        grid_spec=pltpu.PrefetchScalarGridSpec(
            num_scalar_prefetch=1,
            grid=(rows // tile,),
            in_specs=[
                pl.BlockSpec((tile, depth), lambda i, at: (i, 0)),
                pl.BlockSpec((None, depth, vocab), lambda i, at: (m, 0, 0)),
                pl.BlockSpec((1, tile), lambda i, at: (0, i)),
            ],
            out_specs=pl.BlockSpec((group, 8, 128), lambda i, at: (0, 0, 0)),
        ),
        out_shape=jax.ShapeDtypeStruct((group, 8, 128), F32),
        cost_estimate=pl.CostEstimate(
            flops=2 * rows * depth * vocab, bytes_accessed=2 * depth * vocab, transcendentals=rows * vocab
        ),
        name="head_stats",
    )(place, x, head, tgt)


def diff_kernel(s0_ref, s1_ref, live_ref, seg_ref, diff_ref, sums_ref):
    scores = []
    for ref in (s0_ref, s1_ref):
        part = ref[...]
        lse = part[:, 0:4, :]
        top = jnp.max(lse, axis=0)
        total = top + jnp.log(jnp.sum(jnp.exp(lse - top[None]), axis=0))
        scores.append(jnp.sum(part[:, 4:8, :], axis=0) - total)
    lines = lax.broadcasted_iota(jnp.int32, (4, 128), 0)
    alive = jnp.where(lines < 2, live_ref[0].astype(F32), live_ref[1].astype(F32))
    diff = alive * (scores[0] - scores[1])
    diff_ref[...] = diff
    which = lax.broadcasted_iota(jnp.int32, (8, 128), 0)
    sums = jnp.zeros((8, 128), F32)
    for j in range(4):
        mine = jnp.sum(jnp.where(seg_ref[...] == j, diff, 0.0), axis=1, keepdims=True)
        sums = jnp.where(which == j, jnp.sum(mine, axis=0, keepdims=True), sums)
    sums_ref[...] = jnp.broadcast_to(sums[None], sums_ref.shape)


def token_diffs(s0, s1, live, seg, devices):
    vm = pl.BlockSpec(memory_space=pltpu.VMEM)
    return pl.pallas_call(
        diff_kernel,
        in_specs=[vm, vm, pl.BlockSpec(memory_space=pltpu.SMEM), vm],
        out_shape=(jax.ShapeDtypeStruct((4, 128), F32), jax.ShapeDtypeStruct((devices, 8, 128), F32)),
        name="token_diffs",
    )(s0, s1, live, seg)


def per_device(
    hidden, w_inner, w_state, w_step, step_bias, rate, skip_gain, norm_gain, w_out, final_gain, head, pool,
    targets, segment_ids, flags, pages, live, owners,
):
    rows = targets.shape[0]
    depth = hidden.shape[2]
    inner = w_inner.shape[3]
    group = lax.axis_size(VOC)
    devices = lax.axis_size(SEQ)
    place = lax.axis_index(VOC).astype(jnp.int32).reshape(1)
    share = rows // group
    seg = segment_ids.reshape(1, rows)
    tgt = targets.reshape(1, rows)
    w_inner = w_inner.reshape(2, depth, 2 * inner)
    w_state = w_state.reshape(2, depth, -1)
    w_step = jnp.swapaxes(w_step, 1, 2)
    mixed = [
        mix_local(m, hidden, w_inner, w_state, w_step, step_bias, rate, skip_gain, seg) for m in range(2)
    ]
    stats = []
    for m in range(2):
        y, gate, c, e, pay = mixed[m]
        recv = [lax.ppermute(pay, SEQ, [(i, i + k) for i in range(devices - k)]) for k in range(1, REACH + 1)]
        part = gate_out(m, pages, flags, y, gate, c, e, recv, pool, norm_gain, w_out)
        part = lax.all_to_all(part.reshape(group, share, depth + 128), VOC, 0, 0)
        normed = final_norm(m, place, part, hidden, final_gain, inner * group)
        normed = lax.all_to_all(normed, VOC, 0, 0).reshape(rows, depth)
        stats.append(lax.all_to_all(head_stats(m, place, normed, head, tgt, group), VOC, 0, 0))
    diff, sums = token_diffs(stats[0], stats[1], live, segment_ids.reshape(4, 128), devices)
    sums = jnp.sum(lax.all_to_all(sums, SEQ, 0, 0)[:, 0:4, 0], axis=0)
    owned = jnp.where(owners == lax.axis_index(SEQ), sums, 0.0)
    return diff.reshape(rows), owned[None]


def solution(mesh):
    seq, vocab = mesh.devices.shape
    fine = Mesh(mesh.devices.reshape(seq // 2, 2, 4, vocab // 4), ("y", "core", "x", "z"))
    placed = (
        P(None, SEQ, None),
        P(None, None, None, VOC),
        P(),
        P(None, None, VOC),
        P(None, VOC),
        P(None, VOC),
        P(None, VOC),
        P(None, VOC),
        P(None, VOC, None),
        P(),
        P(None, None, VOC),
        P(None, None, VOC, None, None),
        P(SEQ),
        P(SEQ),
        P(),
        P(),
        P(SEQ),
        P(),
    )
    return jax.shard_map(
        per_device, mesh=fine, in_specs=placed, out_specs=(P(SEQ), P(SEQ, None)), check_vma=False
    )
```

```python
import functools

import jax
import jax.numpy as jnp
from jax import lax
from jax.experimental import pallas as pl
from jax.experimental.pallas import tpu as pltpu
from jax.sharding import Mesh
from jax.sharding import PartitionSpec as P

NORM_EPS = 1e-05
SPAN = 256
REACH = 4
SEQ = ("y", "core")
VOC = ("x", "z")
F32 = jnp.float32
BF16 = jnp.bfloat16
LOW = -1e30


def silu(v):
    return v / (1.0 + jnp.exp(-v))


def contract(a, b, dims):
    return lax.dot_general(a, b, (dims, ((), ())), preferred_element_type=F32)


def pieces(value):
    high = value.astype(BF16).astype(F32)
    mid = (value - high).astype(BF16).astype(F32)
    return [high, mid, value - high - mid]


def to_column(row):
    return jnp.transpose(jnp.broadcast_to(row, (8, row.shape[1])))[:, 0:1]


def to_row(column):
    return jnp.transpose(jnp.broadcast_to(column, (column.shape[0], 8)))[0:1, :]


def as_column(row):
    count = row.shape[1]
    spread = jnp.broadcast_to(row, (count, count))
    eye = lax.broadcasted_iota(jnp.int32, spread.shape, 0) == lax.broadcasted_iota(jnp.int32, spread.shape, 1)
    return jnp.sum(jnp.where(eye, spread, 0.0), axis=1, keepdims=True)


def mix_kernel(
    m, tok_ref, wi_ref, ws_ref, wp_ref, bias_ref, rate_ref, skip_ref, seg_ref,
    y_ref, gate_ref, c_ref, e_ref, pay_ref, val_ref, st_ref, stp_ref,
):
    k = pl.program_id(0)
    inner = y_ref.shape[1]

    @pl.when(k == 0)
    def _():
        gate_ref[...] = jnp.zeros_like(gate_ref)
        val_ref[...] = jnp.zeros_like(val_ref)
        st_ref[...] = jnp.zeros_like(st_ref)
        stp_ref[...] = jnp.zeros_like(stp_ref)

    tokens = tok_ref[...]
    gate_ref[...] += contract(tokens, wi_ref[:, 0:inner], ((1,), (0,)))
    val_ref[...] += contract(tokens, wi_ref[:, inner:], ((1,), (0,)))
    st_ref[...] += contract(tokens, ws_ref[...], ((1,), (0,)))
    stp_ref[...] += contract(tokens, wp_ref[...], ((1,), (1,)))

    @pl.when(k == pl.num_programs(0) - 1)
    def _():
        scan_rows(
            m, bias_ref, rate_ref, skip_ref, seg_ref, y_ref, c_ref, e_ref, pay_ref, val_ref, st_ref, stp_ref
        )


def scan_rows(m, bias_ref, rate_ref, skip_ref, seg_ref, y_ref, c_ref, e_ref, pay_ref, val_ref, st_ref, stp_ref):
    rows, inner = y_ref.shape
    heads = bias_ref.shape[1]
    wide = inner // heads
    state = c_ref.shape[1]
    seg = seg_ref[...]
    raw = jnp.transpose(stp_ref[...])[0:heads, :] + as_column(bias_ref[m : m + 1, :])
    dt = jnp.maximum(raw, 0.0) + jnp.log1p(jnp.exp(-jnp.abs(raw)))
    la = -dt * as_column(rate_ref[m : m + 1, :])
    skip = as_column(skip_ref[m : m + 1, :])
    lane = lax.broadcasted_iota(jnp.int32, la.shape, 1)
    run = la
    step = 1
    while step < rows:
        run = run + jnp.where(lane >= step, pltpu.roll(run, step, 1), 0.0)
        step *= 2
    last = jnp.max(seg, axis=1, keepdims=True)
    base = jnp.zeros_like(la)
    for j in range(4):
        base_j = jnp.sum(jnp.where(seg < j, la, 0.0), axis=1, keepdims=True)
        base = jnp.where(seg == j, base_j, base)
    total = jnp.sum(la, axis=1, keepdims=True)
    grow = jnp.exp(run - base)
    keep = jnp.where(seg == last, jnp.exp(jnp.minimum(total - run, 0.0)) * dt, 0.0)
    tail = jnp.exp(jnp.sum(jnp.where(seg == last, la, 0.0), axis=1, keepdims=True))
    cols = jnp.transpose(jnp.concatenate([run, keep], axis=0))
    segf = jnp.broadcast_to(seg.astype(F32), (heads, rows))
    ecol = jnp.transpose(jnp.concatenate([grow, segf], axis=0))
    e_ref[...] = ecol
    values = silu(val_ref[...]).astype(BF16)
    in_map = silu(st_ref[:, 0:state]).astype(BF16)
    out_map = silu(st_ref[:, state:]).astype(BF16)
    c_ref[...] = out_map
    vf = values.astype(F32)
    kept = jnp.concatenate(
        [vf[:, h * wide : (h + 1) * wide] * cols[:, heads + h : heads + h + 1] for h in range(heads)], axis=1
    ).astype(BF16)
    added = contract(kept, in_map, ((0,), (0,)))
    pay_ref[0:inner, :] = added.astype(BF16)
    high = tail.astype(BF16).astype(F32)
    low = tail - high
    meta = jnp.concatenate(
        [
            jnp.broadcast_to(high, (heads, state)),
            jnp.broadcast_to(low, (heads, state)),
            jnp.broadcast_to(last.astype(F32) + 1.0, (8, state)),
        ],
        axis=0,
    )
    pay_ref[inner : inner + 16, :] = meta.astype(BF16)
    blocks = rows // SPAN
    for i in range(blocks):
        t0 = i * SPAN
        acc = [vf[t0 : t0 + SPAN, h * wide : (h + 1) * wide] * skip[h : h + 1, :] for h in range(heads)]
        for j in range(i + 1):
            s0 = j * SPAN
            scores = contract(out_map[t0 : t0 + SPAN], in_map[s0 : s0 + SPAN], ((1,), (1,)))
            same = ecol[t0 : t0 + SPAN, heads : heads + 1] == segf[0:1, s0 : s0 + SPAN]
            if i == j:
                same = same & (
                    lax.broadcasted_iota(jnp.int32, (SPAN, SPAN), 0)
                    >= lax.broadcasted_iota(jnp.int32, (SPAN, SPAN), 1)
                )
            for h in range(heads):
                gap = cols[t0 : t0 + SPAN, h : h + 1] - run[h : h + 1, s0 : s0 + SPAN]
                weight = jnp.exp(jnp.where(same, gap, LOW)) * (scores * dt[h : h + 1, s0 : s0 + SPAN])
                acc[h] = acc[h] + contract(
                    weight.astype(BF16), values[s0 : s0 + SPAN, h * wide : (h + 1) * wide], ((1,), (0,))
                )
        y_ref[t0 : t0 + SPAN, :] = jnp.concatenate(acc, axis=1)


def mix_local(m, hidden, w_inner, w_state, w_step, bias, rate, skip, seg, chunks=4):
    rows, depth = hidden.shape[1:]
    inner = w_inner.shape[2] // 2
    state = w_state.shape[2] // 2
    heads = bias.shape[1]
    deep = depth // chunks
    whole = lambda a: pl.BlockSpec(a.shape, lambda k: (0,) * a.ndim)
    const = lambda shape: pl.BlockSpec(shape, lambda k: (0, 0))
    shapes = ((rows, inner), F32), ((rows, inner), F32), ((rows, state), BF16), ((rows, 2 * heads), F32), (
        (inner + 16, state), BF16)
    return pl.pallas_call(
        functools.partial(mix_kernel, m),
        grid=(chunks,),
        in_specs=[
            pl.BlockSpec((None, rows, deep), lambda k: (m, 0, k)),
            pl.BlockSpec((None, deep, 2 * inner), lambda k: (m, k, 0)),
            pl.BlockSpec((None, deep, 2 * state), lambda k: (m, k, 0)),
            pl.BlockSpec((None, heads, deep), lambda k: (m, 0, k)),
            whole(bias), whole(rate), whole(skip), whole(seg),
        ],
        out_specs=[const(shape) for shape, _ in shapes],
        out_shape=[jax.ShapeDtypeStruct(shape, kind) for shape, kind in shapes],
        scratch_shapes=[
            pltpu.VMEM((rows, inner), F32), pltpu.VMEM((rows, 2 * state), F32), pltpu.VMEM((rows, heads), F32)
        ],
        cost_estimate=pl.CostEstimate(flops=5 * 10**9, bytes_accessed=8 * 10**6, transcendentals=10**6),
        name="mix_local",
    )(hidden, w_inner, w_state, w_step, bias, rate, skip, seg)


def gate_kernel(
    m, pages_ref, flags_ref, y_ref, gate_ref, c_ref, e_ref, r1_ref, r2_ref, r3_ref, r4_ref,
    p0_ref, p1_ref, p2_ref, p3_ref, gain_ref, out_ref,
):
    rows, inner = y_ref.shape
    heads = p0_ref.shape[0]
    wide = inner // heads
    state = c_ref.shape[1]
    e_col = e_ref[...]
    seg_col = e_col[:, heads : heads + 1]
    seg_first = e_col[0:1, heads : heads + 1]
    init = [
        p.reshape(inner, state)[...].astype(F32) * flags_ref[j].astype(F32)
        for j, p in enumerate((p0_ref, p1_ref, p2_ref, p3_ref))
    ]
    through = jnp.ones((heads, state), F32)
    parts = [jnp.zeros((wide, state), F32) for _ in range(heads)]
    for r in (r1_ref, r2_ref, r3_ref, r4_ref):
        meta = r[inner : inner + 16, :].astype(F32)
        hit = meta[8:9, :] == seg_first + 1.0
        piece = r[0:inner, :].astype(F32)
        weight = jnp.where(hit, through, 0.0)
        for h in range(heads):
            parts[h] = parts[h] + weight[h : h + 1, :] * piece[h * wide : (h + 1) * wide, :]
        through = jnp.where(hit, through * (meta[0:heads] + meta[heads : 2 * heads]), through)
    prior = jnp.concatenate(parts, axis=0)
    through = jnp.concatenate([jnp.broadcast_to(through[h : h + 1, :], (wide, state)) for h in range(heads)], axis=0)
    out_map = c_ref[...]
    picked = jnp.zeros((rows, inner), F32)
    for j in range(4):
        start = jnp.where(seg_first == float(j), prior + through * init[j], init[j])
        high = start.astype(BF16)
        low = (start - high.astype(F32)).astype(BF16)
        from_state = contract(out_map, high, ((1,), (1,))) + contract(out_map, low, ((1,), (1,)))
        picked = jnp.where(seg_col == float(j), from_state, picked)
    spread = jnp.concatenate([jnp.broadcast_to(e_col[:, h : h + 1], (rows, wide)) for h in range(heads)], axis=1)
    gated = (y_ref[...] + picked * spread) * silu(gate_ref[...])
    square = jnp.sum(gated * gated, axis=1, keepdims=True)
    out_ref[0:rows, :] = (gated * gain_ref[m : m + 1, :]).astype(BF16)
    lines = jnp.transpose(jnp.broadcast_to(square, (rows, 8)))[0:1, :]
    halves = jnp.concatenate([lines[:, 0:inner], lines[:, inner:]], axis=0)
    extra = jnp.concatenate(pieces(halves) + [jnp.zeros((10, inner), F32)], axis=0)
    out_ref[rows : rows + 16, :] = extra.astype(BF16)


def gate_out(m, pages, flags, y, gate, c, e, recv, pool, gain):
    rows, inner = y.shape
    heads = pool.shape[2]
    state = c.shape[1]
    whole = lambda a: pl.BlockSpec(a.shape, lambda g, pg, fl: (0,) * a.ndim)
    page = lambda j: pl.BlockSpec(
        (None, None, heads, pool.shape[3], state), lambda g, pg, fl: (m, pg[j], 0, 0, 0)
    )
    return pl.pallas_call(
        functools.partial(gate_kernel, m),
        grid_spec=pltpu.PrefetchScalarGridSpec(
            num_scalar_prefetch=2,
            grid=(1,),
            in_specs=[whole(y), whole(gate), whole(c), whole(e)]
            + [whole(r) for r in recv]
            + [page(j) for j in range(4)]
            + [whole(gain)],
            out_specs=pl.BlockSpec((rows + 16, inner), lambda g, pg, fl: (0, 0)),
        ),
        out_shape=jax.ShapeDtypeStruct((rows + 16, inner), BF16),
        cost_estimate=pl.CostEstimate(flops=10**9, bytes_accessed=4 * 10**6, transcendentals=10**5),
        name="gate_out",
    )(pages, flags, y, gate, c, e, *recv, pool, pool, pool, pool, gain)


def out_kernel(at_ref, g0_ref, g1_ref, g2_ref, g3_ref, w_ref, o0_ref, o1_ref, o2_ref, o3_ref, acc_ref, sq_ref):
    rows, width = acc_ref.shape
    inner = g0_ref.shape[1]
    block = rows // 4
    along, across = at_ref[0], at_ref[1]
    gathered = (g0_ref, g1_ref, g2_ref, g3_ref)
    extra = sum(g[rows : rows + 16, :].astype(F32) for g in gathered)
    square = extra[0:2] + extra[2:4] + extra[4:6]
    for n in range(4):
        sq_ref[n : n + 1, :] = square[n // 2 : n // 2 + 1, (n % 2) * block : (n % 2 + 1) * block]
    acc_ref[...] = sum(
        contract(g[0:rows, :], w_ref[lax.rem(along + 4 - k, 4)], ((1,), (0,))) for k, g in enumerate(gathered)
    )
    for k, out in enumerate((o0_ref, o1_ref, o2_ref, o3_ref)):
        at = lax.rem(across + k, 4)
        out[0:block, :] = acc_ref[pl.ds(pl.multiple_of(at * block, block), block), :].astype(BF16)
        line = jnp.concatenate(pieces(sq_ref[pl.ds(at, 1), :]) + [jnp.zeros((1, width - 3 * block), F32)], axis=1)
        out[block : block + 16, :] = jnp.broadcast_to(line, (16, width)).astype(BF16)


def out_blocks(at, gathered, w):
    rows = gathered[0].shape[0] - 16
    width = w.shape[2]
    block = rows // 4
    vm = pl.BlockSpec(memory_space=pltpu.VMEM)
    return pl.pallas_call(
        out_kernel,
        in_specs=[pl.BlockSpec(memory_space=pltpu.SMEM)] + [vm] * 5,
        out_specs=[vm] * 4,
        out_shape=[jax.ShapeDtypeStruct((block + 16, width), BF16)] * 4,
        scratch_shapes=[pltpu.VMEM((rows, width), F32), pltpu.VMEM((4, block), F32)],
        cost_estimate=pl.CostEstimate(flops=10**9, bytes_accessed=3 * 10**6, transcendentals=0),
        name="out_blocks",
    )(at, *gathered, w)


def residual_kernel(m, units, at_ref, o0_ref, o1_ref, o2_ref, o3_ref, hid_ref, gain_ref, out_ref):
    block, width = hid_ref.shape
    total = sum(o[...].astype(F32) for o in (o0_ref, o1_ref, o2_ref, o3_ref))
    line = total[block : block + 1, :]
    square = line[:, 0:block] + line[:, block : 2 * block] + line[:, 2 * block : 3 * block]
    scale = to_column(lax.rsqrt(square / units + NORM_EPS))
    res = hid_ref[...].astype(F32) + total[0:block, :] * scale
    out_ref[0:block, :] = (res * gain_ref[m : m + 1, :]).astype(BF16)
    line = jnp.concatenate(
        pieces(to_row(jnp.sum(res * res, axis=1, keepdims=True))) + [jnp.zeros((1, width - 3 * block), F32)], axis=1
    )
    out_ref[block : block + 16, :] = jnp.broadcast_to(line, (16, width)).astype(BF16)


def residual_block(m, at, parts, hidden, gain, units):
    block, width = parts[0].shape[0] - 16, parts[0].shape[1]
    whole = pl.BlockSpec((block + 16, width), lambda g, at: (0, 0))
    return pl.pallas_call(
        functools.partial(residual_kernel, m, float(units)),
        grid_spec=pltpu.PrefetchScalarGridSpec(
            num_scalar_prefetch=1,
            grid=(1,),
            in_specs=[whole] * 4
            + [
                pl.BlockSpec((None, block, width), lambda g, at: (m, at[1], at[0])),
                pl.BlockSpec((2, width), lambda g, at: (0, at[0])),
            ],
            out_specs=whole,
        ),
        out_shape=jax.ShapeDtypeStruct((block + 16, width), BF16),
        cost_estimate=pl.CostEstimate(flops=10**6, bytes_accessed=10**6, transcendentals=100),
        name="residual_block",
    )(at, *parts, hidden, gain)


def join_kernel(at_ref, u0_ref, u1_ref, u2_ref, u3_ref, out_ref):
    block, width = u0_ref.shape[0] - 16, u0_ref.shape[1]
    square = jnp.zeros((1, block), F32)
    for k, u in enumerate((u0_ref, u1_ref, u2_ref, u3_ref)):
        at = pl.multiple_of(lax.rem(at_ref[0] + 4 - k, 4) * width, width)
        out_ref[0:block, pl.ds(at, width)] = u[0:block, :]
        line = u[block : block + 16, :].astype(F32)[0:1, :]
        square = square + line[:, 0:block] + line[:, block : 2 * block] + line[:, 2 * block : 3 * block]
    scale = lax.rsqrt(square / out_ref.shape[1] + NORM_EPS)
    out_ref[block : block + 16, :] = jnp.zeros((16, out_ref.shape[1]), BF16)
    line = jnp.concatenate(pieces(scale), axis=1)
    out_ref[block : block + 16, 0 : 3 * block] = jnp.broadcast_to(line, (16, 3 * block)).astype(BF16)


def join_columns(at, parts):
    tall, width = parts[0].shape
    vm = pl.BlockSpec(memory_space=pltpu.VMEM)
    return pl.pallas_call(
        join_kernel,
        in_specs=[pl.BlockSpec(memory_space=pltpu.SMEM)] + [vm] * 4,
        out_specs=vm,
        out_shape=jax.ShapeDtypeStruct((tall, 4 * width), BF16),
        cost_estimate=pl.CostEstimate(flops=10**5, bytes_accessed=10**6, transcendentals=100),
        name="join_columns",
    )(at, *parts)


def head_kernel(place_ref, at_ref, x0_ref, x1_ref, x2_ref, x3_ref, w_ref, tgt_ref, out_ref):
    block = x0_ref.shape[0] - 16
    vocab = w_ref.shape[1]
    for pair in (((0, x0_ref), (1, x1_ref)), ((2, x2_ref), (3, x3_ref))):
        rows = jnp.concatenate([x[0:block, :] for _, x in pair], axis=0)
        raw = contract(rows, w_ref[...], ((1,), (0,)))
        for n, (k, x) in enumerate(pair):
            at = lax.rem(at_ref[1] + 4 - k, 4)
            line = x[block : block + 16, 0 : 3 * block].astype(F32)[0:1, :]
            scale = to_column(line[:, 0:block] + line[:, block : 2 * block] + line[:, 2 * block : 3 * block])
            logits = raw[n * block : (n + 1) * block, :] * scale
            top = jnp.max(logits, axis=1, keepdims=True)
            lse = top + jnp.log(jnp.sum(jnp.exp(logits - top), axis=1, keepdims=True))
            target = to_column((tgt_ref[pl.ds(at, 1), :] - place_ref[0] * vocab).astype(F32))
            column = lax.broadcasted_iota(jnp.int32, logits.shape, 1).astype(F32)
            chosen = jnp.sum(jnp.where(column == target, logits, 0.0), axis=1, keepdims=True)
            for which, value in enumerate((lse, chosen)):
                out_ref[:, pl.ds(which * 4 + at, 1), :] = jnp.broadcast_to(
                    to_row(value)[None], (out_ref.shape[0], 1, block)
                )


def head_stats(m, place, at, parts, head, tgt, group):
    tall, depth = parts[0].shape
    block = tall - 16
    vocab = head.shape[2]
    whole = pl.BlockSpec((tall, depth), lambda i, pf, at: (0, 0))
    return pl.pallas_call(
        head_kernel,
        grid_spec=pltpu.PrefetchScalarGridSpec(
            num_scalar_prefetch=2,
            grid=(1,),
            in_specs=[whole] * 4
            + [
                pl.BlockSpec((None, depth, vocab), lambda i, pf, at: (m, 0, 0)),
                pl.BlockSpec(tgt.shape, lambda i, pf, at: (0, 0)),
            ],
            out_specs=pl.BlockSpec((group, 8, block), lambda i, pf, at: (0, 0, 0)),
        ),
        out_shape=jax.ShapeDtypeStruct((group, 8, block), F32),
        cost_estimate=pl.CostEstimate(
            flops=8 * block * depth * vocab, bytes_accessed=2 * depth * vocab, transcendentals=4 * block * vocab
        ),
        name="head_stats",
    )(place, at, *parts, head, tgt)


def diff_kernel(s0_ref, s1_ref, live_ref, seg_ref, diff_ref, sums_ref):
    scores = []
    for ref in (s0_ref, s1_ref):
        part = ref[...]
        lse = part[:, 0:4, :]
        top = jnp.max(lse, axis=0)
        total = top + jnp.log(jnp.sum(jnp.exp(lse - top[None]), axis=0))
        scores.append(jnp.sum(part[:, 4:8, :], axis=0) - total)
    lines = lax.broadcasted_iota(jnp.int32, (4, 128), 0)
    alive = jnp.where(lines < 2, live_ref[0].astype(F32), live_ref[1].astype(F32))
    diff = alive * (scores[0] - scores[1])
    diff_ref[...] = diff
    which = lax.broadcasted_iota(jnp.int32, (8, 128), 0)
    sums = jnp.zeros((8, 128), F32)
    for j in range(4):
        mine = jnp.sum(jnp.where(seg_ref[...] == j, diff, 0.0), axis=1, keepdims=True)
        sums = jnp.where(which == j, jnp.sum(mine, axis=0, keepdims=True), sums)
    sums_ref[...] = jnp.broadcast_to(sums[None], sums_ref.shape)


def token_diffs(s0, s1, live, seg, devices):
    vm = pl.BlockSpec(memory_space=pltpu.VMEM)
    return pl.pallas_call(
        diff_kernel,
        in_specs=[vm, vm, pl.BlockSpec(memory_space=pltpu.SMEM), vm],
        out_shape=(jax.ShapeDtypeStruct((4, 128), F32), jax.ShapeDtypeStruct((devices, 8, 128), F32)),
        name="token_diffs",
    )(s0, s1, live, seg)


def ring(value, axis, by):
    return lax.ppermute(value, axis, [(i, (i + by) % 4) for i in range(4)])


def gathered(value, axis):
    return [value] + [ring(value, axis, k) for k in (1, 2, 3)]


def per_device(
    hidden, w_inner, w_state, w_step, step_bias, rate, skip_gain, norm_gain, w_out, final_gain, head, pool,
    targets, segment_ids, flags, pages, live, owners,
):
    rows = targets.shape[0]
    depth = hidden.shape[2]
    inner = w_inner.shape[3]
    group = lax.axis_size(VOC)
    devices = lax.axis_size(SEQ)
    place = lax.axis_index(VOC).astype(jnp.int32).reshape(1)
    seg = segment_ids.reshape(1, rows)
    tgt = targets.reshape(4, rows // 4)
    w_inner = w_inner.reshape(2, depth, 2 * inner)
    w_state = w_state.reshape(2, depth, -1)
    w_step = jnp.swapaxes(w_step, 1, 2)
    ways = (("x", "z"), ("z", "x"))
    turned = jnp.swapaxes(w_out.reshape(2, inner, 4, depth // 4), 1, 2)
    weights = [lax.all_to_all(turned[m], ways[m][0], 0, 0) for m in range(2)]
    mixed = [
        mix_local(m, hidden, w_inner, w_state, w_step, step_bias, rate, skip_gain, seg) for m in range(2)
    ]
    stats = []
    for m in range(2):
        along, across = ways[m]
        at = jnp.stack([lax.axis_index(along), lax.axis_index(across)]).astype(jnp.int32)
        y, gate, c, e, pay = mixed[m]
        recv = [lax.ppermute(pay, SEQ, [(i, i + k) for i in range(devices - k)]) for k in range(1, REACH + 1)]
        gated = gate_out(m, pages, flags, y, gate, c, e, recv, pool, norm_gain)
        parts = out_blocks(at, gathered(gated, along), weights[m])
        parts = [parts[0]] + [ring(parts[k], across, k) for k in (1, 2, 3)]
        res = residual_block(m, at, parts, hidden, final_gain, inner * group)
        full = join_columns(at, gathered(res, along))
        stat = head_stats(m, place, at, gathered(full, across), head, tgt, group)
        stats.append(lax.all_to_all(stat, VOC, 0, 0))
    diff, sums = token_diffs(stats[0], stats[1], live, segment_ids.reshape(4, 128), devices)
    sums = jnp.sum(lax.all_to_all(sums, SEQ, 0, 0)[:, 0:4, 0], axis=0)
    owned = jnp.where(owners == lax.axis_index(SEQ), sums, 0.0)
    return diff.reshape(rows), owned[None]


def solution(mesh):
    seq, vocab = mesh.devices.shape
    fine = Mesh(mesh.devices.reshape(seq // 2, 2, 4, vocab // 4), ("y", "core", "x", "z"))
    placed = (
        P(None, SEQ, None),
        P(None, None, None, VOC),
        P(),
        P(None, None, VOC),
        P(None, VOC),
        P(None, VOC),
        P(None, VOC),
        P(None, VOC),
        P(None, VOC, None),
        P(),
        P(None, None, VOC),
        P(None, None, VOC, None, None),
        P(SEQ),
        P(SEQ),
        P(),
        P(),
        P(SEQ),
        P(),
    )
    return jax.shard_map(
        per_device, mesh=fine, in_specs=placed, out_specs=(P(SEQ), P(SEQ, None)), check_vma=False
    )
```

```python
import functools

import jax
import jax.numpy as jnp
from jax import lax
from jax.experimental import pallas as pl
from jax.experimental.pallas import tpu as pltpu
from jax.sharding import Mesh
from jax.sharding import PartitionSpec as P

NORM_EPS = 1e-05
SPAN = 256
REACH = 4
SEQ = ("y", "core")
VOC = ("x", "z")
F32 = jnp.float32
BF16 = jnp.bfloat16
LOW = -1e30


def silu(v):
    return v / (1.0 + jnp.exp(-v))


def contract(a, b, dims):
    return lax.dot_general(a, b, (dims, ((), ())), preferred_element_type=F32)


def drop(kernel, inputs, count):
    def body(*refs):
        return kernel(*refs[:inputs], *refs[inputs + count :])

    return body


ANYWHERE = pl.BlockSpec(memory_space=pl.ANY)


def pieces(value):
    high = value.astype(BF16).astype(F32)
    mid = (value - high).astype(BF16).astype(F32)
    return [high, mid, value - high - mid]


def to_column(row):
    return jnp.transpose(jnp.broadcast_to(row, (8, row.shape[1])))[:, 0:1]


def to_row(column):
    return jnp.transpose(jnp.broadcast_to(column, (column.shape[0], 8)))[0:1, :]


def as_column(row):
    count = row.shape[1]
    spread = jnp.broadcast_to(row, (count, count))
    eye = lax.broadcasted_iota(jnp.int32, spread.shape, 0) == lax.broadcasted_iota(jnp.int32, spread.shape, 1)
    return jnp.sum(jnp.where(eye, spread, 0.0), axis=1, keepdims=True)


def mix_kernel(
    m, tok_ref, wi_ref, ws_ref, wp_ref, bias_ref, rate_ref, skip_ref, seg_ref,
    y_ref, gate_ref, c_ref, e_ref, pay_ref, val_ref, st_ref, stp_ref,
):
    k = pl.program_id(0)
    inner = y_ref.shape[1]

    @pl.when(k == 0)
    def _():
        gate_ref[...] = jnp.zeros_like(gate_ref)
        val_ref[...] = jnp.zeros_like(val_ref)
        st_ref[...] = jnp.zeros_like(st_ref)
        stp_ref[...] = jnp.zeros_like(stp_ref)

    tokens = tok_ref[...]
    gate_ref[...] += contract(tokens, wi_ref[:, 0, :], ((1,), (0,)))
    val_ref[...] += contract(tokens, wi_ref[:, 1, :], ((1,), (0,)))
    state = c_ref.shape[1]
    st_ref[:, 0:state] += contract(tokens, ws_ref[:, 0, :], ((1,), (0,)))
    st_ref[:, state:] += contract(tokens, ws_ref[:, 1, :], ((1,), (0,)))
    stp_ref[...] += contract(tokens, wp_ref[...], ((1,), (1,)))

    @pl.when(k == pl.num_programs(0) - 1)
    def _():
        scan_rows(
            m, bias_ref, rate_ref, skip_ref, seg_ref, y_ref, c_ref, e_ref, pay_ref, val_ref, st_ref, stp_ref
        )


def scan_rows(m, bias_ref, rate_ref, skip_ref, seg_ref, y_ref, c_ref, e_ref, pay_ref, val_ref, st_ref, stp_ref):
    rows, inner = y_ref.shape
    heads = bias_ref.shape[1]
    wide = inner // heads
    state = c_ref.shape[1]
    seg = seg_ref[...]
    raw = jnp.transpose(stp_ref[...])[0:heads, :] + as_column(bias_ref[m : m + 1, :])
    dt = jnp.maximum(raw, 0.0) + jnp.log1p(jnp.exp(-jnp.abs(raw)))
    la = -dt * as_column(rate_ref[m : m + 1, :])
    skip = as_column(skip_ref[m : m + 1, :])
    lane = lax.broadcasted_iota(jnp.int32, la.shape, 1)
    run = la
    step = 1
    while step < rows:
        run = run + jnp.where(lane >= step, pltpu.roll(run, step, 1), 0.0)
        step *= 2
    last = jnp.max(seg, axis=1, keepdims=True)
    base = jnp.zeros_like(la)
    for j in range(4):
        base_j = jnp.sum(jnp.where(seg < j, la, 0.0), axis=1, keepdims=True)
        base = jnp.where(seg == j, base_j, base)
    total = jnp.sum(la, axis=1, keepdims=True)
    grow = jnp.exp(run - base)
    keep = jnp.where(seg == last, jnp.exp(jnp.minimum(total - run, 0.0)) * dt, 0.0)
    tail = jnp.exp(jnp.sum(jnp.where(seg == last, la, 0.0), axis=1, keepdims=True))
    cols = jnp.transpose(jnp.concatenate([run, keep], axis=0))
    segf = jnp.broadcast_to(seg.astype(F32), (heads, rows))
    ecol = jnp.transpose(jnp.concatenate([grow, segf], axis=0))
    e_ref[...] = ecol
    values = silu(val_ref[...]).astype(BF16)
    in_map = silu(st_ref[:, 0:state]).astype(BF16)
    out_map = silu(st_ref[:, state:]).astype(BF16)
    c_ref[...] = out_map
    vf = values.astype(F32)
    kept = jnp.concatenate(
        [vf[:, h * wide : (h + 1) * wide] * cols[:, heads + h : heads + h + 1] for h in range(heads)], axis=1
    ).astype(BF16)
    added = contract(kept, in_map, ((0,), (0,)))
    pay_ref[0:inner, :] = added.astype(BF16)
    high = tail.astype(BF16).astype(F32)
    low = tail - high
    meta = jnp.concatenate(
        [
            jnp.broadcast_to(high, (heads, state)),
            jnp.broadcast_to(low, (heads, state)),
            jnp.broadcast_to(last.astype(F32) + 1.0, (8, state)),
        ],
        axis=0,
    )
    pay_ref[inner : inner + 16, :] = meta.astype(BF16)
    blocks = rows // SPAN
    for i in range(blocks):
        t0 = i * SPAN
        acc = [vf[t0 : t0 + SPAN, h * wide : (h + 1) * wide] * skip[h : h + 1, :] for h in range(heads)]
        for j in range(i + 1):
            s0 = j * SPAN
            scores = contract(out_map[t0 : t0 + SPAN], in_map[s0 : s0 + SPAN], ((1,), (1,)))
            same = ecol[t0 : t0 + SPAN, heads : heads + 1] == segf[0:1, s0 : s0 + SPAN]
            if i == j:
                same = same & (
                    lax.broadcasted_iota(jnp.int32, (SPAN, SPAN), 0)
                    >= lax.broadcasted_iota(jnp.int32, (SPAN, SPAN), 1)
                )
            for h in range(heads):
                gap = cols[t0 : t0 + SPAN, h : h + 1] - run[h : h + 1, s0 : s0 + SPAN]
                weight = jnp.exp(jnp.where(same, gap, LOW)) * (scores * dt[h : h + 1, s0 : s0 + SPAN])
                acc[h] = acc[h] + contract(
                    weight.astype(BF16), values[s0 : s0 + SPAN, h * wide : (h + 1) * wide], ((1,), (0,))
                )
        y_ref[t0 : t0 + SPAN, :] = jnp.concatenate(acc, axis=1)


def mix_local(m, hidden, w_inner, w_state, w_step, bias, rate, skip, seg, after=(), chunks=4):
    rows, depth = hidden.shape[1:]
    inner = w_inner.shape[3]
    state = w_state.shape[3]
    heads = bias.shape[1]
    deep = depth // chunks
    whole = lambda a: pl.BlockSpec(a.shape, lambda k: (0,) * a.ndim)
    const = lambda shape: pl.BlockSpec(shape, lambda k: (0, 0))
    shapes = ((rows, inner), F32), ((rows, inner), F32), ((rows, state), BF16), ((rows, 2 * heads), F32), (
        (inner + 16, state), BF16)
    return pl.pallas_call(
        drop(functools.partial(mix_kernel, m), 8, len(after)),
        grid=(chunks,),
        in_specs=[
            pl.BlockSpec((None, rows, deep), lambda k: (m, 0, k)),
            pl.BlockSpec((None, deep, 2, inner), lambda k: (m, k, 0, 0)),
            pl.BlockSpec((None, deep, 2, state), lambda k: (m, k, 0, 0)),
            pl.BlockSpec((None, heads, deep), lambda k: (m, 0, k)),
            whole(bias), whole(rate), whole(skip), whole(seg),
        ]
        + [ANYWHERE] * len(after),
        out_specs=[const(shape) for shape, _ in shapes],
        out_shape=[jax.ShapeDtypeStruct(shape, kind) for shape, kind in shapes],
        scratch_shapes=[
            pltpu.VMEM((rows, inner), F32), pltpu.VMEM((rows, 2 * state), F32), pltpu.VMEM((rows, heads), F32)
        ],
        cost_estimate=pl.CostEstimate(flops=5 * 10**9, bytes_accessed=8 * 10**6, transcendentals=10**6),
        name="mix_local",
    )(hidden, w_inner, w_state, w_step, bias, rate, skip, seg, *after)


def gate_kernel(
    m, pages_ref, flags_ref, y_ref, gate_ref, c_ref, e_ref, r1_ref, r2_ref, r3_ref, r4_ref,
    p0_ref, p1_ref, p2_ref, p3_ref, gain_ref, out_ref,
):
    rows, inner = y_ref.shape
    heads = p0_ref.shape[0]
    wide = inner // heads
    state = c_ref.shape[1]
    e_col = e_ref[...]
    seg_col = e_col[:, heads : heads + 1]
    seg_first = e_col[0:1, heads : heads + 1]
    init = [
        p.reshape(inner, state)[...].astype(F32) * flags_ref[j].astype(F32)
        for j, p in enumerate((p0_ref, p1_ref, p2_ref, p3_ref))
    ]
    through = jnp.ones((heads, state), F32)
    parts = [jnp.zeros((wide, state), F32) for _ in range(heads)]
    for r in (r1_ref, r2_ref, r3_ref, r4_ref):
        meta = r[inner : inner + 16, :].astype(F32)
        hit = meta[8:9, :] == seg_first + 1.0
        piece = r[0:inner, :].astype(F32)
        weight = jnp.where(hit, through, 0.0)
        for h in range(heads):
            parts[h] = parts[h] + weight[h : h + 1, :] * piece[h * wide : (h + 1) * wide, :]
        through = jnp.where(hit, through * (meta[0:heads] + meta[heads : 2 * heads]), through)
    prior = jnp.concatenate(parts, axis=0)
    through = jnp.concatenate([jnp.broadcast_to(through[h : h + 1, :], (wide, state)) for h in range(heads)], axis=0)
    out_map = c_ref[...]
    picked = jnp.zeros((rows, inner), F32)
    for j in range(4):
        start = jnp.where(seg_first == float(j), prior + through * init[j], init[j])
        high = start.astype(BF16)
        low = (start - high.astype(F32)).astype(BF16)
        from_state = contract(out_map, high, ((1,), (1,))) + contract(out_map, low, ((1,), (1,)))
        picked = jnp.where(seg_col == float(j), from_state, picked)
    spread = jnp.concatenate([jnp.broadcast_to(e_col[:, h : h + 1], (rows, wide)) for h in range(heads)], axis=1)
    gated = (y_ref[...] + picked * spread) * silu(gate_ref[...])
    square = jnp.sum(gated * gated, axis=1, keepdims=True)
    out_ref[0:rows, :] = (gated * gain_ref[m : m + 1, :]).astype(BF16)
    lines = jnp.transpose(jnp.broadcast_to(square, (rows, 8)))[0:1, :]
    halves = jnp.concatenate([lines[:, 0:inner], lines[:, inner:]], axis=0)
    extra = jnp.concatenate(pieces(halves) + [jnp.zeros((10, inner), F32)], axis=0)
    out_ref[rows : rows + 16, :] = extra.astype(BF16)


def gate_out(m, pages, flags, y, gate, c, e, recv, pool, gain, after=()):
    rows, inner = y.shape
    heads = pool.shape[2]
    state = c.shape[1]
    whole = lambda a: pl.BlockSpec(a.shape, lambda g, pg, fl: (0,) * a.ndim)
    page = lambda j: pl.BlockSpec(
        (None, None, heads, pool.shape[3], state), lambda g, pg, fl: (m, pg[j], 0, 0, 0)
    )
    return pl.pallas_call(
        drop(functools.partial(gate_kernel, m), 15, len(after)),
        grid_spec=pltpu.PrefetchScalarGridSpec(
            num_scalar_prefetch=2,
            grid=(1,),
            in_specs=[whole(y), whole(gate), whole(c), whole(e)]
            + [whole(r) for r in recv]
            + [page(j) for j in range(4)]
            + [whole(gain)]
            + [ANYWHERE] * len(after),
            out_specs=pl.BlockSpec((rows + 16, inner), lambda g, pg, fl: (0, 0)),
        ),
        out_shape=jax.ShapeDtypeStruct((rows + 16, inner), BF16),
        cost_estimate=pl.CostEstimate(flops=10**9, bytes_accessed=4 * 10**6, transcendentals=10**5),
        name="gate_out",
    )(pages, flags, y, gate, c, e, *recv, pool, pool, pool, pool, gain, *after)


def out_kernel(at_ref, g0_ref, g1_ref, g2_ref, g3_ref, w_ref, o0_ref, o1_ref, o2_ref, o3_ref, acc_ref, sq_ref):
    rows, width = acc_ref.shape
    inner = g0_ref.shape[1]
    block = rows // 4
    along, across = at_ref[0], at_ref[1]
    gathered = (g0_ref, g1_ref, g2_ref, g3_ref)
    extra = sum(g[rows : rows + 16, :].astype(F32) for g in gathered)
    square = extra[0:2] + extra[2:4] + extra[4:6]
    for n in range(4):
        sq_ref[n : n + 1, :] = square[n // 2 : n // 2 + 1, (n % 2) * block : (n % 2 + 1) * block]
    acc_ref[...] = sum(
        contract(g[0:rows, :], w_ref[lax.rem(along + 4 - k, 4)], ((1,), (0,))) for k, g in enumerate(gathered)
    )
    for k, out in enumerate((o0_ref, o1_ref, o2_ref, o3_ref)):
        at = lax.rem(across + k, 4)
        out[0:block, :] = acc_ref[pl.ds(pl.multiple_of(at * block, block), block), :].astype(BF16)
        line = jnp.concatenate(pieces(sq_ref[pl.ds(at, 1), :]) + [jnp.zeros((1, width - 3 * block), F32)], axis=1)
        out[block : block + 16, :] = jnp.broadcast_to(line, (16, width)).astype(BF16)


def out_blocks(at, gathered, w, after=()):
    rows = gathered[0].shape[0] - 16
    width = w.shape[2]
    block = rows // 4
    vm = pl.BlockSpec(memory_space=pltpu.VMEM)
    return pl.pallas_call(
        drop(out_kernel, 6, len(after)),
        in_specs=[pl.BlockSpec(memory_space=pltpu.SMEM)] + [vm] * 5 + [ANYWHERE] * len(after),
        out_specs=[vm] * 4,
        out_shape=[jax.ShapeDtypeStruct((block + 16, width), BF16)] * 4,
        scratch_shapes=[pltpu.VMEM((rows, width), F32), pltpu.VMEM((4, block), F32)],
        cost_estimate=pl.CostEstimate(flops=10**9, bytes_accessed=3 * 10**6, transcendentals=0),
        name="out_blocks",
    )(at, *gathered, w, *after)


def residual_kernel(m, units, at_ref, o0_ref, o1_ref, o2_ref, o3_ref, hid_ref, gain_ref, out_ref):
    block, width = hid_ref.shape
    total = sum(o[...].astype(F32) for o in (o0_ref, o1_ref, o2_ref, o3_ref))
    line = total[block : block + 1, :]
    square = line[:, 0:block] + line[:, block : 2 * block] + line[:, 2 * block : 3 * block]
    scale = to_column(lax.rsqrt(square / units + NORM_EPS))
    res = hid_ref[...].astype(F32) + total[0:block, :] * scale
    out_ref[0:block, :] = (res * gain_ref[m : m + 1, :]).astype(BF16)
    line = jnp.concatenate(
        pieces(to_row(jnp.sum(res * res, axis=1, keepdims=True))) + [jnp.zeros((1, width - 3 * block), F32)], axis=1
    )
    out_ref[block : block + 16, :] = jnp.broadcast_to(line, (16, width)).astype(BF16)


def residual_block(m, at, parts, hidden, gain, units, after=()):
    block, width = parts[0].shape[0] - 16, parts[0].shape[1]
    whole = pl.BlockSpec((block + 16, width), lambda g, at: (0, 0))
    return pl.pallas_call(
        drop(functools.partial(residual_kernel, m, float(units)), 7, len(after)),
        grid_spec=pltpu.PrefetchScalarGridSpec(
            num_scalar_prefetch=1,
            grid=(1,),
            in_specs=[whole] * 4
            + [
                pl.BlockSpec((None, block, width), lambda g, at: (m, at[1], at[0])),
                pl.BlockSpec((2, width), lambda g, at: (0, at[0])),
            ]
            + [ANYWHERE] * len(after),
            out_specs=whole,
        ),
        out_shape=jax.ShapeDtypeStruct((block + 16, width), BF16),
        cost_estimate=pl.CostEstimate(flops=10**6, bytes_accessed=10**6, transcendentals=100),
        name="residual_block",
    )(at, *parts, hidden, gain, *after)


def join_kernel(at_ref, u0_ref, u1_ref, u2_ref, u3_ref, out_ref):
    block, width = u0_ref.shape[0] - 16, u0_ref.shape[1]
    square = jnp.zeros((1, block), F32)
    for k, u in enumerate((u0_ref, u1_ref, u2_ref, u3_ref)):
        at = pl.multiple_of(lax.rem(at_ref[0] + 4 - k, 4) * width, width)
        out_ref[0:block, pl.ds(at, width)] = u[0:block, :]
        line = u[block : block + 16, :].astype(F32)[0:1, :]
        square = square + line[:, 0:block] + line[:, block : 2 * block] + line[:, 2 * block : 3 * block]
    scale = lax.rsqrt(square / out_ref.shape[1] + NORM_EPS)
    out_ref[block : block + 16, :] = jnp.zeros((16, out_ref.shape[1]), BF16)
    line = jnp.concatenate(pieces(scale), axis=1)
    out_ref[block : block + 16, 0 : 3 * block] = jnp.broadcast_to(line, (16, 3 * block)).astype(BF16)


def join_columns(at, parts, after=()):
    tall, width = parts[0].shape
    vm = pl.BlockSpec(memory_space=pltpu.VMEM)
    return pl.pallas_call(
        drop(join_kernel, 5, len(after)),
        in_specs=[pl.BlockSpec(memory_space=pltpu.SMEM)] + [vm] * 4 + [ANYWHERE] * len(after),
        out_specs=vm,
        out_shape=jax.ShapeDtypeStruct((tall, 4 * width), BF16),
        cost_estimate=pl.CostEstimate(flops=10**5, bytes_accessed=10**6, transcendentals=100),
        name="join_columns",
    )(at, *parts, *after)


def head_kernel(place_ref, at_ref, x0_ref, x1_ref, x2_ref, x3_ref, w_ref, tgt_ref, out_ref, acc_ref, scale_ref):
    block = x0_ref.shape[0] - 16
    vocab = w_ref.shape[1]
    step = pl.program_id(0)
    tiles = (x0_ref, x1_ref, x2_ref, x3_ref)

    @pl.when(step == 0)
    def _():
        for k, x in enumerate(tiles):
            line = x[block : block + 16, 0 : 3 * block].astype(F32)[0:1, :]
            scale_ref[k : k + 1, :] = (
                line[:, 0:block] + line[:, block : 2 * block] + line[:, 2 * block : 3 * block]
            )

    for n in range(2):
        rows = jnp.concatenate([x[0:block, :] for x in tiles[2 * n : 2 * n + 2]], axis=0)
        raw = contract(rows, w_ref[...], ((1,), (0,)))
        span = slice(2 * n * block, 2 * (n + 1) * block)

        @pl.when(step == 0)
        def _():
            acc_ref[span, :] = raw

        @pl.when(step > 0)
        def _():
            acc_ref[span, :] += raw

    @pl.when(step == pl.num_programs(0) - 1)
    def _():
        for k in range(4):
            at = lax.rem(at_ref[1] + 4 - k, 4)
            logits = acc_ref[k * block : (k + 1) * block, :] * to_column(scale_ref[k : k + 1, :])
            top = jnp.max(logits, axis=1, keepdims=True)
            lse = top + jnp.log(jnp.sum(jnp.exp(logits - top), axis=1, keepdims=True))
            target = to_column((tgt_ref[pl.ds(at, 1), :] - place_ref[0] * vocab).astype(F32))
            column = lax.broadcasted_iota(jnp.int32, logits.shape, 1).astype(F32)
            chosen = jnp.sum(jnp.where(column == target, logits, 0.0), axis=1, keepdims=True)
            for which, value in enumerate((lse, chosen)):
                out_ref[:, pl.ds(which * 4 + at, 1), :] = jnp.broadcast_to(
                    to_row(value)[None], (out_ref.shape[0], 1, block)
                )


def head_stats(m, place, at, parts, head, tgt, group, after=(), chunks=4):
    tall, depth = parts[0].shape
    block = tall - 16
    vocab = head.shape[2]
    deep = depth // chunks
    return pl.pallas_call(
        drop(head_kernel, 8, len(after)),
        grid_spec=pltpu.PrefetchScalarGridSpec(
            num_scalar_prefetch=2,
            grid=(chunks,),
            in_specs=[pl.BlockSpec((tall, deep), lambda i, pf, at: (0, i))] * 4
            + [
                pl.BlockSpec((None, deep, vocab), lambda i, pf, at: (m, i, 0)),
                pl.BlockSpec(tgt.shape, lambda i, pf, at: (0, 0)),
            ]
            + [ANYWHERE] * len(after),
            out_specs=pl.BlockSpec((group, 8, block), lambda i, pf, at: (0, 0, 0)),
            scratch_shapes=[pltpu.VMEM((4 * block, vocab), F32), pltpu.VMEM((4, block), F32)],
        ),
        out_shape=jax.ShapeDtypeStruct((group, 8, block), F32),
        cost_estimate=pl.CostEstimate(
            flops=8 * block * depth * vocab, bytes_accessed=2 * depth * vocab, transcendentals=4 * block * vocab
        ),
        name="head_stats",
    )(place, at, *parts, head, tgt, *after)


def diff_kernel(s0_ref, s1_ref, live_ref, seg_ref, diff_ref, sums_ref):
    scores = []
    for ref in (s0_ref, s1_ref):
        part = ref[...]
        lse = part[:, 0:4, :]
        top = jnp.max(lse, axis=0)
        total = top + jnp.log(jnp.sum(jnp.exp(lse - top[None]), axis=0))
        scores.append(jnp.sum(part[:, 4:8, :], axis=0) - total)
    lines = lax.broadcasted_iota(jnp.int32, (4, 128), 0)
    alive = jnp.where(lines < 2, live_ref[0].astype(F32), live_ref[1].astype(F32))
    diff = alive * (scores[0] - scores[1])
    diff_ref[...] = diff
    which = lax.broadcasted_iota(jnp.int32, (8, 128), 0)
    sums = jnp.zeros((8, 128), F32)
    for j in range(4):
        mine = jnp.sum(jnp.where(seg_ref[...] == j, diff, 0.0), axis=1, keepdims=True)
        sums = jnp.where(which == j, jnp.sum(mine, axis=0, keepdims=True), sums)
    sums_ref[...] = jnp.broadcast_to(sums[None], sums_ref.shape)


def token_diffs(s0, s1, live, seg, devices):
    vm = pl.BlockSpec(memory_space=pltpu.VMEM)
    return pl.pallas_call(
        diff_kernel,
        in_specs=[vm, vm, pl.BlockSpec(memory_space=pltpu.SMEM), vm],
        out_shape=(jax.ShapeDtypeStruct((4, 128), F32), jax.ShapeDtypeStruct((devices, 8, 128), F32)),
        name="token_diffs",
    )(s0, s1, live, seg)


def turn_kernel(w_ref, out0_ref, out1_ref, sems):
    width = out0_ref.shape[2]
    copies = [
        pltpu.make_async_copy(w_ref.at[m, :, pl.ds(j * width, width)], out.at[j], sems.at[m * 4 + j])
        for m, out in enumerate((out0_ref, out1_ref))
        for j in range(4)
    ]
    for copy in copies:
        copy.start()
    for copy in copies:
        copy.wait()


def turned(w_out):
    _, inner, depth = w_out.shape
    return pl.pallas_call(
        turn_kernel,
        in_specs=[ANYWHERE],
        out_specs=[ANYWHERE] * 2,
        out_shape=[jax.ShapeDtypeStruct((4, inner, depth // 4), w_out.dtype)] * 2,
        scratch_shapes=[pltpu.SemaphoreType.DMA((8,))],
        cost_estimate=pl.CostEstimate(flops=0, bytes_accessed=4 * 10**6, transcendentals=0),
        name="turned",
    )(w_out)


def ring(value, axis, by):
    return lax.ppermute(value, axis, [(i, (i + by) % 4) for i in range(4)])


def gathered(value, axis):
    return [value] + [ring(value, axis, k) for k in (1, 2, 3)]


def per_device(
    hidden, w_inner, w_state, w_step, step_bias, rate, skip_gain, norm_gain, w_out, final_gain, head, pool,
    targets, segment_ids, flags, pages, live, owners,
):
    rows = targets.shape[0]
    depth = hidden.shape[2]
    inner = w_inner.shape[3]
    group = lax.axis_size(VOC)
    devices = lax.axis_size(SEQ)
    place = lax.axis_index(VOC).astype(jnp.int32).reshape(1)
    seg = segment_ids.reshape(1, rows)
    tgt = targets.reshape(4, rows // 4)
    w_step = jnp.swapaxes(w_step, 1, 2)
    ways = (("x", "z"), ("z", "x"))
    both = range(2)
    at = [
        jnp.stack([lax.axis_index(along), lax.axis_index(across)]).astype(jnp.int32) for along, across in ways
    ]
    turns = turned(w_out)
    weights = [lax.all_to_all(turns[m], ways[m][0], 0, 0) for m in both]

    def mix(m, after):
        y, gate, c, e, pay = mix_local(
            m, hidden, w_inner, w_state, w_step, step_bias, rate, skip_gain, seg, after
        )
        recv = [lax.ppermute(pay, SEQ, [(i, i + k) for i in range(devices - k)]) for k in range(1, REACH + 1)]
        return y, gate, c, e, recv

    mixed = [None, None]
    mixed[0] = mix(0, ())
    mixed[1] = mix(1, (mixed[0][2],))
    gated, parts, res, full, stats = [], [], [], [], []
    for m in both:
        y, gate, c, e, recv = mixed[m]
        gated.append(gate_out(m, pages, flags, y, gate, c, e, recv, pool, norm_gain, (mixed[1][2],)))
    for m in both:
        out = out_blocks(at[m], gathered(gated[m], ways[m][0]), weights[m], (gated[1],))
        parts.append([out[0]] + [ring(out[k], ways[m][1], k) for k in (1, 2, 3)])
    for m in both:
        res.append(residual_block(m, at[m], parts[m], hidden, final_gain, inner * group, (parts[1][0],)))
    for m in both:
        full.append(join_columns(at[m], gathered(res[m], ways[m][0]), (res[1],)))
    for m in both:
        stat = head_stats(m, place, at[m], gathered(full[m], ways[m][1]), head, tgt, group, (full[1],))
        stats.append(lax.all_to_all(stat, VOC, 0, 0))
    diff, sums = token_diffs(stats[0], stats[1], live, segment_ids.reshape(4, 128), devices)
    sums = jnp.sum(lax.all_to_all(sums, SEQ, 0, 0)[:, 0:4, 0], axis=0)
    owned = jnp.where(owners == lax.axis_index(SEQ), sums, 0.0)
    return diff.reshape(rows), owned[None]


def solution(mesh):
    seq, vocab = mesh.devices.shape
    fine = Mesh(mesh.devices.reshape(seq // 2, 2, 4, vocab // 4), ("y", "core", "x", "z"))
    placed = (
        P(None, SEQ, None),
        P(None, None, None, VOC),
        P(),
        P(None, None, VOC),
        P(None, VOC),
        P(None, VOC),
        P(None, VOC),
        P(None, VOC),
        P(None, VOC, None),
        P(),
        P(None, None, VOC),
        P(None, None, VOC, None, None),
        P(SEQ),
        P(SEQ),
        P(),
        P(),
        P(SEQ),
        P(),
    )
    return jax.shard_map(
        per_device, mesh=fine, in_specs=placed, out_specs=(P(SEQ), P(SEQ, None)), check_vma=False
    )
```

```python
import functools

import jax
import jax.numpy as jnp
from jax import lax
from jax.experimental import pallas as pl
from jax.experimental.pallas import tpu as pltpu
from jax.sharding import Mesh
from jax.sharding import PartitionSpec as P

NORM_EPS = 1e-05
SPAN = 256
REACH = 4
SEQ = ("y", "core")
VOC = ("x", "z")
F32 = jnp.float32
BF16 = jnp.bfloat16
LOW = -1e30


def silu(v):
    return v / (1.0 + jnp.exp(-v))


def contract(a, b, dims):
    return lax.dot_general(a, b, (dims, ((), ())), preferred_element_type=F32)


def drop(kernel, inputs, count):
    def body(*refs):
        return kernel(*refs[:inputs], *refs[inputs + count :])

    return body


ANYWHERE = pl.BlockSpec(memory_space=pl.ANY)


def pieces(value):
    high = value.astype(BF16).astype(F32)
    mid = (value - high).astype(BF16).astype(F32)
    return [high, mid, value - high - mid]


def to_column(row):
    return jnp.transpose(jnp.broadcast_to(row, (8, row.shape[1])))[:, 0:1]


def to_row(column):
    return jnp.transpose(jnp.broadcast_to(column, (column.shape[0], 8)))[0:1, :]


def as_column(row):
    count = row.shape[1]
    spread = jnp.broadcast_to(row, (count, count))
    eye = lax.broadcasted_iota(jnp.int32, spread.shape, 0) == lax.broadcasted_iota(jnp.int32, spread.shape, 1)
    return jnp.sum(jnp.where(eye, spread, 0.0), axis=1, keepdims=True)


def mix_kernel(
    tok_ref, wi_ref, ws_ref, wp_ref, bias_ref, rate_ref, skip_ref, seg_ref,
    y_ref, gate_ref, c_ref, e_ref, pay_ref, val_ref, st_ref, stp_ref,
):
    m = pl.program_id(0)
    k = pl.program_id(1)
    inner = y_ref.shape[1]

    @pl.when(k == 0)
    def _():
        gate_ref[...] = jnp.zeros_like(gate_ref)
        val_ref[...] = jnp.zeros_like(val_ref)
        st_ref[...] = jnp.zeros_like(st_ref)
        stp_ref[...] = jnp.zeros_like(stp_ref)

    tokens = tok_ref[...]
    gate_ref[...] += contract(tokens, wi_ref[:, 0:inner], ((1,), (0,)))
    val_ref[...] += contract(tokens, wi_ref[:, inner:], ((1,), (0,)))
    st_ref[...] += contract(tokens, ws_ref[...], ((1,), (0,)))
    stp_ref[...] += contract(tokens, wp_ref[...], ((1,), (1,)))

    @pl.when(k == pl.num_programs(1) - 1)
    def _():
        scan_rows(
            m, bias_ref, rate_ref, skip_ref, seg_ref, y_ref, c_ref, e_ref, pay_ref, val_ref, st_ref, stp_ref
        )


def scan_rows(m, bias_ref, rate_ref, skip_ref, seg_ref, y_ref, c_ref, e_ref, pay_ref, val_ref, st_ref, stp_ref):
    rows, inner = y_ref.shape
    heads = bias_ref.shape[1]
    wide = inner // heads
    state = c_ref.shape[1]
    seg = seg_ref[...]
    raw = jnp.transpose(stp_ref[...])[0:heads, :] + as_column(bias_ref[pl.ds(m, 1), :])
    dt = jnp.maximum(raw, 0.0) + jnp.log1p(jnp.exp(-jnp.abs(raw)))
    la = -dt * as_column(rate_ref[pl.ds(m, 1), :])
    skip = as_column(skip_ref[pl.ds(m, 1), :])
    lane = lax.broadcasted_iota(jnp.int32, la.shape, 1)
    run = la
    step = 1
    while step < rows:
        run = run + jnp.where(lane >= step, pltpu.roll(run, step, 1), 0.0)
        step *= 2
    last = jnp.max(seg, axis=1, keepdims=True)
    base = jnp.zeros_like(la)
    for j in range(4):
        base_j = jnp.sum(jnp.where(seg < j, la, 0.0), axis=1, keepdims=True)
        base = jnp.where(seg == j, base_j, base)
    total = jnp.sum(la, axis=1, keepdims=True)
    grow = jnp.exp(run - base)
    keep = jnp.where(seg == last, jnp.exp(jnp.minimum(total - run, 0.0)) * dt, 0.0)
    tail = jnp.exp(jnp.sum(jnp.where(seg == last, la, 0.0), axis=1, keepdims=True))
    cols = jnp.transpose(jnp.concatenate([run, keep], axis=0))
    segf = jnp.broadcast_to(seg.astype(F32), (heads, rows))
    ecol = jnp.transpose(jnp.concatenate([grow, segf], axis=0))
    e_ref[...] = ecol
    values = silu(val_ref[...]).astype(BF16)
    in_map = silu(st_ref[:, 0:state]).astype(BF16)
    out_map = silu(st_ref[:, state:]).astype(BF16)
    c_ref[...] = out_map
    vf = values.astype(F32)
    kept = jnp.concatenate(
        [vf[:, h * wide : (h + 1) * wide] * cols[:, heads + h : heads + h + 1] for h in range(heads)], axis=1
    ).astype(BF16)
    added = contract(kept, in_map, ((0,), (0,)))
    pay_ref[0:inner, :] = added.astype(BF16)
    high = tail.astype(BF16).astype(F32)
    low = tail - high
    meta = jnp.concatenate(
        [
            jnp.broadcast_to(high, (heads, state)),
            jnp.broadcast_to(low, (heads, state)),
            jnp.broadcast_to(last.astype(F32) + 1.0, (8, state)),
        ],
        axis=0,
    )
    pay_ref[inner : inner + 16, :] = meta.astype(BF16)
    blocks = rows // SPAN
    for i in range(blocks):
        t0 = i * SPAN
        acc = [vf[t0 : t0 + SPAN, h * wide : (h + 1) * wide] * skip[h : h + 1, :] for h in range(heads)]
        for j in range(i + 1):
            s0 = j * SPAN
            scores = contract(out_map[t0 : t0 + SPAN], in_map[s0 : s0 + SPAN], ((1,), (1,)))
            same = ecol[t0 : t0 + SPAN, heads : heads + 1] == segf[0:1, s0 : s0 + SPAN]
            if i == j:
                same = same & (
                    lax.broadcasted_iota(jnp.int32, (SPAN, SPAN), 0)
                    >= lax.broadcasted_iota(jnp.int32, (SPAN, SPAN), 1)
                )
            for h in range(heads):
                gap = cols[t0 : t0 + SPAN, h : h + 1] - run[h : h + 1, s0 : s0 + SPAN]
                weight = jnp.exp(jnp.where(same, gap, LOW)) * (scores * dt[h : h + 1, s0 : s0 + SPAN])
                acc[h] = acc[h] + contract(
                    weight.astype(BF16), values[s0 : s0 + SPAN, h * wide : (h + 1) * wide], ((1,), (0,))
                )
        y_ref[t0 : t0 + SPAN, :] = jnp.concatenate(acc, axis=1)


def mix_local(hidden, w_inner, w_state, w_step, bias, rate, skip, seg, chunks=4):
    models, rows, depth = hidden.shape
    inner = w_inner.shape[2] // 2
    state = w_state.shape[2] // 2
    heads = bias.shape[1]
    deep = depth // chunks
    whole = lambda a: pl.BlockSpec(a.shape, lambda m, k: (0,) * a.ndim)
    shapes = ((rows, inner), F32), ((rows, inner), F32), ((rows, state), BF16), ((rows, 2 * heads), F32), (
        (inner + 16, state), BF16)
    return pl.pallas_call(
        mix_kernel,
        grid=(models, chunks),
        in_specs=[
            pl.BlockSpec((None, rows, deep), lambda m, k: (m, 0, k)),
            pl.BlockSpec((None, deep, 2 * inner), lambda m, k: (m, k, 0)),
            pl.BlockSpec((None, deep, 2 * state), lambda m, k: (m, k, 0)),
            pl.BlockSpec((None, heads, deep), lambda m, k: (m, 0, k)),
            whole(bias), whole(rate), whole(skip), whole(seg),
        ],
        out_specs=[pl.BlockSpec((None,) + shape, lambda m, k: (m, 0, 0)) for shape, _ in shapes],
        out_shape=[jax.ShapeDtypeStruct((models,) + shape, kind) for shape, kind in shapes],
        scratch_shapes=[
            pltpu.VMEM((rows, inner), F32), pltpu.VMEM((rows, 2 * state), F32), pltpu.VMEM((rows, heads), F32)
        ],
        cost_estimate=pl.CostEstimate(flops=10**10, bytes_accessed=16 * 10**6, transcendentals=2 * 10**6),
        name="mix_local",
    )(hidden, w_inner, w_state, w_step, bias, rate, skip, seg)


def gate_kernel(
    m, pages_ref, flags_ref, y_ref, gate_ref, c_ref, e_ref, r1_ref, r2_ref, r3_ref, r4_ref,
    p0_ref, p1_ref, p2_ref, p3_ref, gain_ref, out_ref,
):
    rows, inner = y_ref.shape
    heads = p0_ref.shape[0]
    wide = inner // heads
    state = c_ref.shape[1]
    e_col = e_ref[...]
    seg_col = e_col[:, heads : heads + 1]
    seg_first = e_col[0:1, heads : heads + 1]
    init = [
        p.reshape(inner, state)[...].astype(F32) * flags_ref[j].astype(F32)
        for j, p in enumerate((p0_ref, p1_ref, p2_ref, p3_ref))
    ]
    through = jnp.ones((heads, state), F32)
    parts = [jnp.zeros((wide, state), F32) for _ in range(heads)]
    for r in (r1_ref, r2_ref, r3_ref, r4_ref):
        meta = r[inner : inner + 16, :].astype(F32)
        hit = meta[8:9, :] == seg_first + 1.0
        piece = r[0:inner, :].astype(F32)
        weight = jnp.where(hit, through, 0.0)
        for h in range(heads):
            parts[h] = parts[h] + weight[h : h + 1, :] * piece[h * wide : (h + 1) * wide, :]
        through = jnp.where(hit, through * (meta[0:heads] + meta[heads : 2 * heads]), through)
    prior = jnp.concatenate(parts, axis=0)
    through = jnp.concatenate([jnp.broadcast_to(through[h : h + 1, :], (wide, state)) for h in range(heads)], axis=0)
    out_map = c_ref[...]
    picked = jnp.zeros((rows, inner), F32)
    for j in range(4):
        start = jnp.where(seg_first == float(j), prior + through * init[j], init[j])
        high = start.astype(BF16)
        low = (start - high.astype(F32)).astype(BF16)
        from_state = contract(out_map, high, ((1,), (1,))) + contract(out_map, low, ((1,), (1,)))
        picked = jnp.where(seg_col == float(j), from_state, picked)
    spread = jnp.concatenate([jnp.broadcast_to(e_col[:, h : h + 1], (rows, wide)) for h in range(heads)], axis=1)
    gated = (y_ref[...] + picked * spread) * silu(gate_ref[...])
    square = jnp.sum(gated * gated, axis=1, keepdims=True)
    out_ref[0:rows, :] = (gated * gain_ref[m : m + 1, :]).astype(BF16)
    lines = jnp.transpose(jnp.broadcast_to(square, (rows, 8)))[0:1, :]
    halves = jnp.concatenate([lines[:, 0:inner], lines[:, inner:]], axis=0)
    extra = jnp.concatenate(pieces(halves) + [jnp.zeros((10, inner), F32)], axis=0)
    out_ref[rows : rows + 16, :] = extra.astype(BF16)


def gate_out(m, pages, flags, y, gate, c, e, recv, pool, gain, after=()):
    rows, inner = y.shape[1:]
    heads = pool.shape[2]
    state = c.shape[2]
    whole = lambda a: pl.BlockSpec(a.shape, lambda g, pg, fl: (0,) * a.ndim)
    mine = lambda a: pl.BlockSpec((None,) + a.shape[1:], lambda g, pg, fl: (m, 0, 0))
    page = lambda j: pl.BlockSpec(
        (None, None, heads, pool.shape[3], state), lambda g, pg, fl: (m, pg[j], 0, 0, 0)
    )
    return pl.pallas_call(
        drop(functools.partial(gate_kernel, m), 15, len(after)),
        grid_spec=pltpu.PrefetchScalarGridSpec(
            num_scalar_prefetch=2,
            grid=(1,),
            in_specs=[mine(y), mine(gate), mine(c), mine(e)]
            + [mine(r) for r in recv]
            + [page(j) for j in range(4)]
            + [whole(gain)]
            + [ANYWHERE] * len(after),
            out_specs=pl.BlockSpec((rows + 16, inner), lambda g, pg, fl: (0, 0)),
        ),
        out_shape=jax.ShapeDtypeStruct((rows + 16, inner), BF16),
        cost_estimate=pl.CostEstimate(flops=10**9, bytes_accessed=4 * 10**6, transcendentals=10**5),
        name="gate_out",
    )(pages, flags, y, gate, c, e, *recv, pool, pool, pool, pool, gain, *after)


def out_kernel(at_ref, g0_ref, g1_ref, g2_ref, g3_ref, w_ref, o0_ref, o1_ref, o2_ref, o3_ref, acc_ref, sq_ref):
    rows, width = acc_ref.shape
    inner = g0_ref.shape[1]
    block = rows // 4
    along, across = at_ref[0], at_ref[1]
    gathered = (g0_ref, g1_ref, g2_ref, g3_ref)
    extra = sum(g[rows : rows + 16, :].astype(F32) for g in gathered)
    square = extra[0:2] + extra[2:4] + extra[4:6]
    for n in range(4):
        sq_ref[n : n + 1, :] = square[n // 2 : n // 2 + 1, (n % 2) * block : (n % 2 + 1) * block]
    acc_ref[...] = sum(
        contract(g[0:rows, :], w_ref[lax.rem(along + 4 - k, 4)], ((1,), (0,))) for k, g in enumerate(gathered)
    )
    for k, out in enumerate((o0_ref, o1_ref, o2_ref, o3_ref)):
        at = lax.rem(across + k, 4)
        out[0:block, :] = acc_ref[pl.ds(pl.multiple_of(at * block, block), block), :].astype(BF16)
        line = jnp.concatenate(pieces(sq_ref[pl.ds(at, 1), :]) + [jnp.zeros((1, width - 3 * block), F32)], axis=1)
        out[block : block + 16, :] = jnp.broadcast_to(line, (16, width)).astype(BF16)


def out_blocks(at, gathered, w, after=()):
    rows = gathered[0].shape[0] - 16
    width = w.shape[2]
    block = rows // 4
    vm = pl.BlockSpec(memory_space=pltpu.VMEM)
    return pl.pallas_call(
        drop(out_kernel, 6, len(after)),
        in_specs=[pl.BlockSpec(memory_space=pltpu.SMEM)] + [vm] * 5 + [ANYWHERE] * len(after),
        out_specs=[vm] * 4,
        out_shape=[jax.ShapeDtypeStruct((block + 16, width), BF16)] * 4,
        scratch_shapes=[pltpu.VMEM((rows, width), F32), pltpu.VMEM((4, block), F32)],
        cost_estimate=pl.CostEstimate(flops=10**9, bytes_accessed=3 * 10**6, transcendentals=0),
        name="out_blocks",
    )(at, *gathered, w, *after)


def residual_kernel(m, units, at_ref, o0_ref, o1_ref, o2_ref, o3_ref, hid_ref, gain_ref, out_ref):
    block, width = hid_ref.shape
    total = sum(o[...].astype(F32) for o in (o0_ref, o1_ref, o2_ref, o3_ref))
    line = total[block : block + 1, :]
    square = line[:, 0:block] + line[:, block : 2 * block] + line[:, 2 * block : 3 * block]
    scale = to_column(lax.rsqrt(square / units + NORM_EPS))
    res = hid_ref[...].astype(F32) + total[0:block, :] * scale
    out_ref[0:block, :] = (res * gain_ref[m : m + 1, :]).astype(BF16)
    line = jnp.concatenate(
        pieces(to_row(jnp.sum(res * res, axis=1, keepdims=True))) + [jnp.zeros((1, width - 3 * block), F32)], axis=1
    )
    out_ref[block : block + 16, :] = jnp.broadcast_to(line, (16, width)).astype(BF16)


def residual_block(m, at, parts, hidden, gain, units, after=()):
    block, width = parts[0].shape[0] - 16, parts[0].shape[1]
    whole = pl.BlockSpec((block + 16, width), lambda g, at: (0, 0))
    return pl.pallas_call(
        drop(functools.partial(residual_kernel, m, float(units)), 7, len(after)),
        grid_spec=pltpu.PrefetchScalarGridSpec(
            num_scalar_prefetch=1,
            grid=(1,),
            in_specs=[whole] * 4
            + [
                pl.BlockSpec((None, block, width), lambda g, at: (m, at[1], at[0])),
                pl.BlockSpec((2, width), lambda g, at: (0, at[0])),
            ]
            + [ANYWHERE] * len(after),
            out_specs=whole,
        ),
        out_shape=jax.ShapeDtypeStruct((block + 16, width), BF16),
        cost_estimate=pl.CostEstimate(flops=10**6, bytes_accessed=10**6, transcendentals=100),
        name="residual_block",
    )(at, *parts, hidden, gain, *after)


def join_kernel(at_ref, u0_ref, u1_ref, u2_ref, u3_ref, out_ref):
    block, width = u0_ref.shape[0] - 16, u0_ref.shape[1]
    square = jnp.zeros((1, block), F32)
    for k, u in enumerate((u0_ref, u1_ref, u2_ref, u3_ref)):
        at = pl.multiple_of(lax.rem(at_ref[0] + 4 - k, 4) * width, width)
        out_ref[0:block, pl.ds(at, width)] = u[0:block, :]
        line = u[block : block + 16, :].astype(F32)[0:1, :]
        square = square + line[:, 0:block] + line[:, block : 2 * block] + line[:, 2 * block : 3 * block]
    scale = lax.rsqrt(square / out_ref.shape[1] + NORM_EPS)
    out_ref[block : block + 16, :] = jnp.zeros((16, out_ref.shape[1]), BF16)
    line = jnp.concatenate(pieces(scale), axis=1)
    out_ref[block : block + 16, 0 : 3 * block] = jnp.broadcast_to(line, (16, 3 * block)).astype(BF16)


def join_columns(at, parts, after=()):
    tall, width = parts[0].shape
    vm = pl.BlockSpec(memory_space=pltpu.VMEM)
    return pl.pallas_call(
        drop(join_kernel, 5, len(after)),
        in_specs=[pl.BlockSpec(memory_space=pltpu.SMEM)] + [vm] * 4 + [ANYWHERE] * len(after),
        out_specs=vm,
        out_shape=jax.ShapeDtypeStruct((tall, 4 * width), BF16),
        cost_estimate=pl.CostEstimate(flops=10**5, bytes_accessed=10**6, transcendentals=100),
        name="join_columns",
    )(at, *parts, *after)


def head_kernel(m, place_ref, at_ref, x0_ref, x1_ref, x2_ref, x3_ref, w_ref, tgt_ref, out_ref, wv_ref, acc_ref, sems):
    block = x0_ref.shape[0] - 16
    vocab = w_ref.shape[2]
    cut = 768
    spans = (pl.ds(0, cut), pl.ds(cut, vocab - cut))
    copies = [
        pltpu.make_async_copy(w_ref.at[m, :, span], wv_ref.at[:, span], sems.at[n]) for n, span in enumerate(spans)
    ]
    for copy in copies:
        copy.start()
    tiles = (x0_ref, x1_ref, x2_ref, x3_ref)
    for copy, span in zip(copies, spans):
        copy.wait()
        for n in range(2):
            rows = jnp.concatenate([x[0:block, :] for x in tiles[2 * n : 2 * n + 2]], axis=0)
            acc_ref[2 * n * block : 2 * (n + 1) * block, span] = contract(rows, wv_ref[:, span], ((1,), (0,)))
    for k, x in enumerate(tiles):
        at = lax.rem(at_ref[1] + 4 - k, 4)
        line = x[block : block + 16, 0 : 3 * block].astype(F32)[0:1, :]
        scale = to_column(line[:, 0:block] + line[:, block : 2 * block] + line[:, 2 * block : 3 * block])
        logits = acc_ref[k * block : (k + 1) * block, :] * scale
        top = jnp.max(logits, axis=1, keepdims=True)
        lse = top + jnp.log(jnp.sum(jnp.exp(logits - top), axis=1, keepdims=True))
        target = to_column((tgt_ref[pl.ds(at, 1), :] - place_ref[0] * vocab).astype(F32)).astype(jnp.int32)
        column = lax.broadcasted_iota(jnp.int32, logits.shape, 1)
        chosen = jnp.sum(jnp.where(column == target, logits, 0.0), axis=1, keepdims=True)
        for which, value in enumerate((lse, chosen)):
            out_ref[:, pl.ds(which * 4 + at, 1), :] = jnp.broadcast_to(
                to_row(value)[None], (out_ref.shape[0], 1, block)
            )


def head_stats(m, place, at, parts, head, tgt, group, after=()):
    tall, depth = parts[0].shape
    block = tall - 16
    vocab = head.shape[2]
    vm = pl.BlockSpec(memory_space=pltpu.VMEM)
    sm = pl.BlockSpec(memory_space=pltpu.SMEM)
    return pl.pallas_call(
        drop(functools.partial(head_kernel, m), 8, len(after)),
        in_specs=[sm, sm] + [vm] * 4 + [ANYWHERE, vm] + [ANYWHERE] * len(after),
        out_specs=vm,
        scratch_shapes=[
            pltpu.VMEM((depth, vocab), BF16), pltpu.VMEM((4 * block, vocab), F32), pltpu.SemaphoreType.DMA((2,))
        ],
        out_shape=jax.ShapeDtypeStruct((group, 8, block), F32),
        cost_estimate=pl.CostEstimate(
            flops=8 * block * depth * vocab, bytes_accessed=2 * depth * vocab, transcendentals=4 * block * vocab
        ),
        name="head_stats",
    )(place, at, *parts, head, tgt, *after)


def diff_kernel(s0_ref, s1_ref, live_ref, seg_ref, diff_ref, sums_ref):
    scores = []
    for ref in (s0_ref, s1_ref):
        part = ref[...]
        lse = part[:, 0:4, :]
        top = jnp.max(lse, axis=0)
        total = top + jnp.log(jnp.sum(jnp.exp(lse - top[None]), axis=0))
        scores.append(jnp.sum(part[:, 4:8, :], axis=0) - total)
    lines = lax.broadcasted_iota(jnp.int32, (4, 128), 0)
    alive = jnp.where(lines < 2, live_ref[0].astype(F32), live_ref[1].astype(F32))
    diff = alive * (scores[0] - scores[1])
    diff_ref[...] = diff
    which = lax.broadcasted_iota(jnp.int32, (8, 128), 0)
    sums = jnp.zeros((8, 128), F32)
    for j in range(4):
        mine = jnp.sum(jnp.where(seg_ref[...] == j, diff, 0.0), axis=1, keepdims=True)
        sums = jnp.where(which == j, jnp.sum(mine, axis=0, keepdims=True), sums)
    sums_ref[...] = jnp.broadcast_to(sums[None], sums_ref.shape)


def token_diffs(s0, s1, live, seg, devices):
    vm = pl.BlockSpec(memory_space=pltpu.VMEM)
    return pl.pallas_call(
        diff_kernel,
        in_specs=[vm, vm, pl.BlockSpec(memory_space=pltpu.SMEM), vm],
        out_shape=(jax.ShapeDtypeStruct((4, 128), F32), jax.ShapeDtypeStruct((devices, 8, 128), F32)),
        name="token_diffs",
    )(s0, s1, live, seg)


def turn_kernel(w_ref, out_ref):
    out_ref[...] = w_ref[...]


def turned(m, w_out):
    _, inner, depth = w_out.shape
    width = depth // 4
    return pl.pallas_call(
        turn_kernel,
        grid=(4,),
        in_specs=[pl.BlockSpec((None, inner, width), lambda j: (m, 0, j))],
        out_specs=pl.BlockSpec((None, inner, width), lambda j: (j, 0, 0)),
        out_shape=jax.ShapeDtypeStruct((4, inner, width), w_out.dtype),
        cost_estimate=pl.CostEstimate(flops=0, bytes_accessed=2 * 10**6, transcendentals=0),
        name="turned",
    )(w_out)


def ring(value, axis, by):
    return lax.ppermute(value, axis, [(i, (i + by) % 4) for i in range(4)])


def gathered(value, axis):
    return [value] + [ring(value, axis, k) for k in (1, 2, 3)]


def per_device(
    hidden, w_inner, w_state, w_step, step_bias, rate, skip_gain, norm_gain, w_out, final_gain, head, pool,
    targets, segment_ids, flags, pages, live, owners,
):
    rows = targets.shape[0]
    depth = hidden.shape[2]
    inner = w_inner.shape[3]
    group = lax.axis_size(VOC)
    devices = lax.axis_size(SEQ)
    place = lax.axis_index(VOC).astype(jnp.int32).reshape(1)
    seg = segment_ids.reshape(1, rows)
    tgt = targets.reshape(4, rows // 4)
    w_inner = w_inner.reshape(2, depth, 2 * inner)
    w_state = w_state.reshape(2, depth, -1)
    w_step = jnp.swapaxes(w_step, 1, 2)
    ways = (("x", "z"), ("z", "x"))
    both = range(2)
    at = [
        jnp.stack([lax.axis_index(along), lax.axis_index(across)]).astype(jnp.int32) for along, across in ways
    ]
    weights = [lax.all_to_all(turned(m, w_out), ways[m][0], 0, 0) for m in both]
    y, gate, c, e, pay = mix_local(hidden, w_inner, w_state, w_step, step_bias, rate, skip_gain, seg)
    recv = [lax.ppermute(pay, SEQ, [(i, i + k) for i in range(devices - k)]) for k in range(1, REACH + 1)]
    gated, parts, res, full, stats = [], [], [], [], []
    for m in both:
        gated.append(gate_out(m, pages, flags, y, gate, c, e, recv, pool, norm_gain, tuple(gated)))
    for m in both:
        out = out_blocks(at[m], gathered(gated[m], ways[m][0]), weights[m], (gated[1],))
        parts.append([out[0]] + [ring(out[k], ways[m][1], k) for k in (1, 2, 3)])
    for m in both:
        res.append(residual_block(m, at[m], parts[m], hidden, final_gain, inner * group, (parts[1][0],)))
    blocks = [gathered(res[m], ways[m][0]) for m in both]
    for m in both:
        full.append(join_columns(at[m], blocks[m], tuple(blocks[1 - m][1:])))
    for m in both:
        stat = head_stats(m, place, at[m], gathered(full[m], ways[m][1]), head, tgt, group, (full[1],))
        stats.append(lax.all_to_all(stat, VOC, 0, 0))
    diff, sums = token_diffs(stats[0], stats[1], live, segment_ids.reshape(4, 128), devices)
    sums = jnp.sum(lax.all_to_all(sums, SEQ, 0, 0)[:, 0:4, 0], axis=0)
    owned = jnp.where(owners == lax.axis_index(SEQ), sums, 0.0)
    return diff.reshape(rows), owned[None]


def solution(mesh):
    seq, vocab = mesh.devices.shape
    fine = Mesh(mesh.devices.reshape(seq // 2, 2, 4, vocab // 4), ("y", "core", "x", "z"))
    placed = (
        P(None, SEQ, None),
        P(None, None, None, VOC),
        P(),
        P(None, None, VOC),
        P(None, VOC),
        P(None, VOC),
        P(None, VOC),
        P(None, VOC),
        P(None, VOC, None),
        P(),
        P(None, None, VOC),
        P(None, None, VOC, None, None),
        P(SEQ),
        P(SEQ),
        P(),
        P(),
        P(SEQ),
        P(),
    )
    return jax.shard_map(
        per_device, mesh=fine, in_specs=placed, out_specs=(P(SEQ), P(SEQ, None)), check_vma=False
    )
```

```python
import functools

import jax
import jax.numpy as jnp
from jax import lax
from jax.experimental import pallas as pl
from jax.experimental.pallas import tpu as pltpu
from jax.sharding import Mesh
from jax.sharding import PartitionSpec as P

NORM_EPS = 1e-05
SPAN = 256
REACH = 4
SEQ = ("y", "core")
VOC = ("x", "z")
F32 = jnp.float32
BF16 = jnp.bfloat16
LOW = -1e30
LOG2E = 1.4426950408889634


def silu(v):
    return v / (1.0 + jnp.exp(-v))


def contract(a, b, dims):
    return lax.dot_general(a, b, (dims, ((), ())), preferred_element_type=F32)


def drop(kernel, inputs, count):
    def body(*refs):
        return kernel(*refs[:inputs], *refs[inputs + count :])

    return body


ANYWHERE = pl.BlockSpec(memory_space=pl.ANY)


def pieces(value):
    high = value.astype(BF16).astype(F32)
    mid = (value - high).astype(BF16).astype(F32)
    return [high, mid, value - high - mid]


def to_column(row):
    return jnp.transpose(jnp.broadcast_to(row, (8, row.shape[1])))[:, 0:1]


def to_row(column):
    return jnp.transpose(jnp.broadcast_to(column, (column.shape[0], 8)))[0:1, :]


def as_column(row):
    count = row.shape[1]
    spread = jnp.broadcast_to(row, (count, count))
    eye = lax.broadcasted_iota(jnp.int32, spread.shape, 0) == lax.broadcasted_iota(jnp.int32, spread.shape, 1)
    return jnp.sum(jnp.where(eye, spread, 0.0), axis=1, keepdims=True)


def mix_kernel(
    tok_ref, wi_ref, ws_ref, wp_ref, bias_ref, rate_ref, skip_ref, seg_ref,
    y_ref, gate_ref, c_ref, e_ref, pay_ref, val_ref, st_ref, stp_ref,
):
    m = pl.program_id(0)
    k = pl.program_id(1)
    inner = y_ref.shape[1]

    @pl.when(k == 0)
    def _():
        gate_ref[...] = jnp.zeros_like(gate_ref)
        val_ref[...] = jnp.zeros_like(val_ref)
        st_ref[...] = jnp.zeros_like(st_ref)
        stp_ref[...] = jnp.zeros_like(stp_ref)

    tokens = tok_ref[...]
    state = c_ref.shape[1]
    gate_ref[...] += contract(tokens, wi_ref[0], ((1,), (0,)))
    val_ref[...] += contract(tokens, wi_ref[1], ((1,), (0,)))
    st_ref[:, 0:state] += contract(tokens, ws_ref[0], ((1,), (0,)))
    st_ref[:, state:] += contract(tokens, ws_ref[1], ((1,), (0,)))
    stp_ref[...] += contract(tokens, wp_ref[...], ((1,), (1,)))

    @pl.when(k == pl.num_programs(1) - 1)
    def _():
        scan_rows(
            m, bias_ref, rate_ref, skip_ref, seg_ref, y_ref, c_ref, e_ref, pay_ref, val_ref, st_ref, stp_ref
        )


def scan_rows(m, bias_ref, rate_ref, skip_ref, seg_ref, y_ref, c_ref, e_ref, pay_ref, val_ref, st_ref, stp_ref):
    rows, inner = y_ref.shape
    heads = bias_ref.shape[1]
    wide = inner // heads
    state = c_ref.shape[1]
    seg = seg_ref[...]
    raw = jnp.transpose(stp_ref[...])[0:heads, :] + as_column(bias_ref[pl.ds(m, 1), :])
    dt = jnp.maximum(raw, 0.0) + jnp.log1p(jnp.exp(-jnp.abs(raw)))
    la = -dt * as_column(rate_ref[pl.ds(m, 1), :])
    skip = as_column(skip_ref[pl.ds(m, 1), :])
    lane = lax.broadcasted_iota(jnp.int32, la.shape, 1)
    run = la
    step = 1
    while step < rows:
        run = run + jnp.where(lane >= step, pltpu.roll(run, step, 1), 0.0)
        step *= 2
    last = jnp.max(seg, axis=1, keepdims=True)
    base = jnp.zeros_like(la)
    for j in range(4):
        base_j = jnp.sum(jnp.where(seg < j, la, 0.0), axis=1, keepdims=True)
        base = jnp.where(seg == j, base_j, base)
    total = jnp.sum(la, axis=1, keepdims=True)
    grow = jnp.exp(run - base)
    keep = jnp.where(seg == last, jnp.exp(jnp.minimum(total - run, 0.0)) * dt, 0.0)
    tail = jnp.exp(jnp.sum(jnp.where(seg == last, la, 0.0), axis=1, keepdims=True))
    cols = jnp.transpose(jnp.concatenate([run, keep], axis=0))
    segf = jnp.broadcast_to(seg.astype(F32), (heads, rows))
    ecol = jnp.transpose(jnp.concatenate([grow, segf], axis=0))
    e_ref[...] = ecol
    values = silu(val_ref[...]).astype(BF16)
    in_map = silu(st_ref[:, 0:state]).astype(BF16)
    out_map = silu(st_ref[:, state:]).astype(BF16)
    c_ref[...] = out_map
    vf = values.astype(F32)
    kept = jnp.concatenate(
        [vf[:, h * wide : (h + 1) * wide] * cols[:, heads + h : heads + h + 1] for h in range(heads)], axis=1
    ).astype(BF16)
    added = contract(kept, in_map, ((0,), (0,)))
    pay_ref[0:inner, :] = added.astype(BF16)
    high = tail.astype(BF16).astype(F32)
    low = tail - high
    meta = jnp.concatenate(
        [
            jnp.broadcast_to(high, (heads, state)),
            jnp.broadcast_to(low, (heads, state)),
            jnp.broadcast_to(last.astype(F32) + 1.0, (8, state)),
        ],
        axis=0,
    )
    pay_ref[inner : inner + 16, :] = meta.astype(BF16)
    blocks = rows // SPAN
    for i in range(blocks):
        t0 = i * SPAN
        acc = [vf[t0 : t0 + SPAN, h * wide : (h + 1) * wide] * skip[h : h + 1, :] for h in range(heads)]
        for j in range(i + 1):
            s0 = j * SPAN
            scores = contract(out_map[t0 : t0 + SPAN], in_map[s0 : s0 + SPAN], ((1,), (1,)))
            same = ecol[t0 : t0 + SPAN, heads : heads + 1] == segf[0:1, s0 : s0 + SPAN]
            if i == j:
                same = same & (
                    lax.broadcasted_iota(jnp.int32, (SPAN, SPAN), 0)
                    >= lax.broadcasted_iota(jnp.int32, (SPAN, SPAN), 1)
                )
            for h in range(heads):
                gap = cols[t0 : t0 + SPAN, h : h + 1] - run[h : h + 1, s0 : s0 + SPAN]
                weight = jnp.exp(jnp.where(same, gap, LOW)) * (scores * dt[h : h + 1, s0 : s0 + SPAN])
                acc[h] = acc[h] + contract(
                    weight.astype(BF16), values[s0 : s0 + SPAN, h * wide : (h + 1) * wide], ((1,), (0,))
                )
        y_ref[t0 : t0 + SPAN, :] = jnp.concatenate(acc, axis=1)


def mix_local(hidden, w_inner, w_state, w_step, bias, rate, skip, seg, chunks=4):
    models, rows, depth = hidden.shape
    inner = w_inner.shape[3]
    state = w_state.shape[3]
    heads = bias.shape[1]
    deep = depth // chunks
    whole = lambda a: pl.BlockSpec(a.shape, lambda m, k: (0,) * a.ndim)
    shapes = ((rows, inner), F32), ((rows, inner), F32), ((rows, state), BF16), ((rows, 2 * heads), F32), (
        (inner + 16, state), BF16)
    return pl.pallas_call(
        mix_kernel,
        grid=(models, chunks),
        in_specs=[
            pl.BlockSpec((None, rows, deep), lambda m, k: (m, 0, k)),
            pl.BlockSpec((None, 2, deep, inner), lambda m, k: (m, 0, k, 0)),
            pl.BlockSpec((None, 2, deep, state), lambda m, k: (m, 0, k, 0)),
            pl.BlockSpec((None, heads, deep), lambda m, k: (m, 0, k)),
            whole(bias), whole(rate), whole(skip), whole(seg),
        ],
        out_specs=[pl.BlockSpec((None,) + shape, lambda m, k: (m, 0, 0)) for shape, _ in shapes],
        out_shape=[jax.ShapeDtypeStruct((models,) + shape, kind) for shape, kind in shapes],
        scratch_shapes=[
            pltpu.VMEM((rows, inner), F32), pltpu.VMEM((rows, 2 * state), F32), pltpu.VMEM((rows, heads), F32)
        ],
        cost_estimate=pl.CostEstimate(flops=10**10, bytes_accessed=16 * 10**6, transcendentals=2 * 10**6),
        name="mix_local",
    )(hidden, w_inner, w_state, w_step, bias, rate, skip, seg)


def gate_kernel(
    m, pages_ref, flags_ref, y_ref, gate_ref, c_ref, e_ref, r1_ref, r2_ref, r3_ref, r4_ref,
    p0_ref, p1_ref, p2_ref, p3_ref, gain_ref, out_ref, pick_ref,
):
    rows, inner = y_ref.shape
    heads = p0_ref.shape[0]
    wide = inner // heads
    state = c_ref.shape[1]
    e_col = e_ref[...]
    seg_col = e_col[:, heads : heads + 1]
    seg_first = e_col[0:1, heads : heads + 1]
    init = [
        p.reshape(inner, state)[...].astype(F32) * flags_ref[j].astype(F32)
        for j, p in enumerate((p0_ref, p1_ref, p2_ref, p3_ref))
    ]
    through = jnp.ones((heads, state), F32)
    parts = [jnp.zeros((wide, state), F32) for _ in range(heads)]
    for r in (r1_ref, r2_ref, r3_ref, r4_ref):
        meta = r[inner : inner + 16, :].astype(F32)
        hit = meta[8:9, :] == seg_first + 1.0
        piece = r[0:inner, :].astype(F32)
        weight = jnp.where(hit, through, 0.0)
        for h in range(heads):
            parts[h] = parts[h] + weight[h : h + 1, :] * piece[h * wide : (h + 1) * wide, :]
        through = jnp.where(hit, through * (meta[0:heads] + meta[heads : 2 * heads]), through)
    prior = jnp.concatenate(parts, axis=0)
    through = jnp.concatenate([jnp.broadcast_to(through[h : h + 1, :], (wide, state)) for h in range(heads)], axis=0)
    out_map = c_ref[...]
    low_id, high_id = jnp.min(seg_col), jnp.max(seg_col)
    pick_ref[...] = jnp.zeros_like(pick_ref)
    for j in range(4):

        @pl.when((low_id <= j) & (high_id >= j))
        def _():
            start = jnp.where(seg_first == float(j), prior + through * init[j], init[j])
            high = start.astype(BF16)
            low = (start - high.astype(F32)).astype(BF16)
            from_state = contract(out_map, high, ((1,), (1,))) + contract(out_map, low, ((1,), (1,)))
            pick_ref[...] = jnp.where(seg_col == float(j), from_state, pick_ref[...])

    picked = pick_ref[...]
    spread = jnp.concatenate([jnp.broadcast_to(e_col[:, h : h + 1], (rows, wide)) for h in range(heads)], axis=1)
    gated = (y_ref[...] + picked * spread) * silu(gate_ref[...])
    square = jnp.sum(gated * gated, axis=1, keepdims=True)
    out_ref[0:rows, :] = (gated * gain_ref[m : m + 1, :]).astype(BF16)
    lines = jnp.transpose(jnp.broadcast_to(square, (rows, 8)))[0:1, :]
    halves = jnp.concatenate([lines[:, 0:inner], lines[:, inner:]], axis=0)
    extra = jnp.concatenate(pieces(halves) + [jnp.zeros((10, inner), F32)], axis=0)
    out_ref[rows : rows + 16, :] = extra.astype(BF16)


def gate_out(m, pages, flags, y, gate, c, e, recv, pool, gain, after=()):
    rows, inner = y.shape[1:]
    heads = pool.shape[2]
    state = c.shape[2]
    whole = lambda a: pl.BlockSpec(a.shape, lambda g, pg, fl: (0,) * a.ndim)
    mine = lambda a: pl.BlockSpec((None,) + a.shape[1:], lambda g, pg, fl: (m, 0, 0))
    page = lambda j: pl.BlockSpec(
        (None, None, heads, pool.shape[3], state), lambda g, pg, fl: (m, pg[j], 0, 0, 0)
    )
    return pl.pallas_call(
        drop(functools.partial(gate_kernel, m), 15, len(after)),
        grid_spec=pltpu.PrefetchScalarGridSpec(
            num_scalar_prefetch=2,
            grid=(1,),
            in_specs=[mine(y), mine(gate), mine(c), mine(e)]
            + [mine(r) for r in recv]
            + [page(j) for j in range(4)]
            + [whole(gain)]
            + [ANYWHERE] * len(after),
            out_specs=pl.BlockSpec((rows + 16, inner), lambda g, pg, fl: (0, 0)),
            scratch_shapes=[pltpu.VMEM((rows, inner), F32)],
        ),
        out_shape=jax.ShapeDtypeStruct((rows + 16, inner), BF16),
        cost_estimate=pl.CostEstimate(flops=10**9, bytes_accessed=4 * 10**6, transcendentals=10**5),
        name="gate_out",
    )(pages, flags, y, gate, c, e, *recv, pool, pool, pool, pool, gain, *after)


def out_kernel(at_ref, g0_ref, g1_ref, g2_ref, g3_ref, w_ref, o0_ref, o1_ref, o2_ref, o3_ref, acc_ref, sq_ref):
    rows, width = acc_ref.shape
    inner = g0_ref.shape[1]
    block = rows // 4
    along, across = at_ref[0], at_ref[1]
    gathered = (g0_ref, g1_ref, g2_ref, g3_ref)
    extra = sum(g[rows : rows + 16, :].astype(F32) for g in gathered)
    square = extra[0:2] + extra[2:4] + extra[4:6]
    for n in range(4):
        sq_ref[n : n + 1, :] = square[n // 2 : n // 2 + 1, (n % 2) * block : (n % 2 + 1) * block]
    acc_ref[...] = sum(
        contract(g[0:rows, :], w_ref[lax.rem(along + 4 - k, 4)], ((1,), (0,))) for k, g in enumerate(gathered)
    )
    for k, out in enumerate((o0_ref, o1_ref, o2_ref, o3_ref)):
        at = lax.rem(across + k, 4)
        out[0:block, :] = acc_ref[pl.ds(pl.multiple_of(at * block, block), block), :].astype(BF16)
        line = jnp.concatenate(pieces(sq_ref[pl.ds(at, 1), :]) + [jnp.zeros((1, width - 3 * block), F32)], axis=1)
        out[block : block + 16, :] = jnp.broadcast_to(line, (16, width)).astype(BF16)


def out_blocks(at, gathered, w, after=()):
    rows = gathered[0].shape[0] - 16
    width = w.shape[2]
    block = rows // 4
    vm = pl.BlockSpec(memory_space=pltpu.VMEM)
    return pl.pallas_call(
        drop(out_kernel, 6, len(after)),
        in_specs=[pl.BlockSpec(memory_space=pltpu.SMEM)] + [vm] * 5 + [ANYWHERE] * len(after),
        out_specs=[vm] * 4,
        out_shape=[jax.ShapeDtypeStruct((block + 16, width), BF16)] * 4,
        scratch_shapes=[pltpu.VMEM((rows, width), F32), pltpu.VMEM((4, block), F32)],
        cost_estimate=pl.CostEstimate(flops=10**9, bytes_accessed=3 * 10**6, transcendentals=0),
        name="out_blocks",
    )(at, *gathered, w, *after)


def residual_kernel(m, units, at_ref, o0_ref, o1_ref, o2_ref, o3_ref, hid_ref, gain_ref, out_ref):
    block, width = hid_ref.shape
    total = sum(o[...].astype(F32) for o in (o0_ref, o1_ref, o2_ref, o3_ref))
    line = total[block : block + 1, :]
    square = line[:, 0:block] + line[:, block : 2 * block] + line[:, 2 * block : 3 * block]
    scale = to_column(lax.rsqrt(square / units + NORM_EPS))
    res = hid_ref[...].astype(F32) + total[0:block, :] * scale
    out_ref[0:block, :] = (res * gain_ref[m : m + 1, :]).astype(BF16)
    line = jnp.concatenate(
        pieces(to_row(jnp.sum(res * res, axis=1, keepdims=True))) + [jnp.zeros((1, width - 3 * block), F32)], axis=1
    )
    out_ref[block : block + 16, :] = jnp.broadcast_to(line, (16, width)).astype(BF16)


def residual_block(m, at, parts, hidden, gain, units, after=()):
    block, width = parts[0].shape[0] - 16, parts[0].shape[1]
    whole = pl.BlockSpec((block + 16, width), lambda g, at: (0, 0))
    return pl.pallas_call(
        drop(functools.partial(residual_kernel, m, float(units)), 7, len(after)),
        grid_spec=pltpu.PrefetchScalarGridSpec(
            num_scalar_prefetch=1,
            grid=(1,),
            in_specs=[whole] * 4
            + [
                pl.BlockSpec((None, block, width), lambda g, at: (m, at[1], at[0])),
                pl.BlockSpec((2, width), lambda g, at: (0, at[0])),
            ]
            + [ANYWHERE] * len(after),
            out_specs=whole,
        ),
        out_shape=jax.ShapeDtypeStruct((block + 16, width), BF16),
        cost_estimate=pl.CostEstimate(flops=10**6, bytes_accessed=10**6, transcendentals=100),
        name="residual_block",
    )(at, *parts, hidden, gain, *after)


def join_kernel(at_ref, u0_ref, u1_ref, u2_ref, u3_ref, out_ref):
    block, width = u0_ref.shape[0] - 16, u0_ref.shape[1]
    square = jnp.zeros((1, block), F32)
    for k, u in enumerate((u0_ref, u1_ref, u2_ref, u3_ref)):
        at = pl.multiple_of(lax.rem(at_ref[0] + 4 - k, 4) * width, width)
        out_ref[0:block, pl.ds(at, width)] = u[0:block, :]
        line = u[block : block + 16, :].astype(F32)[0:1, :]
        square = square + line[:, 0:block] + line[:, block : 2 * block] + line[:, 2 * block : 3 * block]
    scale = lax.rsqrt(square / out_ref.shape[1] + NORM_EPS)
    out_ref[block : block + 16, :] = jnp.zeros((16, out_ref.shape[1]), BF16)
    line = jnp.concatenate(pieces(scale), axis=1)
    out_ref[block : block + 16, 0 : 3 * block] = jnp.broadcast_to(line, (16, 3 * block)).astype(BF16)


def join_columns(at, parts, after=()):
    tall, width = parts[0].shape
    vm = pl.BlockSpec(memory_space=pltpu.VMEM)
    return pl.pallas_call(
        drop(join_kernel, 5, len(after)),
        in_specs=[pl.BlockSpec(memory_space=pltpu.SMEM)] + [vm] * 4 + [ANYWHERE] * len(after),
        out_specs=vm,
        out_shape=jax.ShapeDtypeStruct((tall, 4 * width), BF16),
        cost_estimate=pl.CostEstimate(flops=10**5, bytes_accessed=10**6, transcendentals=100),
        name="join_columns",
    )(at, *parts, *after)


def fetch_kernel(w_ref, out_ref, sems):
    depth = w_ref.shape[1]
    half = depth // 2
    copies = [
        pltpu.make_async_copy(
            w_ref.at[m, pl.ds(n * half, half), :], out_ref.at[m, pl.ds(n * half, half), :], sems.at[2 * m + n]
        )
        for m in range(2)
        for n in range(2)
    ]
    for copy in copies:
        copy.start()
    for copy in copies:
        copy.wait()


def fetched(head, after):
    return pl.pallas_call(
        drop(fetch_kernel, 1, len(after)),
        in_specs=[ANYWHERE] + [ANYWHERE] * len(after),
        out_specs=pl.BlockSpec(memory_space=pltpu.VMEM),
        out_shape=pltpu.VMEM(head.shape, head.dtype),
        scratch_shapes=[pltpu.SemaphoreType.DMA((4,))],
        compiler_params=pltpu.CompilerParams(vmem_limit_bytes=16 * 2**20),
        cost_estimate=pl.CostEstimate(flops=0, bytes_accessed=3 * 10**7, transcendentals=0),
        name="fetched",
    )(head, *after)


def head_kernel(place_ref, at0_ref, at1_ref, *refs):
    w_ref, tgt_ref, out_ref, acc_ref = refs[8:]
    block = refs[0].shape[0] - 16
    vocab = w_ref.shape[2]
    for m, at_ref in enumerate((at0_ref, at1_ref)):
        tiles = refs[4 * m : 4 * m + 4]
        for n in range(2):
            rows = jnp.concatenate([x[0:block, :] for x in tiles[2 * n : 2 * n + 2]], axis=0)
            acc_ref[2 * n * block : 2 * (n + 1) * block, :] = contract(rows, w_ref[m], ((1,), (0,)))
        for k, x in enumerate(tiles):
            at = lax.rem(at_ref[1] + 4 - k, 4)
            line = x[block : block + 16, 0 : 3 * block].astype(F32)[0:1, :]
            scale = to_column(line[:, 0:block] + line[:, block : 2 * block] + line[:, 2 * block : 3 * block])
            raw = acc_ref[k * block : (k + 1) * block, :]
            top = jnp.max(raw, axis=1, keepdims=True)
            total = jnp.sum(jnp.exp2((raw - top) * (scale * LOG2E)), axis=1, keepdims=True)
            lse = top * scale + jnp.log(total)
            target = to_column((tgt_ref[pl.ds(at, 1), :] - place_ref[0] * vocab).astype(F32)).astype(jnp.int32)
            column = lax.broadcasted_iota(jnp.int32, raw.shape, 1)
            chosen = jnp.sum(jnp.where(column == target, raw, 0.0), axis=1, keepdims=True) * scale
            for which, value in enumerate((lse, chosen)):
                out_ref[:, pl.ds(m * 8 + which * 4 + at, 1), :] = jnp.broadcast_to(
                    to_row(value)[None], (out_ref.shape[0], 1, block)
                )


def head_stats(place, at, parts, head, tgt, group):
    tall, depth = parts[0][0].shape
    block = tall - 16
    vocab = head.shape[2]
    vm = pl.BlockSpec(memory_space=pltpu.VMEM)
    sm = pl.BlockSpec(memory_space=pltpu.SMEM)
    return pl.pallas_call(
        head_kernel,
        in_specs=[sm] * 3 + [vm] * 10,
        out_specs=vm,
        scratch_shapes=[pltpu.VMEM((4 * block, vocab), F32)],
        out_shape=jax.ShapeDtypeStruct((group, 16, block), F32),
        compiler_params=pltpu.CompilerParams(vmem_limit_bytes=36 * 2**20),
        cost_estimate=pl.CostEstimate(
            flops=16 * block * depth * vocab, bytes_accessed=10**7, transcendentals=8 * block * vocab
        ),
        name="head_stats",
    )(place, *at, *parts[0], *parts[1], head, tgt)


def diff_kernel(stat_ref, live_ref, seg_ref, diff_ref, sums_ref):
    scores = []
    for m in range(2):
        part = stat_ref[:, 8 * m : 8 * m + 8, :]
        lse = part[:, 0:4, :]
        top = jnp.max(lse, axis=0)
        total = top + jnp.log(jnp.sum(jnp.exp(lse - top[None]), axis=0))
        scores.append(jnp.sum(part[:, 4:8, :], axis=0) - total)
    lines = lax.broadcasted_iota(jnp.int32, (4, 128), 0)
    alive = jnp.where(lines < 2, live_ref[0].astype(F32), live_ref[1].astype(F32))
    diff = alive * (scores[0] - scores[1])
    diff_ref[...] = diff
    which = lax.broadcasted_iota(jnp.int32, (8, 128), 0)
    sums = jnp.zeros((8, 128), F32)
    for j in range(4):
        mine = jnp.sum(jnp.where(seg_ref[...] == j, diff, 0.0), axis=1, keepdims=True)
        sums = jnp.where(which == j, jnp.sum(mine, axis=0, keepdims=True), sums)
    sums_ref[...] = sums


def token_diffs(stats, live, seg):
    vm = pl.BlockSpec(memory_space=pltpu.VMEM)
    return pl.pallas_call(
        diff_kernel,
        in_specs=[vm, pl.BlockSpec(memory_space=pltpu.SMEM), vm],
        out_shape=(jax.ShapeDtypeStruct((4, 128), F32), jax.ShapeDtypeStruct((8, 128), F32)),
        name="token_diffs",
    )(stats, live, seg)


def turn_kernel(w_ref, out_ref):
    width = out_ref.shape[2]
    for j in range(4):
        out_ref[j] = w_ref[:, j * width : (j + 1) * width]


def turned(m, w_out):
    _, inner, depth = w_out.shape
    width = depth // 4
    return pl.pallas_call(
        turn_kernel,
        grid=(1,),
        in_specs=[pl.BlockSpec((None, inner, depth), lambda j: (m, 0, 0))],
        out_specs=pl.BlockSpec((4, inner, width), lambda j: (0, 0, 0)),
        out_shape=jax.ShapeDtypeStruct((4, inner, width), w_out.dtype),
        cost_estimate=pl.CostEstimate(flops=0, bytes_accessed=2 * 10**6, transcendentals=0),
        name="turned",
    )(w_out)


def ring(value, axis, by):
    return lax.ppermute(value, axis, [(i, (i + by) % 4) for i in range(4)])


def gathered(value, axis):
    return [value] + [ring(value, axis, k) for k in (1, 2, 3)]


def per_device(
    hidden, w_inner, w_state, w_step, step_bias, rate, skip_gain, norm_gain, w_out, final_gain, head, pool,
    targets, segment_ids, flags, pages, live, owners,
):
    rows = targets.shape[0]
    depth = hidden.shape[2]
    inner = w_inner.shape[3]
    group = lax.axis_size(VOC)
    devices = lax.axis_size(SEQ)
    place = lax.axis_index(VOC).astype(jnp.int32).reshape(1)
    seg = segment_ids.reshape(1, rows)
    tgt = targets.reshape(4, rows // 4)
    w_inner = jnp.swapaxes(w_inner, 1, 2)
    w_state = jnp.swapaxes(w_state, 1, 2)
    w_step = jnp.swapaxes(w_step, 1, 2)
    ways = (("x", "z"), ("z", "x"))
    both = range(2)
    at = [
        jnp.stack([lax.axis_index(along), lax.axis_index(across)]).astype(jnp.int32) for along, across in ways
    ]
    weights = [lax.all_to_all(turned(m, w_out), ways[m][0], 0, 0) for m in both]
    y, gate, c, e, pay = mix_local(hidden, w_inner, w_state, w_step, step_bias, rate, skip_gain, seg)
    recv = [lax.ppermute(pay, SEQ, [(i, i + k) for i in range(devices - k)]) for k in range(1, REACH + 1)]
    gated, parts, res, full = [], [], [], []
    for m in both:
        gated.append(gate_out(m, pages, flags, y, gate, c, e, recv, pool, norm_gain, tuple(gated)))
    for m in both:
        out = out_blocks(at[m], gathered(gated[m], ways[m][0]), weights[m], (gated[1],))
        parts.append([out[0]] + [ring(out[k], ways[m][1], k) for k in (1, 2, 3)])
    for m in both:
        res.append(residual_block(m, at[m], parts[m], hidden, final_gain, inner * group, (parts[1][0],)))
    blocks = [gathered(res[m], ways[m][0]) for m in both]
    for m in both:
        full.append(join_columns(at[m], blocks[m], tuple(blocks[1 - m][1:])))
    ready = fetched(head, tuple(full))
    last = [gathered(full[m], ways[m][1]) for m in both]
    merged = lax.all_to_all(head_stats(place, at, last, ready, tgt, group), VOC, 0, 0)
    diff, sums = token_diffs(merged, live, segment_ids.reshape(4, 128))
    sums = sums + lax.ppermute(sums, "core", [(0, 1), (1, 0)])
    sums = sum(gathered(sums, "y"))[0:4, 0]
    owned = jnp.where(owners == lax.axis_index(SEQ), sums, 0.0)
    return diff.reshape(rows), owned[None]


def solution(mesh):
    seq, vocab = mesh.devices.shape
    fine = Mesh(mesh.devices.reshape(seq // 2, 2, 4, vocab // 4), ("y", "core", "x", "z"))
    placed = (
        P(None, SEQ, None),
        P(None, None, None, VOC),
        P(),
        P(None, None, VOC),
        P(None, VOC),
        P(None, VOC),
        P(None, VOC),
        P(None, VOC),
        P(None, VOC, None),
        P(),
        P(None, None, VOC),
        P(None, None, VOC, None, None),
        P(SEQ),
        P(SEQ),
        P(),
        P(),
        P(SEQ),
        P(),
    )
    return jax.shard_map(
        per_device, mesh=fine, in_specs=placed, out_specs=(P(SEQ), P(SEQ, None)), check_vma=False
    )
```

```python
import functools

import jax
import jax.numpy as jnp
from jax import lax
from jax.experimental import pallas as pl
from jax.experimental.pallas import tpu as pltpu
from jax.sharding import Mesh
from jax.sharding import PartitionSpec as P

NORM_EPS = 1e-05
SPAN = 256
REACH = 4
SEQ = ("y", "core")
VOC = ("x", "z")
F32 = jnp.float32
BF16 = jnp.bfloat16
LOW = -1e30
LOG2E = 1.4426950408889634


def silu(v):
    return v / (1.0 + jnp.exp(-v))


def contract(a, b, dims):
    return lax.dot_general(a, b, (dims, ((), ())), preferred_element_type=F32)


def drop(kernel, inputs, count):
    def body(*refs):
        return kernel(*refs[:inputs], *refs[inputs + count :])

    return body


ANYWHERE = pl.BlockSpec(memory_space=pl.ANY)


def pieces(value):
    high = value.astype(BF16).astype(F32)
    mid = (value - high).astype(BF16).astype(F32)
    return [high, mid, value - high - mid]


def to_column(row):
    return jnp.transpose(jnp.broadcast_to(row, (8, row.shape[1])))[:, 0:1]


def to_row(column):
    return jnp.transpose(jnp.broadcast_to(column, (column.shape[0], 8)))[0:1, :]


def as_column(row):
    count = row.shape[1]
    spread = jnp.broadcast_to(row, (count, count))
    eye = lax.broadcasted_iota(jnp.int32, spread.shape, 0) == lax.broadcasted_iota(jnp.int32, spread.shape, 1)
    return jnp.sum(jnp.where(eye, spread, 0.0), axis=1, keepdims=True)


def mix_kernel(
    tok_ref, wi_ref, ws_ref, wp_ref, bias_ref, rate_ref, skip_ref, seg_ref,
    y_ref, gate_ref, c_ref, e_ref, pay_ref, val_ref, st_ref, stp_ref,
):
    m = pl.program_id(0)
    k = pl.program_id(1)
    inner = y_ref.shape[1]

    @pl.when(k == 0)
    def _():
        gate_ref[...] = jnp.zeros_like(gate_ref)
        val_ref[...] = jnp.zeros_like(val_ref)
        st_ref[...] = jnp.zeros_like(st_ref)
        stp_ref[...] = jnp.zeros_like(stp_ref)

    tokens = tok_ref[...]
    state = c_ref.shape[1]
    gate_ref[...] += contract(tokens, wi_ref[0], ((1,), (0,)))
    val_ref[...] += contract(tokens, wi_ref[1], ((1,), (0,)))
    st_ref[:, 0:state] += contract(tokens, ws_ref[0], ((1,), (0,)))
    st_ref[:, state:] += contract(tokens, ws_ref[1], ((1,), (0,)))
    stp_ref[...] += contract(tokens, wp_ref[...], ((1,), (1,)))

    @pl.when(k == pl.num_programs(1) - 1)
    def _():
        scan_rows(
            m, bias_ref, rate_ref, skip_ref, seg_ref, y_ref, c_ref, e_ref, pay_ref, val_ref, st_ref, stp_ref
        )


def scan_rows(m, bias_ref, rate_ref, skip_ref, seg_ref, y_ref, c_ref, e_ref, pay_ref, val_ref, st_ref, stp_ref):
    rows, inner = y_ref.shape
    heads = bias_ref.shape[1]
    wide = inner // heads
    state = c_ref.shape[1]
    seg = seg_ref[...]
    raw = jnp.transpose(stp_ref[...])[0:heads, :] + as_column(bias_ref[pl.ds(m, 1), :])
    dt = jnp.maximum(raw, 0.0) + jnp.log1p(jnp.exp(-jnp.abs(raw)))
    la = -dt * as_column(rate_ref[pl.ds(m, 1), :])
    skip = as_column(skip_ref[pl.ds(m, 1), :])
    lane = lax.broadcasted_iota(jnp.int32, la.shape, 1)
    run = la
    step = 1
    while step < rows:
        run = run + jnp.where(lane >= step, pltpu.roll(run, step, 1), 0.0)
        step *= 2
    last = jnp.max(seg, axis=1, keepdims=True)
    base = jnp.zeros_like(la)
    for j in range(4):
        base_j = jnp.sum(jnp.where(seg < j, la, 0.0), axis=1, keepdims=True)
        base = jnp.where(seg == j, base_j, base)
    total = jnp.sum(la, axis=1, keepdims=True)
    grow = jnp.exp(run - base)
    keep = jnp.where(seg == last, jnp.exp(jnp.minimum(total - run, 0.0)) * dt, 0.0)
    tail = jnp.exp(jnp.sum(jnp.where(seg == last, la, 0.0), axis=1, keepdims=True))
    cols = jnp.transpose(jnp.concatenate([run, keep], axis=0))
    segf = jnp.broadcast_to(seg.astype(F32), (heads, rows))
    ecol = jnp.transpose(jnp.concatenate([grow, segf], axis=0))
    e_ref[...] = ecol
    values = silu(val_ref[...]).astype(BF16)
    in_map = silu(st_ref[:, 0:state]).astype(BF16)
    out_map = silu(st_ref[:, state:]).astype(BF16)
    c_ref[...] = out_map
    vf = values.astype(F32)
    kept = jnp.concatenate(
        [vf[:, h * wide : (h + 1) * wide] * cols[:, heads + h : heads + h + 1] for h in range(heads)], axis=1
    ).astype(BF16)
    added = contract(kept, in_map, ((0,), (0,)))
    pay_ref[0:inner, :] = added.astype(BF16)
    high = tail.astype(BF16).astype(F32)
    low = tail - high
    meta = jnp.concatenate(
        [
            jnp.broadcast_to(high, (heads, state)),
            jnp.broadcast_to(low, (heads, state)),
            jnp.broadcast_to(last.astype(F32) + 1.0, (8, state)),
        ],
        axis=0,
    )
    pay_ref[inner : inner + 16, :] = meta.astype(BF16)
    blocks = rows // SPAN
    for i in range(blocks):
        t0 = i * SPAN
        acc = [vf[t0 : t0 + SPAN, h * wide : (h + 1) * wide] * skip[h : h + 1, :] for h in range(heads)]
        for j in range(i + 1):
            s0 = j * SPAN
            scores = contract(out_map[t0 : t0 + SPAN], in_map[s0 : s0 + SPAN], ((1,), (1,)))
            same = ecol[t0 : t0 + SPAN, heads : heads + 1] == segf[0:1, s0 : s0 + SPAN]
            if i == j:
                same = same & (
                    lax.broadcasted_iota(jnp.int32, (SPAN, SPAN), 0)
                    >= lax.broadcasted_iota(jnp.int32, (SPAN, SPAN), 1)
                )
            for h in range(heads):
                gap = cols[t0 : t0 + SPAN, h : h + 1] - run[h : h + 1, s0 : s0 + SPAN]
                weight = jnp.exp(jnp.where(same, gap, LOW)) * (scores * dt[h : h + 1, s0 : s0 + SPAN])
                acc[h] = acc[h] + contract(
                    weight.astype(BF16), values[s0 : s0 + SPAN, h * wide : (h + 1) * wide], ((1,), (0,))
                )
        y_ref[t0 : t0 + SPAN, :] = jnp.concatenate(acc, axis=1)


def mix_local(hidden, w_inner, w_state, w_step, bias, rate, skip, seg, chunks=4):
    models, rows, depth = hidden.shape
    inner = w_inner.shape[3]
    state = w_state.shape[3]
    heads = bias.shape[1]
    deep = depth // chunks
    whole = lambda a: pl.BlockSpec(a.shape, lambda m, k: (0,) * a.ndim)
    shapes = ((rows, inner), F32), ((rows, inner), F32), ((rows, state), BF16), ((rows, 2 * heads), F32), (
        (inner + 16, state), BF16)
    return pl.pallas_call(
        mix_kernel,
        grid=(models, chunks),
        in_specs=[
            pl.BlockSpec((None, rows, deep), lambda m, k: (m, 0, k)),
            pl.BlockSpec((None, 2, deep, inner), lambda m, k: (m, 0, k, 0)),
            pl.BlockSpec((None, 2, deep, state), lambda m, k: (m, 0, k, 0)),
            pl.BlockSpec((None, heads, deep), lambda m, k: (m, 0, k)),
            whole(bias), whole(rate), whole(skip), whole(seg),
        ],
        out_specs=[pl.BlockSpec((None,) + shape, lambda m, k: (m, 0, 0)) for shape, _ in shapes],
        out_shape=[jax.ShapeDtypeStruct((models,) + shape, kind) for shape, kind in shapes],
        scratch_shapes=[
            pltpu.VMEM((rows, inner), F32), pltpu.VMEM((rows, 2 * state), F32), pltpu.VMEM((rows, heads), F32)
        ],
        cost_estimate=pl.CostEstimate(flops=10**10, bytes_accessed=16 * 10**6, transcendentals=2 * 10**6),
        name="mix_local",
    )(hidden, w_inner, w_state, w_step, bias, rate, skip, seg)


def gate_kernel(
    m, pages_ref, flags_ref, y_ref, gate_ref, c_ref, e_ref, r1_ref, r2_ref, r3_ref, r4_ref,
    p0_ref, p1_ref, p2_ref, p3_ref, gain_ref, out_ref, pick_ref,
):
    rows, inner = y_ref.shape
    heads = p0_ref.shape[0]
    wide = inner // heads
    state = c_ref.shape[1]
    e_col = e_ref[...]
    seg_col = e_col[:, heads : heads + 1]
    seg_first = e_col[0:1, heads : heads + 1]
    init = [
        p.reshape(inner, state)[...].astype(F32) * flags_ref[j].astype(F32)
        for j, p in enumerate((p0_ref, p1_ref, p2_ref, p3_ref))
    ]
    through = jnp.ones((heads, state), F32)
    parts = [jnp.zeros((wide, state), F32) for _ in range(heads)]
    for r in (r1_ref, r2_ref, r3_ref, r4_ref):
        meta = r[inner : inner + 16, :].astype(F32)
        hit = meta[8:9, :] == seg_first + 1.0
        piece = r[0:inner, :].astype(F32)
        weight = jnp.where(hit, through, 0.0)
        for h in range(heads):
            parts[h] = parts[h] + weight[h : h + 1, :] * piece[h * wide : (h + 1) * wide, :]
        through = jnp.where(hit, through * (meta[0:heads] + meta[heads : 2 * heads]), through)
    prior = jnp.concatenate(parts, axis=0)
    through = jnp.concatenate([jnp.broadcast_to(through[h : h + 1, :], (wide, state)) for h in range(heads)], axis=0)
    out_map = c_ref[...]
    low_id, high_id = jnp.min(seg_col), jnp.max(seg_col)
    pick_ref[...] = jnp.zeros_like(pick_ref)
    for j in range(4):

        @pl.when((low_id <= j) & (high_id >= j))
        def _():
            start = jnp.where(seg_first == float(j), prior + through * init[j], init[j])
            high = start.astype(BF16)
            low = (start - high.astype(F32)).astype(BF16)
            from_state = contract(out_map, high, ((1,), (1,))) + contract(out_map, low, ((1,), (1,)))
            pick_ref[...] = jnp.where(seg_col == float(j), from_state, pick_ref[...])

    picked = pick_ref[...]
    spread = jnp.concatenate([jnp.broadcast_to(e_col[:, h : h + 1], (rows, wide)) for h in range(heads)], axis=1)
    gated = (y_ref[...] + picked * spread) * silu(gate_ref[...])
    square = jnp.sum(gated * gated, axis=1, keepdims=True)
    out_ref[0:rows, :] = (gated * gain_ref[m : m + 1, :]).astype(BF16)
    lines = jnp.transpose(jnp.broadcast_to(square, (rows, 8)))[0:1, :]
    halves = jnp.concatenate([lines[:, 0:inner], lines[:, inner:]], axis=0)
    extra = jnp.concatenate(pieces(halves) + [jnp.zeros((10, inner), F32)], axis=0)
    out_ref[rows : rows + 16, :] = extra.astype(BF16)


def gate_out(m, pages, flags, y, gate, c, e, recv, pool, gain, after=()):
    rows, inner = y.shape[1:]
    heads = pool.shape[2]
    state = c.shape[2]
    whole = lambda a: pl.BlockSpec(a.shape, lambda g, pg, fl: (0,) * a.ndim)
    mine = lambda a: pl.BlockSpec((None,) + a.shape[1:], lambda g, pg, fl: (m, 0, 0))
    page = lambda j: pl.BlockSpec(
        (None, None, heads, pool.shape[3], state), lambda g, pg, fl: (m, pg[j], 0, 0, 0)
    )
    return pl.pallas_call(
        drop(functools.partial(gate_kernel, m), 15, len(after)),
        grid_spec=pltpu.PrefetchScalarGridSpec(
            num_scalar_prefetch=2,
            grid=(1,),
            in_specs=[mine(y), mine(gate), mine(c), mine(e)]
            + [mine(r) for r in recv]
            + [page(j) for j in range(4)]
            + [whole(gain)]
            + [ANYWHERE] * len(after),
            out_specs=pl.BlockSpec((rows + 16, inner), lambda g, pg, fl: (0, 0)),
            scratch_shapes=[pltpu.VMEM((rows, inner), F32)],
        ),
        out_shape=jax.ShapeDtypeStruct((rows + 16, inner), BF16),
        cost_estimate=pl.CostEstimate(flops=10**9, bytes_accessed=12 * 10**6, transcendentals=10**5),
        name="gate_out",
    )(pages, flags, y, gate, c, e, *recv, pool, pool, pool, pool, gain, *after)


def out_kernel(at_ref, g0_ref, g1_ref, g2_ref, g3_ref, w_ref, o0_ref, o1_ref, o2_ref, o3_ref, acc_ref, sq_ref):
    rows, width = acc_ref.shape
    inner = g0_ref.shape[1]
    block = rows // 4
    along, across = at_ref[0], at_ref[1]
    gathered = (g0_ref, g1_ref, g2_ref, g3_ref)
    extra = sum(g[rows : rows + 16, :].astype(F32) for g in gathered)
    square = extra[0:2] + extra[2:4] + extra[4:6]
    for n in range(4):
        sq_ref[n : n + 1, :] = square[n // 2 : n // 2 + 1, (n % 2) * block : (n % 2 + 1) * block]
    acc_ref[...] = sum(
        contract(g[0:rows, :], w_ref[lax.rem(along + 4 - k, 4)], ((1,), (0,))) for k, g in enumerate(gathered)
    )
    for k, out in enumerate((o0_ref, o1_ref, o2_ref, o3_ref)):
        at = lax.rem(across + k, 4)
        out[0:block, :] = acc_ref[pl.ds(pl.multiple_of(at * block, block), block), :].astype(BF16)
        line = jnp.concatenate(pieces(sq_ref[pl.ds(at, 1), :]) + [jnp.zeros((1, width - 3 * block), F32)], axis=1)
        out[block : block + 16, :] = jnp.broadcast_to(line, (16, width)).astype(BF16)


def out_blocks(at, gathered, w, after=()):
    rows = gathered[0].shape[0] - 16
    width = w.shape[2]
    block = rows // 4
    vm = pl.BlockSpec(memory_space=pltpu.VMEM)
    return pl.pallas_call(
        drop(out_kernel, 6, len(after)),
        in_specs=[pl.BlockSpec(memory_space=pltpu.SMEM)] + [vm] * 5 + [ANYWHERE] * len(after),
        out_specs=[vm] * 4,
        out_shape=[jax.ShapeDtypeStruct((block + 16, width), BF16)] * 4,
        scratch_shapes=[pltpu.VMEM((rows, width), F32), pltpu.VMEM((4, block), F32)],
        cost_estimate=pl.CostEstimate(flops=10**9, bytes_accessed=10**7, transcendentals=0),
        name="out_blocks",
    )(at, *gathered, w, *after)


def residual_kernel(m, units, at_ref, o0_ref, o1_ref, o2_ref, o3_ref, hid_ref, gain_ref, out_ref):
    block, width = hid_ref.shape
    total = sum(o[...].astype(F32) for o in (o0_ref, o1_ref, o2_ref, o3_ref))
    line = total[block : block + 1, :]
    square = line[:, 0:block] + line[:, block : 2 * block] + line[:, 2 * block : 3 * block]
    scale = to_column(lax.rsqrt(square / units + NORM_EPS))
    res = hid_ref[...].astype(F32) + total[0:block, :] * scale
    out_ref[0:block, :] = (res * gain_ref[m : m + 1, :]).astype(BF16)
    line = jnp.concatenate(
        pieces(to_row(jnp.sum(res * res, axis=1, keepdims=True))) + [jnp.zeros((1, width - 3 * block), F32)], axis=1
    )
    out_ref[block : block + 16, :] = jnp.broadcast_to(line, (16, width)).astype(BF16)


def residual_block(m, at, parts, hidden, gain, units, after=()):
    block, width = parts[0].shape[0] - 16, parts[0].shape[1]
    whole = pl.BlockSpec((block + 16, width), lambda g, at: (0, 0))
    return pl.pallas_call(
        drop(functools.partial(residual_kernel, m, float(units)), 7, len(after)),
        grid_spec=pltpu.PrefetchScalarGridSpec(
            num_scalar_prefetch=1,
            grid=(1,),
            in_specs=[whole] * 4
            + [
                pl.BlockSpec((None, block, width), lambda g, at: (m, at[1], at[0])),
                pl.BlockSpec((2, width), lambda g, at: (0, at[0])),
            ]
            + [ANYWHERE] * len(after),
            out_specs=whole,
        ),
        out_shape=jax.ShapeDtypeStruct((block + 16, width), BF16),
        cost_estimate=pl.CostEstimate(flops=10**6, bytes_accessed=9 * 10**6, transcendentals=100),
        name="residual_block",
    )(at, *parts, hidden, gain, *after)


def join_kernel(at_ref, u0_ref, u1_ref, u2_ref, u3_ref, out_ref):
    block, width = u0_ref.shape[0] - 16, u0_ref.shape[1]
    square = jnp.zeros((1, block), F32)
    half = block // 2
    for k, u in enumerate((u0_ref, u1_ref, u2_ref, u3_ref)):
        at = pl.multiple_of(lax.rem(at_ref[0] + 4 - k, 4) * width, width)
        for n in range(2):
            out_ref[n * (half + 8) + 8 : (n + 1) * (half + 8), pl.ds(at, width)] = u[n * half : (n + 1) * half, :]
        line = u[block : block + 16, :].astype(F32)[0:1, :]
        square = square + line[:, 0:block] + line[:, block : 2 * block] + line[:, 2 * block : 3 * block]
    parts = pieces(lax.rsqrt(square / out_ref.shape[1] + NORM_EPS))
    for n in range(2):
        line = jnp.concatenate(
            [p[:, n * half : (n + 1) * half] for p in parts] + [jnp.zeros((1, 256 - 3 * half), F32)], axis=1
        )
        out_ref[n * (half + 8) : n * (half + 8) + 8, 0:256] = jnp.broadcast_to(line, (8, 256)).astype(BF16)
        out_ref[n * (half + 8) : n * (half + 8) + 8, 256:] = jnp.zeros((8, out_ref.shape[1] - 256), BF16)


def join_columns(at, parts, after=()):
    tall, width = parts[0].shape
    vm = pl.BlockSpec(memory_space=pltpu.VMEM)
    return pl.pallas_call(
        drop(join_kernel, 5, len(after)),
        in_specs=[pl.BlockSpec(memory_space=pltpu.SMEM)] + [vm] * 4 + [ANYWHERE] * len(after),
        out_specs=vm,
        out_shape=jax.ShapeDtypeStruct((tall, 4 * width), BF16),
        cost_estimate=pl.CostEstimate(flops=10**5, bytes_accessed=6 * 10**6, transcendentals=100),
        name="join_columns",
    )(at, *parts, *after)


def fetch_kernel(w_ref, out_ref, sems):
    depth = w_ref.shape[1]
    half = depth // 2
    copies = [
        pltpu.make_async_copy(
            w_ref.at[m, pl.ds(n * half, half), :], out_ref.at[m, pl.ds(n * half, half), :], sems.at[2 * m + n]
        )
        for m in range(2)
        for n in range(2)
    ]
    for copy in copies:
        copy.start()
    for copy in copies:
        copy.wait()


def fetched(head, after):
    return pl.pallas_call(
        drop(fetch_kernel, 1, len(after)),
        in_specs=[ANYWHERE] + [ANYWHERE] * len(after),
        out_specs=pl.BlockSpec(memory_space=pltpu.VMEM),
        out_shape=pltpu.VMEM(head.shape, head.dtype),
        scratch_shapes=[pltpu.SemaphoreType.DMA((4,))],
        compiler_params=pltpu.CompilerParams(vmem_limit_bytes=40 * 2**20),
        cost_estimate=pl.CostEstimate(flops=0, bytes_accessed=3 * 10**7, transcendentals=0),
        name="fetched",
    )(head, *after)


def score_rows(m, halves, places, base, w_ref, tgt_ref, acc_ref, put):
    half = halves[0].shape[0] - 8
    block = 2 * half
    rows = jnp.concatenate([x[8 : half + 8, :] for x in halves], axis=0)
    acc_ref[0 : rows.shape[0], :] = contract(rows, w_ref[m], ((1,), (0,)))
    for k, at in enumerate(places):
        lines = [x[0:8, 0:256].astype(F32)[0:1, :] for x in halves[2 * k : 2 * k + 2]]
        scale = to_column(
            jnp.concatenate(
                [v[:, 0:half] + v[:, half : 2 * half] + v[:, 2 * half : 3 * half] for v in lines], axis=1
            )
        )
        raw = acc_ref[k * block : (k + 1) * block, :]
        top = jnp.max(raw, axis=1, keepdims=True)
        total = jnp.sum(jnp.exp2((raw - top) * (scale * LOG2E)), axis=1, keepdims=True)
        target = to_column((tgt_ref[pl.ds(at, 1), :] - base).astype(F32)).astype(jnp.int32)
        column = lax.broadcasted_iota(jnp.int32, raw.shape, 1)
        chosen = jnp.sum(jnp.where(column == target, raw, 0.0), axis=1, keepdims=True) * scale
        put(m * 8 + at, to_row(top * scale + jnp.log(total)))
        put(m * 8 + 4 + at, to_row(chosen))


def near_kernel(place_ref, at0_ref, at1_ref, *refs):
    w_ref, tgt_ref, out_ref, acc_ref = refs[6:]
    half = refs[0].shape[0] // 2
    base = place_ref[0] * w_ref.shape[2]

    def put(row, value):
        out_ref[pl.ds(row, 1), :] = value

    for m, at_ref in enumerate((at0_ref, at1_ref)):
        tiles = refs[3 * m : 3 * m + 3]
        halves = [x.at[pl.ds(n * half, half), :] for x in tiles for n in range(2)]
        places = [lax.rem(at_ref[1] + 4 - k, 4) for k in (0, 1, 3)]
        score_rows(m, halves, places, base, w_ref, tgt_ref, acc_ref, put)


def far_kernel(place_ref, at0_ref, at1_ref, *refs):
    w_ref, tgt_ref, near_ref, out_ref, acc_ref = refs[4:]
    base = place_ref[0] * w_ref.shape[2]
    out_ref[...] = jnp.broadcast_to(near_ref[...][None], out_ref.shape)

    def put(row, value):
        out_ref[:, pl.ds(row, 1), :] = jnp.broadcast_to(value[None], (out_ref.shape[0], 1, value.shape[1]))

    for m, at_ref in enumerate((at0_ref, at1_ref)):
        places = [lax.rem(at_ref[1] + 2, 4)]
        score_rows(m, refs[2 * m : 2 * m + 2], places, base, w_ref, tgt_ref, acc_ref, put)


def head_stats(place, at, near, cut, head, tgt, group):
    tall, depth = near[0][0].shape
    block = tall - 16
    vocab = head.shape[2]
    vm = pl.BlockSpec(memory_space=pltpu.VMEM)
    sm = pl.BlockSpec(memory_space=pltpu.SMEM)
    common = dict(out_specs=vm, compiler_params=pltpu.CompilerParams(vmem_limit_bytes=24 * 2**20))
    cost = lambda blocks: pl.CostEstimate(
        flops=4 * blocks * block * depth * vocab, bytes_accessed=10**7, transcendentals=2 * blocks * block * vocab
    )
    first = pl.pallas_call(
        near_kernel,
        in_specs=[sm] * 3 + [vm] * 8,
        scratch_shapes=[pltpu.VMEM((3 * block, vocab), F32)],
        out_shape=jax.ShapeDtypeStruct((16, block), F32),
        cost_estimate=cost(3),
        name="head_near",
        **common,
    )(place, *at, *near[0], *near[1], head, tgt)
    return pl.pallas_call(
        far_kernel,
        in_specs=[sm] * 3 + [vm] * 7,
        scratch_shapes=[pltpu.VMEM((block, vocab), F32)],
        out_shape=jax.ShapeDtypeStruct((group, 16, block), F32),
        cost_estimate=cost(1),
        name="head_far",
        **common,
    )(place, *at, *cut[0], *cut[1], head, tgt, first)


def cut_kernel(a_ref, b_ref, c_ref, d_ref, oa_ref, ob_ref, oc_ref, od_ref):
    oa_ref[...] = a_ref[...]
    ob_ref[...] = b_ref[...]
    oc_ref[...] = c_ref[...]
    od_ref[...] = d_ref[...]


def cut_halves(pairs, after):
    tall, depth = pairs[0][0].shape
    low = pl.BlockSpec((tall // 2, depth), lambda g: (0, 0))
    high = pl.BlockSpec((tall // 2, depth), lambda g: (1, 0))
    return pl.pallas_call(
        drop(cut_kernel, 4, len(after)),
        grid=(1,),
        in_specs=[low, high] * 2 + [ANYWHERE] * len(after),
        out_specs=[low] * 4,
        out_shape=[jax.ShapeDtypeStruct((tall // 2, depth), BF16)] * 4,
        compiler_params=pltpu.CompilerParams(vmem_limit_bytes=8 * 2**20),
        cost_estimate=pl.CostEstimate(flops=0, bytes_accessed=2 * 10**6, transcendentals=0),
        name="cut_halves",
    )(*pairs[0], *pairs[1], *after)


def diff_kernel(stat_ref, live_ref, seg_ref, diff_ref, sums_ref):
    scores = []
    for m in range(2):
        part = stat_ref[:, 8 * m : 8 * m + 8, :]
        lse = part[:, 0:4, :]
        top = jnp.max(lse, axis=0)
        total = top + jnp.log(jnp.sum(jnp.exp(lse - top[None]), axis=0))
        scores.append(jnp.sum(part[:, 4:8, :], axis=0) - total)
    lines = lax.broadcasted_iota(jnp.int32, (4, 128), 0)
    alive = jnp.where(lines < 2, live_ref[0].astype(F32), live_ref[1].astype(F32))
    diff = alive * (scores[0] - scores[1])
    diff_ref[...] = diff
    which = lax.broadcasted_iota(jnp.int32, (8, 128), 0)
    sums = jnp.zeros((8, 128), F32)
    for j in range(4):
        mine = jnp.sum(jnp.where(seg_ref[...] == j, diff, 0.0), axis=1, keepdims=True)
        sums = jnp.where(which == j, jnp.sum(mine, axis=0, keepdims=True), sums)
    sums_ref[...] = sums


def token_diffs(stats, live, seg):
    vm = pl.BlockSpec(memory_space=pltpu.VMEM)
    return pl.pallas_call(
        diff_kernel,
        in_specs=[vm, pl.BlockSpec(memory_space=pltpu.SMEM), vm],
        out_shape=(jax.ShapeDtypeStruct((4, 128), F32), jax.ShapeDtypeStruct((8, 128), F32)),
        name="token_diffs",
    )(stats, live, seg)


def turn_kernel(w_ref, out_ref):
    width = out_ref.shape[2]
    for j in range(4):
        out_ref[j] = w_ref[:, j * width : (j + 1) * width]


def turned(m, w_out):
    _, inner, depth = w_out.shape
    width = depth // 4
    return pl.pallas_call(
        turn_kernel,
        grid=(1,),
        in_specs=[pl.BlockSpec((None, inner, depth), lambda j: (m, 0, 0))],
        out_specs=pl.BlockSpec((4, inner, width), lambda j: (0, 0, 0)),
        out_shape=jax.ShapeDtypeStruct((4, inner, width), w_out.dtype),
        cost_estimate=pl.CostEstimate(flops=0, bytes_accessed=2 * 10**6, transcendentals=0),
        name="turned",
    )(w_out)


def ring(value, axis, by):
    return lax.ppermute(value, axis, [(i, (i + by) % 4) for i in range(4)])


def gathered(value, axis):
    return [value] + [ring(value, axis, k) for k in (1, 2, 3)]


def per_device(
    hidden, w_inner, w_state, w_step, step_bias, rate, skip_gain, norm_gain, w_out, final_gain, head, pool,
    targets, segment_ids, flags, pages, live, owners,
):
    rows = targets.shape[0]
    depth = hidden.shape[2]
    inner = w_inner.shape[3]
    group = lax.axis_size(VOC)
    devices = lax.axis_size(SEQ)
    place = lax.axis_index(VOC).astype(jnp.int32).reshape(1)
    seg = segment_ids.reshape(1, rows)
    tgt = targets.reshape(4, rows // 4)
    w_inner = jnp.swapaxes(w_inner, 1, 2)
    w_state = jnp.swapaxes(w_state, 1, 2)
    w_step = jnp.swapaxes(w_step, 1, 2)
    ways = (("x", "z"), ("z", "x"))
    both = range(2)
    at = [
        jnp.stack([lax.axis_index(along), lax.axis_index(across)]).astype(jnp.int32) for along, across in ways
    ]
    weights = [lax.all_to_all(turned(m, w_out), ways[m][0], 0, 0) for m in both]
    y, gate, c, e, pay = mix_local(hidden, w_inner, w_state, w_step, step_bias, rate, skip_gain, seg)
    recv = [lax.ppermute(pay, SEQ, [(i, i + k) for i in range(devices - k)]) for k in range(1, REACH + 1)]
    gated, parts, res, full = [], [], [], []
    for m in both:
        gated.append(gate_out(m, pages, flags, y, gate, c, e, recv, pool, norm_gain, tuple(gated)))
    for m in both:
        out = out_blocks(at[m], gathered(gated[m], ways[m][0]), weights[m], (gated[1],))
        parts.append([out[0]] + [ring(out[k], ways[m][1], k) for k in (1, 2, 3)])
    for m in both:
        res.append(residual_block(m, at[m], parts[m], hidden, final_gain, inner * group, (parts[1][0],)))
    blocks = [gathered(res[m], ways[m][0]) for m in both]
    for m in both:
        full.append(join_columns(at[m], blocks[m], tuple(blocks[1 - m][1:])))
    ready = fetched(head, tuple(full))
    near = [[full[m]] + [ring(full[m], ways[m][1], k) for k in (1, 3)] for m in both]
    halves = cut_halves([near[m][1:] for m in both], (ready,))
    cut = [[ring(halves[2 * m], ways[m][1], 1), ring(halves[2 * m + 1], ways[m][1], 3)] for m in both]
    merged = lax.all_to_all(head_stats(place, at, near, cut, ready, tgt, group), VOC, 0, 0)
    diff, sums = token_diffs(merged, live, segment_ids.reshape(4, 128))
    sums = sums + lax.ppermute(sums, "core", [(0, 1), (1, 0)])
    sums = sum(gathered(sums, "y"))[0:4, 0]
    owned = jnp.where(owners == lax.axis_index(SEQ), sums, 0.0)
    return diff.reshape(rows), owned[None]


def solution(mesh):
    seq, vocab = mesh.devices.shape
    fine = Mesh(mesh.devices.reshape(seq // 2, 2, 4, vocab // 4), ("y", "core", "x", "z"))
    placed = (
        P(None, SEQ, None),
        P(None, None, None, VOC),
        P(),
        P(None, None, VOC),
        P(None, VOC),
        P(None, VOC),
        P(None, VOC),
        P(None, VOC),
        P(None, VOC, None),
        P(),
        P(None, None, VOC),
        P(None, None, VOC, None, None),
        P(SEQ),
        P(SEQ),
        P(),
        P(),
        P(SEQ),
        P(),
    )
    return jax.shard_map(
        per_device, mesh=fine, in_specs=placed, out_specs=(P(SEQ), P(SEQ, None)), check_vma=False
    )
```

```python
import functools

import jax
import jax.numpy as jnp
from jax import lax
from jax.experimental import pallas as pl
from jax.experimental.pallas import tpu as pltpu
from jax.sharding import Mesh
from jax.sharding import PartitionSpec as P

NORM_EPS = 1e-05
SPAN = 256
REACH = 4
SEQ = ("y", "core")
VOC = ("x", "z")
F32 = jnp.float32
BF16 = jnp.bfloat16
LOW = -1e30
LOG2E = 1.4426950408889634


def silu(v):
    return v / (1.0 + jnp.exp(-v))


def contract(a, b, dims):
    return lax.dot_general(a, b, (dims, ((), ())), preferred_element_type=F32)


def drop(kernel, inputs, count):
    def body(*refs):
        return kernel(*refs[:inputs], *refs[inputs + count :])

    return body


ANYWHERE = pl.BlockSpec(memory_space=pl.ANY)


def pieces(value):
    high = value.astype(BF16).astype(F32)
    mid = (value - high).astype(BF16).astype(F32)
    return [high, mid, value - high - mid]


def to_column(row):
    return jnp.transpose(jnp.broadcast_to(row, (8, row.shape[1])))[:, 0:1]


def to_row(column):
    return jnp.transpose(jnp.broadcast_to(column, (column.shape[0], 8)))[0:1, :]


def as_column(row):
    count = row.shape[1]
    spread = jnp.broadcast_to(row, (count, count))
    eye = lax.broadcasted_iota(jnp.int32, spread.shape, 0) == lax.broadcasted_iota(jnp.int32, spread.shape, 1)
    return jnp.sum(jnp.where(eye, spread, 0.0), axis=1, keepdims=True)


def mix_kernel(
    tok_ref, wi_ref, ws_ref, wp_ref, bias_ref, rate_ref, skip_ref, seg_ref,
    y_ref, gate_ref, c_ref, e_ref, pay_ref, val_ref, st_ref, stp_ref,
):
    m = pl.program_id(0)
    k = pl.program_id(1)
    inner = y_ref.shape[1]

    @pl.when(k == 0)
    def _():
        gate_ref[...] = jnp.zeros_like(gate_ref)
        val_ref[...] = jnp.zeros_like(val_ref)
        st_ref[...] = jnp.zeros_like(st_ref)
        stp_ref[...] = jnp.zeros_like(stp_ref)

    tokens = tok_ref[...]
    state = c_ref.shape[1]
    gate_ref[...] += contract(tokens, wi_ref[0], ((1,), (0,)))
    val_ref[...] += contract(tokens, wi_ref[1], ((1,), (0,)))
    st_ref[:, 0:state] += contract(tokens, ws_ref[0], ((1,), (0,)))
    st_ref[:, state:] += contract(tokens, ws_ref[1], ((1,), (0,)))
    stp_ref[...] += contract(tokens, wp_ref[...], ((1,), (1,)))

    @pl.when(k == pl.num_programs(1) - 1)
    def _():
        scan_rows(
            m, bias_ref, rate_ref, skip_ref, seg_ref, y_ref, c_ref, e_ref, pay_ref, val_ref, st_ref, stp_ref
        )


def scan_rows(m, bias_ref, rate_ref, skip_ref, seg_ref, y_ref, c_ref, e_ref, pay_ref, val_ref, st_ref, stp_ref):
    rows, inner = y_ref.shape
    heads = bias_ref.shape[1]
    wide = inner // heads
    state = c_ref.shape[1]
    seg = seg_ref[...]
    raw = jnp.transpose(stp_ref[...])[0:heads, :] + as_column(bias_ref[pl.ds(m, 1), :])
    dt = jnp.maximum(raw, 0.0) + jnp.log1p(jnp.exp(-jnp.abs(raw)))
    la = -dt * as_column(rate_ref[pl.ds(m, 1), :])
    skip = as_column(skip_ref[pl.ds(m, 1), :])
    lane = lax.broadcasted_iota(jnp.int32, la.shape, 1)
    run = la
    step = 1
    while step < rows:
        run = run + jnp.where(lane >= step, pltpu.roll(run, step, 1), 0.0)
        step *= 2
    last = jnp.max(seg, axis=1, keepdims=True)
    base = jnp.zeros_like(la)
    for j in range(4):
        base_j = jnp.sum(jnp.where(seg < j, la, 0.0), axis=1, keepdims=True)
        base = jnp.where(seg == j, base_j, base)
    total = jnp.sum(la, axis=1, keepdims=True)
    grow = jnp.exp(run - base)
    keep = jnp.where(seg == last, jnp.exp(jnp.minimum(total - run, 0.0)) * dt, 0.0)
    tail = jnp.exp(jnp.sum(jnp.where(seg == last, la, 0.0), axis=1, keepdims=True))
    cols = jnp.transpose(jnp.concatenate([run, keep], axis=0))
    segf = jnp.broadcast_to(seg.astype(F32), (heads, rows))
    ecol = jnp.transpose(jnp.concatenate([grow, segf], axis=0))
    e_ref[...] = ecol
    values = silu(val_ref[...]).astype(BF16)
    in_map = silu(st_ref[:, 0:state]).astype(BF16)
    out_map = silu(st_ref[:, state:]).astype(BF16)
    c_ref[...] = out_map
    vf = values.astype(F32)
    kept = jnp.concatenate(
        [vf[:, h * wide : (h + 1) * wide] * cols[:, heads + h : heads + h + 1] for h in range(heads)], axis=1
    ).astype(BF16)
    added = contract(kept, in_map, ((0,), (0,)))
    pay_ref[0:inner, :] = added.astype(BF16)
    high = tail.astype(BF16).astype(F32)
    low = tail - high
    meta = jnp.concatenate(
        [
            jnp.broadcast_to(high, (heads, state)),
            jnp.broadcast_to(low, (heads, state)),
            jnp.broadcast_to(last.astype(F32) + 1.0, (8, state)),
        ],
        axis=0,
    )
    pay_ref[inner : inner + 16, :] = meta.astype(BF16)
    blocks = rows // SPAN
    for i in range(blocks):
        t0 = i * SPAN
        acc = [vf[t0 : t0 + SPAN, h * wide : (h + 1) * wide] * skip[h : h + 1, :] for h in range(heads)]
        for j in range(i + 1):
            s0 = j * SPAN
            scores = contract(out_map[t0 : t0 + SPAN], in_map[s0 : s0 + SPAN], ((1,), (1,)))
            same = ecol[t0 : t0 + SPAN, heads : heads + 1] == segf[0:1, s0 : s0 + SPAN]
            if i == j:
                same = same & (
                    lax.broadcasted_iota(jnp.int32, (SPAN, SPAN), 0)
                    >= lax.broadcasted_iota(jnp.int32, (SPAN, SPAN), 1)
                )
            for h in range(heads):
                gap = cols[t0 : t0 + SPAN, h : h + 1] - run[h : h + 1, s0 : s0 + SPAN]
                weight = jnp.exp(jnp.where(same, gap, LOW)) * (scores * dt[h : h + 1, s0 : s0 + SPAN])
                acc[h] = acc[h] + contract(
                    weight.astype(BF16), values[s0 : s0 + SPAN, h * wide : (h + 1) * wide], ((1,), (0,))
                )
        y_ref[t0 : t0 + SPAN, :] = jnp.concatenate(acc, axis=1)


def mix_local(hidden, w_inner, w_state, w_step, bias, rate, skip, seg, chunks=2):
    models, rows, depth = hidden.shape
    inner = w_inner.shape[3]
    state = w_state.shape[3]
    heads = bias.shape[1]
    deep = depth // chunks
    whole = lambda a: pl.BlockSpec(a.shape, lambda m, k: (0,) * a.ndim)
    shapes = ((rows, inner), F32), ((rows, inner), F32), ((rows, state), BF16), ((rows, 2 * heads), F32), (
        (inner + 16, state), BF16)
    return pl.pallas_call(
        mix_kernel,
        grid=(models, chunks),
        in_specs=[
            pl.BlockSpec((None, rows, deep), lambda m, k: (m, 0, k)),
            pl.BlockSpec((None, 2, deep, inner), lambda m, k: (m, 0, k, 0)),
            pl.BlockSpec((None, 2, deep, state), lambda m, k: (m, 0, k, 0)),
            pl.BlockSpec((None, heads, deep), lambda m, k: (m, 0, k)),
            whole(bias), whole(rate), whole(skip), whole(seg),
        ],
        out_specs=[pl.BlockSpec((None,) + shape, lambda m, k: (m, 0, 0)) for shape, _ in shapes],
        out_shape=[jax.ShapeDtypeStruct((models,) + shape, kind) for shape, kind in shapes],
        scratch_shapes=[
            pltpu.VMEM((rows, inner), F32), pltpu.VMEM((rows, 2 * state), F32), pltpu.VMEM((rows, heads), F32)
        ],
        cost_estimate=pl.CostEstimate(flops=10**10, bytes_accessed=16 * 10**6, transcendentals=2 * 10**6),
        name="mix_local",
    )(hidden, w_inner, w_state, w_step, bias, rate, skip, seg)


def gate_kernel(
    pages_ref, flags_ref, y_ref, gate_ref, c_ref, e_ref, r1_ref, r2_ref, r3_ref, r4_ref,
    p0_ref, p1_ref, p2_ref, p3_ref, gain_ref, out0_ref, out1_ref, pick_ref,
):
    m = pl.program_id(0)
    rows, inner = y_ref.shape
    heads = p0_ref.shape[0]
    wide = inner // heads
    state = c_ref.shape[1]
    e_col = e_ref[...]
    seg_col = e_col[:, heads : heads + 1]
    seg_first = e_col[0:1, heads : heads + 1]
    init = [
        p.reshape(inner, state)[...].astype(F32) * flags_ref[j].astype(F32)
        for j, p in enumerate((p0_ref, p1_ref, p2_ref, p3_ref))
    ]
    through = jnp.ones((heads, state), F32)
    parts = [jnp.zeros((wide, state), F32) for _ in range(heads)]
    for r in (r1_ref, r2_ref, r3_ref, r4_ref):
        meta = r[inner : inner + 16, :].astype(F32)
        hit = meta[8:9, :] == seg_first + 1.0
        piece = r[0:inner, :].astype(F32)
        weight = jnp.where(hit, through, 0.0)
        for h in range(heads):
            parts[h] = parts[h] + weight[h : h + 1, :] * piece[h * wide : (h + 1) * wide, :]
        through = jnp.where(hit, through * (meta[0:heads] + meta[heads : 2 * heads]), through)
    prior = jnp.concatenate(parts, axis=0)
    through = jnp.concatenate([jnp.broadcast_to(through[h : h + 1, :], (wide, state)) for h in range(heads)], axis=0)
    out_map = c_ref[...]
    low_id, high_id = jnp.min(seg_col), jnp.max(seg_col)
    pick_ref[...] = jnp.zeros_like(pick_ref)
    for j in range(4):

        @pl.when((low_id <= j) & (high_id >= j))
        def _():
            start = jnp.where(seg_first == float(j), prior + through * init[j], init[j])
            high = start.astype(BF16)
            low = (start - high.astype(F32)).astype(BF16)
            from_state = contract(out_map, high, ((1,), (1,))) + contract(out_map, low, ((1,), (1,)))
            pick_ref[...] = jnp.where(seg_col == float(j), from_state, pick_ref[...])

    picked = pick_ref[...]
    spread = jnp.concatenate([jnp.broadcast_to(e_col[:, h : h + 1], (rows, wide)) for h in range(heads)], axis=1)
    gated = (y_ref[...] + picked * spread) * silu(gate_ref[...])
    square = jnp.sum(gated * gated, axis=1, keepdims=True)
    mixed = (gated * gain_ref[pl.ds(m, 1), :]).astype(BF16)
    lines = to_row(square)
    halves = jnp.concatenate([lines[:, 0:inner], lines[:, inner:]], axis=0)
    extra = jnp.concatenate(pieces(halves) + [jnp.zeros((10, inner), F32)], axis=0).astype(BF16)
    for n, out in enumerate((out0_ref, out1_ref)):

        @pl.when(m == n)
        def _():
            out[0:rows, :] = mixed
            out[rows : rows + 16, :] = extra


def gate_out(pages, flags, y, gate, c, e, recv, pool, gain):
    models, rows, inner = y.shape
    heads = pool.shape[2]
    state = c.shape[2]
    mine = lambda a: pl.BlockSpec((None,) + a.shape[1:], lambda m, pg, fl: (m, 0, 0))
    page = lambda j: pl.BlockSpec(
        (None, None, heads, pool.shape[3], state), lambda m, pg, fl: (m, pg[j], 0, 0, 0)
    )
    return pl.pallas_call(
        gate_kernel,
        grid_spec=pltpu.PrefetchScalarGridSpec(
            num_scalar_prefetch=2,
            grid=(models,),
            in_specs=[mine(y), mine(gate), mine(c), mine(e)]
            + [mine(r) for r in recv]
            + [page(j) for j in range(4)]
            + [pl.BlockSpec(gain.shape, lambda m, pg, fl: (0, 0))],
            out_specs=[pl.BlockSpec((rows + 16, inner), lambda m, pg, fl: (0, 0))] * models,
            scratch_shapes=[pltpu.VMEM((rows, inner), F32)],
        ),
        out_shape=[jax.ShapeDtypeStruct((rows + 16, inner), BF16)] * models,
        cost_estimate=pl.CostEstimate(flops=2 * 10**9, bytes_accessed=2 * 10**7, transcendentals=10**5),
        name="gate_out",
    )(pages, flags, y, gate, c, e, *recv, pool, pool, pool, pool, gain)


def out_kernel(at_ref, g0_ref, g1_ref, g2_ref, g3_ref, w_ref, o0_ref, o1_ref, o2_ref, o3_ref, acc_ref, sq_ref):
    rows, width = acc_ref.shape
    inner = g0_ref.shape[1]
    block = rows // 4
    along, across = at_ref[0], at_ref[1]
    gathered = (g0_ref, g1_ref, g2_ref, g3_ref)
    extra = sum(g[rows : rows + 16, :].astype(F32) for g in gathered)
    square = extra[0:2] + extra[2:4] + extra[4:6]
    for n in range(4):
        sq_ref[n : n + 1, :] = square[n // 2 : n // 2 + 1, (n % 2) * block : (n % 2 + 1) * block]
    acc_ref[...] = sum(
        contract(g[0:rows, :], w_ref[lax.rem(along + 4 - k, 4)], ((1,), (0,))) for k, g in enumerate(gathered)
    )
    for k, out in enumerate((o0_ref, o1_ref, o2_ref, o3_ref)):
        at = lax.rem(across + k, 4)
        out[0:block, :] = acc_ref[pl.ds(pl.multiple_of(at * block, block), block), :].astype(BF16)
        line = jnp.concatenate(pieces(sq_ref[pl.ds(at, 1), :]) + [jnp.zeros((1, width - 3 * block), F32)], axis=1)
        out[block : block + 16, :] = jnp.broadcast_to(line, (16, width)).astype(BF16)


def out_blocks(at, gathered, w, after=()):
    rows = gathered[0].shape[0] - 16
    width = w.shape[2]
    block = rows // 4
    vm = pl.BlockSpec(memory_space=pltpu.VMEM)
    return pl.pallas_call(
        drop(out_kernel, 6, len(after)),
        in_specs=[pl.BlockSpec(memory_space=pltpu.SMEM)] + [vm] * 5 + [ANYWHERE] * len(after),
        out_specs=[vm] * 4,
        out_shape=[jax.ShapeDtypeStruct((block + 16, width), BF16)] * 4,
        scratch_shapes=[pltpu.VMEM((rows, width), F32), pltpu.VMEM((4, block), F32)],
        cost_estimate=pl.CostEstimate(flops=10**9, bytes_accessed=10**7, transcendentals=0),
        compiler_params=pltpu.CompilerParams(vmem_limit_bytes=14 * 2**20),
        name="out_blocks",
    )(at, *gathered, w, *after)


def residual_kernel(m, units, at_ref, o0_ref, o1_ref, o2_ref, o3_ref, hid_ref, gain_ref, out_ref):
    block, width = hid_ref.shape
    total = sum(o[...].astype(F32) for o in (o0_ref, o1_ref, o2_ref, o3_ref))
    line = total[block : block + 1, :]
    square = line[:, 0:block] + line[:, block : 2 * block] + line[:, 2 * block : 3 * block]
    scale = to_column(lax.rsqrt(square / units + NORM_EPS))
    res = hid_ref[...].astype(F32) + total[0:block, :] * scale
    out_ref[0:block, :] = (res * gain_ref[m : m + 1, :]).astype(BF16)
    line = jnp.concatenate(
        pieces(to_row(jnp.sum(res * res, axis=1, keepdims=True))) + [jnp.zeros((1, width - 3 * block), F32)], axis=1
    )
    out_ref[block : block + 16, :] = jnp.broadcast_to(line, (16, width)).astype(BF16)


def residual_block(m, at, parts, hidden, gain, units, after=()):
    block, width = parts[0].shape[0] - 16, parts[0].shape[1]
    whole = pl.BlockSpec((block + 16, width), lambda g, at: (0, 0))
    return pl.pallas_call(
        drop(functools.partial(residual_kernel, m, float(units)), 7, len(after)),
        grid_spec=pltpu.PrefetchScalarGridSpec(
            num_scalar_prefetch=1,
            grid=(1,),
            in_specs=[whole] * 4
            + [
                pl.BlockSpec((block, width), lambda g, at: (0, 0)),
                pl.BlockSpec((2, width), lambda g, at: (0, at[0])),
            ]
            + [ANYWHERE] * len(after),
            out_specs=whole,
        ),
        out_shape=jax.ShapeDtypeStruct((block + 16, width), BF16),
        cost_estimate=pl.CostEstimate(flops=10**6, bytes_accessed=9 * 10**6, transcendentals=100),
        compiler_params=pltpu.CompilerParams(vmem_limit_bytes=8 * 2**20),
        name="residual_block",
    )(at, *parts, hidden, gain, *after)


def join_kernel(at_ref, u0_ref, u1_ref, u2_ref, u3_ref, out_ref):
    block, width = u0_ref.shape[0] - 16, u0_ref.shape[1]
    square = jnp.zeros((1, block), F32)
    half = block // 2
    for k, u in enumerate((u0_ref, u1_ref, u2_ref, u3_ref)):
        at = pl.multiple_of(lax.rem(at_ref[0] + 4 - k, 4) * width, width)
        for n in range(2):
            out_ref[n * (half + 8) + 8 : (n + 1) * (half + 8), pl.ds(at, width)] = u[n * half : (n + 1) * half, :]
        line = u[block : block + 16, :].astype(F32)[0:1, :]
        square = square + line[:, 0:block] + line[:, block : 2 * block] + line[:, 2 * block : 3 * block]
    parts = pieces(lax.rsqrt(square / out_ref.shape[1] + NORM_EPS))
    for n in range(2):
        line = jnp.concatenate(
            [p[:, n * half : (n + 1) * half] for p in parts] + [jnp.zeros((1, 256 - 3 * half), F32)], axis=1
        )
        out_ref[n * (half + 8) : n * (half + 8) + 8, 0:256] = jnp.broadcast_to(line, (8, 256)).astype(BF16)
        out_ref[n * (half + 8) : n * (half + 8) + 8, 256:] = jnp.zeros((8, out_ref.shape[1] - 256), BF16)


def join_columns(at, parts, after=()):
    tall, width = parts[0].shape
    vm = pl.BlockSpec(memory_space=pltpu.VMEM)
    return pl.pallas_call(
        drop(join_kernel, 5, len(after)),
        in_specs=[pl.BlockSpec(memory_space=pltpu.SMEM)] + [vm] * 4 + [ANYWHERE] * len(after),
        out_specs=vm,
        out_shape=jax.ShapeDtypeStruct((tall, 4 * width), BF16),
        cost_estimate=pl.CostEstimate(flops=10**5, bytes_accessed=6 * 10**6, transcendentals=100),
        compiler_params=pltpu.CompilerParams(vmem_limit_bytes=8 * 2**20),
        name="join_columns",
    )(at, *parts, *after)


def fetch_kernel(w_ref, out_ref, sems):
    depth = w_ref.shape[1]
    half = depth // 2
    copies = [
        pltpu.make_async_copy(
            w_ref.at[m, pl.ds(n * half, half), :], out_ref.at[m, pl.ds(n * half, half), :], sems.at[2 * m + n]
        )
        for m in range(2)
        for n in range(2)
    ]
    for copy in copies:
        copy.start()
    for copy in copies:
        copy.wait()


def fetched(head, after):
    return pl.pallas_call(
        drop(fetch_kernel, 1, len(after)),
        in_specs=[ANYWHERE] + [ANYWHERE] * len(after),
        out_specs=pl.BlockSpec(memory_space=pltpu.VMEM),
        out_shape=pltpu.VMEM(head.shape, head.dtype),
        scratch_shapes=[pltpu.SemaphoreType.DMA((4,))],
        compiler_params=pltpu.CompilerParams(vmem_limit_bytes=40 * 2**20),
        cost_estimate=pl.CostEstimate(flops=0, bytes_accessed=3 * 10**7, transcendentals=0),
        name="fetched",
    )(head, *after)


def score_rows(m, halves, places, base, w_ref, tgt_ref, acc_ref, put):
    half = halves[0].shape[0] - 8
    block = 2 * half
    rows = jnp.concatenate([x[8 : half + 8, :] for x in halves], axis=0)
    acc_ref[0 : rows.shape[0], :] = contract(rows, w_ref[m], ((1,), (0,)))
    for k, at in enumerate(places):
        lines = [x[0:8, 0:256].astype(F32)[0:1, :] for x in halves[2 * k : 2 * k + 2]]
        scale = to_column(
            jnp.concatenate(
                [v[:, 0:half] + v[:, half : 2 * half] + v[:, 2 * half : 3 * half] for v in lines], axis=1
            )
        )
        raw = acc_ref[k * block : (k + 1) * block, :]
        top = jnp.max(raw, axis=1, keepdims=True)
        total = jnp.sum(jnp.exp2((raw - top) * (scale * LOG2E)), axis=1, keepdims=True)
        target = to_column((tgt_ref[pl.ds(at, 1), :] - base).astype(F32)).astype(jnp.int32)
        column = lax.broadcasted_iota(jnp.int32, raw.shape, 1)
        chosen = jnp.sum(jnp.where(column == target, raw, 0.0), axis=1, keepdims=True) * scale
        put(m * 8 + at, to_row(top * scale + jnp.log(total)))
        put(m * 8 + 4 + at, to_row(chosen))


def near_kernel(place_ref, at0_ref, at1_ref, *refs):
    w_ref, tgt_ref, out_ref, acc_ref = refs[6:]
    half = refs[0].shape[0] // 2
    base = place_ref[0] * w_ref.shape[2]

    def put(row, value):
        out_ref[pl.ds(row, 1), :] = value

    for m, at_ref in enumerate((at0_ref, at1_ref)):
        tiles = refs[3 * m : 3 * m + 3]
        halves = [x.at[pl.ds(n * half, half), :] for x in tiles for n in range(2)]
        places = [lax.rem(at_ref[1] + 4 - k, 4) for k in (0, 1, 3)]
        score_rows(m, halves, places, base, w_ref, tgt_ref, acc_ref, put)


def far_kernel(place_ref, at0_ref, at1_ref, *refs):
    w_ref, tgt_ref, near_ref, out_ref, acc_ref = refs[4:]
    base = place_ref[0] * w_ref.shape[2]
    out_ref[...] = jnp.broadcast_to(near_ref[...][None], out_ref.shape)

    def put(row, value):
        out_ref[:, pl.ds(row, 1), :] = jnp.broadcast_to(value[None], (out_ref.shape[0], 1, value.shape[1]))

    for m, at_ref in enumerate((at0_ref, at1_ref)):
        places = [lax.rem(at_ref[1] + 2, 4)]
        score_rows(m, refs[2 * m : 2 * m + 2], places, base, w_ref, tgt_ref, acc_ref, put)


def head_stats(place, at, near, cut, head, tgt, group):
    tall, depth = near[0][0].shape
    block = tall - 16
    vocab = head.shape[2]
    vm = pl.BlockSpec(memory_space=pltpu.VMEM)
    sm = pl.BlockSpec(memory_space=pltpu.SMEM)
    common = dict(out_specs=vm, compiler_params=pltpu.CompilerParams(vmem_limit_bytes=24 * 2**20))
    cost = lambda blocks: pl.CostEstimate(
        flops=4 * blocks * block * depth * vocab, bytes_accessed=10**7, transcendentals=2 * blocks * block * vocab
    )
    first = pl.pallas_call(
        near_kernel,
        in_specs=[sm] * 3 + [vm] * 8,
        scratch_shapes=[pltpu.VMEM((3 * block, vocab), F32)],
        out_shape=jax.ShapeDtypeStruct((16, block), F32),
        cost_estimate=cost(3),
        name="head_near",
        **common,
    )(place, *at, *near[0], *near[1], head, tgt)
    return pl.pallas_call(
        far_kernel,
        in_specs=[sm] * 3 + [vm] * 7,
        scratch_shapes=[pltpu.VMEM((block, vocab), F32)],
        out_shape=jax.ShapeDtypeStruct((group, 16, block), F32),
        cost_estimate=cost(1),
        name="head_far",
        **common,
    )(place, *at, *cut[0], *cut[1], head, tgt, first)


def cut_kernel(a_ref, b_ref, c_ref, d_ref, oa_ref, ob_ref, oc_ref, od_ref):
    oa_ref[...] = a_ref[...]
    ob_ref[...] = b_ref[...]
    oc_ref[...] = c_ref[...]
    od_ref[...] = d_ref[...]


def cut_halves(pairs, after):
    tall, depth = pairs[0][0].shape
    low = pl.BlockSpec((tall // 2, depth), lambda g: (0, 0))
    high = pl.BlockSpec((tall // 2, depth), lambda g: (1, 0))
    return pl.pallas_call(
        drop(cut_kernel, 4, len(after)),
        grid=(1,),
        in_specs=[low, high] * 2 + [ANYWHERE] * len(after),
        out_specs=[low] * 4,
        out_shape=[jax.ShapeDtypeStruct((tall // 2, depth), BF16)] * 4,
        compiler_params=pltpu.CompilerParams(vmem_limit_bytes=8 * 2**20),
        cost_estimate=pl.CostEstimate(flops=0, bytes_accessed=2 * 10**6, transcendentals=0),
        name="cut_halves",
    )(*pairs[0], *pairs[1], *after)


def diff_kernel(stat_ref, live_ref, seg_ref, diff_ref, sums_ref):
    scores = []
    for m in range(2):
        part = stat_ref[:, 8 * m : 8 * m + 8, :]
        lse = part[:, 0:4, :]
        top = jnp.max(lse, axis=0)
        total = top + jnp.log(jnp.sum(jnp.exp(lse - top[None]), axis=0))
        scores.append(jnp.sum(part[:, 4:8, :], axis=0) - total)
    lines = lax.broadcasted_iota(jnp.int32, (4, 128), 0)
    alive = jnp.where(lines < 2, live_ref[0].astype(F32), live_ref[1].astype(F32))
    diff = alive * (scores[0] - scores[1])
    diff_ref[...] = diff
    which = lax.broadcasted_iota(jnp.int32, (8, 128), 0)
    sums = jnp.zeros((8, 128), F32)
    for j in range(4):
        mine = jnp.sum(jnp.where(seg_ref[...] == j, diff, 0.0), axis=1, keepdims=True)
        sums = jnp.where(which == j, jnp.sum(mine, axis=0, keepdims=True), sums)
    sums_ref[...] = sums


def token_diffs(stats, live, seg):
    vm = pl.BlockSpec(memory_space=pltpu.VMEM)
    return pl.pallas_call(
        diff_kernel,
        in_specs=[vm, pl.BlockSpec(memory_space=pltpu.SMEM), vm],
        out_shape=(jax.ShapeDtypeStruct((4, 128), F32), jax.ShapeDtypeStruct((8, 128), F32)),
        name="token_diffs",
    )(stats, live, seg)


def turn_kernel(at_ref, w_ref, hid_ref, out_ref, mine_ref):
    width = out_ref.shape[2]
    for j in range(4):
        out_ref[j] = w_ref[:, j * width : (j + 1) * width]
    mine_ref[...] = hid_ref[...]


def turned(m, at, w_out, hidden):
    _, inner, depth = w_out.shape
    width = depth // 4
    block = hidden.shape[1] // 4
    return pl.pallas_call(
        turn_kernel,
        grid_spec=pltpu.PrefetchScalarGridSpec(
            num_scalar_prefetch=1,
            grid=(1,),
            in_specs=[
                pl.BlockSpec((None, inner, depth), lambda j, at: (m, 0, 0)),
                pl.BlockSpec((None, block, width), lambda j, at: (m, at[1], at[0])),
            ],
            out_specs=[
                pl.BlockSpec((4, inner, width), lambda j, at: (0, 0, 0)),
                pl.BlockSpec((block, width), lambda j, at: (0, 0)),
            ],
        ),
        out_shape=[
            jax.ShapeDtypeStruct((4, inner, width), w_out.dtype),
            jax.ShapeDtypeStruct((block, width), hidden.dtype),
        ],
        cost_estimate=pl.CostEstimate(flops=0, bytes_accessed=6 * 10**6, transcendentals=0),
        name="turned",
    )(at, w_out, hidden)


def ring(value, axis, by):
    return lax.ppermute(value, axis, [(i, (i + by) % 4) for i in range(4)])


def gathered(value, axis):
    return [value] + [ring(value, axis, k) for k in (1, 2, 3)]


def per_device(
    hidden, w_inner, w_state, w_step, step_bias, rate, skip_gain, norm_gain, w_out, final_gain, head, pool,
    targets, segment_ids, flags, pages, live, owners,
):
    rows = targets.shape[0]
    depth = hidden.shape[2]
    inner = w_inner.shape[3]
    group = lax.axis_size(VOC)
    devices = lax.axis_size(SEQ)
    place = lax.axis_index(VOC).astype(jnp.int32).reshape(1)
    seg = segment_ids.reshape(1, rows)
    tgt = targets.reshape(4, rows // 4)
    w_inner = jnp.swapaxes(w_inner, 1, 2)
    w_state = jnp.swapaxes(w_state, 1, 2)
    w_step = jnp.swapaxes(w_step, 1, 2)
    ways = (("x", "z"), ("z", "x"))
    both = range(2)
    at = [
        jnp.stack([lax.axis_index(along), lax.axis_index(across)]).astype(jnp.int32) for along, across in ways
    ]
    turns = [turned(m, at[m], w_out, hidden) for m in both]
    weights = [lax.all_to_all(turns[m][0], ways[m][0], 0, 0) for m in both]
    y, gate, c, e, pay = mix_local(hidden, w_inner, w_state, w_step, step_bias, rate, skip_gain, seg)
    recv = [lax.ppermute(pay, SEQ, [(i, i + k) for i in range(devices - k)]) for k in range(1, REACH + 1)]
    parts, res, full = [], [], []
    gated = gate_out(pages, flags, y, gate, c, e, recv, pool, norm_gain)
    for m in both:
        out = out_blocks(at[m], gathered(gated[m], ways[m][0]), weights[m])
        parts.append([out[0]] + [ring(out[k], ways[m][1], k) for k in (1, 2, 3)])
    for m in both:
        res.append(residual_block(m, at[m], parts[m], turns[m][1], final_gain, inner * group, (parts[1][0],)))
    blocks = [gathered(res[m], ways[m][0]) for m in both]
    for m in both:
        full.append(join_columns(at[m], blocks[m], tuple(blocks[1 - m][1:])))
    ready = fetched(head, tuple(full))
    near = [[full[m]] + [ring(full[m], ways[m][1], k) for k in (1, 3)] for m in both]
    halves = cut_halves([near[m][1:] for m in both], (ready,))
    cut = [[ring(halves[2 * m], ways[m][1], 1), ring(halves[2 * m + 1], ways[m][1], 3)] for m in both]
    merged = lax.all_to_all(head_stats(place, at, near, cut, ready, tgt, group), VOC, 0, 0)
    diff, sums = token_diffs(merged, live, segment_ids.reshape(4, 128))
    sums = sums + lax.ppermute(sums, "core", [(0, 1), (1, 0)])
    sums = sum(gathered(sums, "y"))[0:4, 0]
    owned = jnp.where(owners == lax.axis_index(SEQ), sums, 0.0)
    return diff.reshape(rows), owned[None]


def solution(mesh):
    seq, vocab = mesh.devices.shape
    fine = Mesh(mesh.devices.reshape(seq // 2, 2, 4, vocab // 4), ("y", "core", "x", "z"))
    placed = (
        P(None, SEQ, None),
        P(None, None, None, VOC),
        P(),
        P(None, None, VOC),
        P(None, VOC),
        P(None, VOC),
        P(None, VOC),
        P(None, VOC),
        P(None, VOC, None),
        P(),
        P(None, None, VOC),
        P(None, None, VOC, None, None),
        P(SEQ),
        P(SEQ),
        P(),
        P(),
        P(SEQ),
        P(),
    )
    return jax.shard_map(
        per_device, mesh=fine, in_specs=placed, out_specs=(P(SEQ), P(SEQ, None)), check_vma=False
    )
```

```python
import functools

import jax
import jax.numpy as jnp
from jax import lax
from jax.experimental import pallas as pl
from jax.experimental.pallas import tpu as pltpu
from jax.sharding import Mesh
from jax.sharding import PartitionSpec as P

NORM_EPS = 1e-05
SPAN = 256
REACH = 4
SEQ = ("y", "core")
VOC = ("x", "z")
F32 = jnp.float32
BF16 = jnp.bfloat16
LOW = -1e30
LOG2E = 1.4426950408889634


def silu(v):
    return v / (1.0 + jnp.exp(-v))


def contract(a, b, dims):
    return lax.dot_general(a, b, (dims, ((), ())), preferred_element_type=F32)


def drop(kernel, inputs, count):
    def body(*refs):
        return kernel(*refs[:inputs], *refs[inputs + count :])

    return body


ANYWHERE = pl.BlockSpec(memory_space=pl.ANY)


def pieces(value):
    high = value.astype(BF16).astype(F32)
    mid = (value - high).astype(BF16).astype(F32)
    return [high, mid, value - high - mid]


def to_column(row):
    return jnp.transpose(jnp.broadcast_to(row, (8, row.shape[1])))[:, 0:1]


def to_row(column):
    return jnp.transpose(jnp.broadcast_to(column, (column.shape[0], 8)))[0:1, :]


def as_column(row):
    count = row.shape[1]
    spread = jnp.broadcast_to(row, (count, count))
    eye = lax.broadcasted_iota(jnp.int32, spread.shape, 0) == lax.broadcasted_iota(jnp.int32, spread.shape, 1)
    return jnp.sum(jnp.where(eye, spread, 0.0), axis=1, keepdims=True)


def mix_kernel(
    tok_ref, wi_ref, ws_ref, wp_ref, bias_ref, rate_ref, skip_ref, seg_ref,
    y_ref, gate_ref, c_ref, e_ref, pay_ref, val_ref, st_ref, stp_ref,
):
    m = pl.program_id(0)
    k = pl.program_id(1)
    inner = y_ref.shape[1]

    @pl.when(k == 0)
    def _():
        gate_ref[...] = jnp.zeros_like(gate_ref)
        val_ref[...] = jnp.zeros_like(val_ref)
        st_ref[...] = jnp.zeros_like(st_ref)
        stp_ref[...] = jnp.zeros_like(stp_ref)

    tokens = tok_ref[...]
    state = c_ref.shape[1]
    gate_ref[...] += contract(tokens, wi_ref[0], ((1,), (0,)))
    val_ref[...] += contract(tokens, wi_ref[1], ((1,), (0,)))
    st_ref[:, 0:state] += contract(tokens, ws_ref[0], ((1,), (0,)))
    st_ref[:, state:] += contract(tokens, ws_ref[1], ((1,), (0,)))
    stp_ref[...] += contract(tokens, wp_ref[...], ((1,), (1,)))

    @pl.when(k == pl.num_programs(1) - 1)
    def _():
        scan_rows(
            m, bias_ref, rate_ref, skip_ref, seg_ref, y_ref, c_ref, e_ref, pay_ref, val_ref, st_ref, stp_ref
        )


def scan_rows(m, bias_ref, rate_ref, skip_ref, seg_ref, y_ref, c_ref, e_ref, pay_ref, val_ref, st_ref, stp_ref):
    rows, inner = y_ref.shape
    heads = bias_ref.shape[1]
    wide = inner // heads
    state = c_ref.shape[1]
    seg = seg_ref[...]
    raw = jnp.transpose(stp_ref[...])[0:heads, :] + as_column(bias_ref[pl.ds(m, 1), :])
    dt = jnp.maximum(raw, 0.0) + jnp.log1p(jnp.exp(-jnp.abs(raw)))
    la = -dt * as_column(rate_ref[pl.ds(m, 1), :])
    skip = as_column(skip_ref[pl.ds(m, 1), :])
    lane = lax.broadcasted_iota(jnp.int32, la.shape, 1)
    run = la
    step = 1
    while step < rows:
        run = run + jnp.where(lane >= step, pltpu.roll(run, step, 1), 0.0)
        step *= 2
    last = jnp.max(seg, axis=1, keepdims=True)
    base = jnp.zeros_like(la)
    for j in range(4):
        base_j = jnp.sum(jnp.where(seg < j, la, 0.0), axis=1, keepdims=True)
        base = jnp.where(seg == j, base_j, base)
    total = jnp.sum(la, axis=1, keepdims=True)
    grow = jnp.exp(run - base)
    keep = jnp.where(seg == last, jnp.exp(jnp.minimum(total - run, 0.0)) * dt, 0.0)
    tail = jnp.exp(jnp.sum(jnp.where(seg == last, la, 0.0), axis=1, keepdims=True))
    cols = jnp.transpose(jnp.concatenate([run, keep], axis=0))
    segf = jnp.broadcast_to(seg.astype(F32), (heads, rows))
    ecol = jnp.transpose(jnp.concatenate([grow, segf], axis=0))
    e_ref[...] = ecol
    values = silu(val_ref[...]).astype(BF16)
    in_map = silu(st_ref[:, 0:state]).astype(BF16)
    out_map = silu(st_ref[:, state:]).astype(BF16)
    c_ref[...] = out_map
    vf = values.astype(F32)
    kept = jnp.concatenate(
        [vf[:, h * wide : (h + 1) * wide] * cols[:, heads + h : heads + h + 1] for h in range(heads)], axis=1
    ).astype(BF16)
    added = contract(kept, in_map, ((0,), (0,)))
    pay_ref[0:inner, :] = added.astype(BF16)
    high = tail.astype(BF16).astype(F32)
    low = tail - high
    meta = jnp.concatenate(
        [
            jnp.broadcast_to(high, (heads, state)),
            jnp.broadcast_to(low, (heads, state)),
            jnp.broadcast_to(last.astype(F32) + 1.0, (8, state)),
        ],
        axis=0,
    )
    pay_ref[inner : inner + 16, :] = meta.astype(BF16)
    blocks = rows // SPAN
    for i in range(blocks):
        t0 = i * SPAN
        acc = [vf[t0 : t0 + SPAN, h * wide : (h + 1) * wide] * skip[h : h + 1, :] for h in range(heads)]
        for j in range(i + 1):
            s0 = j * SPAN
            scores = contract(out_map[t0 : t0 + SPAN], in_map[s0 : s0 + SPAN], ((1,), (1,)))
            same = ecol[t0 : t0 + SPAN, heads : heads + 1] == segf[0:1, s0 : s0 + SPAN]
            if i == j:
                same = same & (
                    lax.broadcasted_iota(jnp.int32, (SPAN, SPAN), 0)
                    >= lax.broadcasted_iota(jnp.int32, (SPAN, SPAN), 1)
                )
            for h in range(heads):
                gap = cols[t0 : t0 + SPAN, h : h + 1] - run[h : h + 1, s0 : s0 + SPAN]
                weight = jnp.exp(jnp.where(same, gap, LOW)) * (scores * dt[h : h + 1, s0 : s0 + SPAN])
                acc[h] = acc[h] + contract(
                    weight.astype(BF16), values[s0 : s0 + SPAN, h * wide : (h + 1) * wide], ((1,), (0,))
                )
        y_ref[t0 : t0 + SPAN, :] = jnp.concatenate(acc, axis=1)


def mix_local(hidden, w_inner, w_state, w_step, bias, rate, skip, seg, chunks=1):
    models, rows, depth = hidden.shape
    inner = w_inner.shape[3]
    state = w_state.shape[3]
    heads = bias.shape[1]
    deep = depth // chunks
    whole = lambda a: pl.BlockSpec(a.shape, lambda m, k: (0,) * a.ndim)
    shapes = ((rows, inner), F32), ((rows, inner), F32), ((rows, state), BF16), ((rows, 2 * heads), F32), (
        (inner + 16, state), BF16)
    return pl.pallas_call(
        mix_kernel,
        grid=(models, chunks),
        in_specs=[
            pl.BlockSpec((None, rows, deep), lambda m, k: (m, 0, k)),
            pl.BlockSpec((None, 2, deep, inner), lambda m, k: (m, 0, k, 0)),
            pl.BlockSpec((None, 2, deep, state), lambda m, k: (m, 0, k, 0)),
            pl.BlockSpec((None, heads, deep), lambda m, k: (m, 0, k)),
            whole(bias), whole(rate), whole(skip), whole(seg),
        ],
        out_specs=[pl.BlockSpec((None,) + shape, lambda m, k: (m, 0, 0)) for shape, _ in shapes],
        out_shape=[jax.ShapeDtypeStruct((models,) + shape, kind) for shape, kind in shapes],
        scratch_shapes=[
            pltpu.VMEM((rows, inner), F32), pltpu.VMEM((rows, 2 * state), F32), pltpu.VMEM((rows, heads), F32)
        ],
        cost_estimate=pl.CostEstimate(flops=10**10, bytes_accessed=16 * 10**6, transcendentals=2 * 10**6),
        name="mix_local",
    )(hidden, w_inner, w_state, w_step, bias, rate, skip, seg)


def gate_kernel(
    pages_ref, flags_ref, y_ref, gate_ref, c_ref, e_ref, r1_ref, r2_ref, r3_ref, r4_ref,
    p0_ref, p1_ref, p2_ref, p3_ref, gain_ref, out0_ref, out1_ref, pick_ref,
):
    m = pl.program_id(0)
    rows, inner = y_ref.shape
    heads = p0_ref.shape[0]
    wide = inner // heads
    state = c_ref.shape[1]
    e_col = e_ref[...]
    seg_col = e_col[:, heads : heads + 1]
    seg_first = e_col[0:1, heads : heads + 1]
    init = [
        p.reshape(inner, state)[...].astype(F32) * flags_ref[j].astype(F32)
        for j, p in enumerate((p0_ref, p1_ref, p2_ref, p3_ref))
    ]
    through = jnp.ones((heads, state), F32)
    parts = [jnp.zeros((wide, state), F32) for _ in range(heads)]
    for r in (r1_ref, r2_ref, r3_ref, r4_ref):
        meta = r[inner : inner + 16, :].astype(F32)
        hit = meta[8:9, :] == seg_first + 1.0
        piece = r[0:inner, :].astype(F32)
        weight = jnp.where(hit, through, 0.0)
        for h in range(heads):
            parts[h] = parts[h] + weight[h : h + 1, :] * piece[h * wide : (h + 1) * wide, :]
        through = jnp.where(hit, through * (meta[0:heads] + meta[heads : 2 * heads]), through)
    prior = jnp.concatenate(parts, axis=0)
    through = jnp.concatenate([jnp.broadcast_to(through[h : h + 1, :], (wide, state)) for h in range(heads)], axis=0)
    out_map = c_ref[...]
    low_id, high_id = jnp.min(seg_col), jnp.max(seg_col)
    pick_ref[...] = jnp.zeros_like(pick_ref)
    for j in range(4):

        @pl.when((low_id <= j) & (high_id >= j))
        def _():
            start = jnp.where(seg_first == float(j), prior + through * init[j], init[j])
            high = start.astype(BF16)
            low = (start - high.astype(F32)).astype(BF16)
            from_state = contract(out_map, high, ((1,), (1,))) + contract(out_map, low, ((1,), (1,)))
            pick_ref[...] = jnp.where(seg_col == float(j), from_state, pick_ref[...])

    picked = pick_ref[...]
    spread = jnp.concatenate([jnp.broadcast_to(e_col[:, h : h + 1], (rows, wide)) for h in range(heads)], axis=1)
    gated = (y_ref[...] + picked * spread) * silu(gate_ref[...])
    square = jnp.sum(gated * gated, axis=1, keepdims=True)
    mixed = (gated * gain_ref[pl.ds(m, 1), :]).astype(BF16)
    lines = to_row(square)
    halves = jnp.concatenate([lines[:, 0:inner], lines[:, inner:]], axis=0)
    extra = jnp.concatenate(pieces(halves) + [jnp.zeros((10, inner), F32)], axis=0).astype(BF16)
    for n, out in enumerate((out0_ref, out1_ref)):

        @pl.when(m == n)
        def _():
            out[0:rows, :] = mixed
            out[rows : rows + 16, :] = extra


def gate_out(pages, flags, y, gate, c, e, recv, pool, gain):
    models, rows, inner = y.shape
    heads = pool.shape[2]
    state = c.shape[2]
    mine = lambda a: pl.BlockSpec((None,) + a.shape[1:], lambda m, pg, fl: (m, 0, 0))
    page = lambda j: pl.BlockSpec(
        (None, None, heads, pool.shape[3], state), lambda m, pg, fl: (m, pg[j], 0, 0, 0)
    )
    return pl.pallas_call(
        gate_kernel,
        grid_spec=pltpu.PrefetchScalarGridSpec(
            num_scalar_prefetch=2,
            grid=(models,),
            in_specs=[mine(y), mine(gate), mine(c), mine(e)]
            + [mine(r) for r in recv]
            + [page(j) for j in range(4)]
            + [pl.BlockSpec(gain.shape, lambda m, pg, fl: (0, 0))],
            out_specs=[pl.BlockSpec((rows + 16, inner), lambda m, pg, fl: (0, 0))] * models,
            scratch_shapes=[pltpu.VMEM((rows, inner), F32)],
        ),
        out_shape=[jax.ShapeDtypeStruct((rows + 16, inner), BF16)] * models,
        cost_estimate=pl.CostEstimate(flops=2 * 10**9, bytes_accessed=2 * 10**7, transcendentals=10**5),
        name="gate_out",
    )(pages, flags, y, gate, c, e, *recv, pool, pool, pool, pool, gain)


def out_kernel(m, at_ref, g0_ref, g1_ref, g2_ref, g3_ref, w_ref, o0_ref, o1_ref, o2_ref, o3_ref, acc_ref, sq_ref):
    rows, width = acc_ref.shape
    inner = g0_ref.shape[1]
    block = rows // 4
    along, across = at_ref[m], at_ref[1 - m]
    gathered = (g0_ref, g1_ref, g2_ref, g3_ref)
    extra = sum(g[rows : rows + 16, :].astype(F32) for g in gathered)
    square = extra[0:2] + extra[2:4] + extra[4:6]
    for n in range(4):
        sq_ref[n : n + 1, :] = square[n // 2 : n // 2 + 1, (n % 2) * block : (n % 2 + 1) * block]
    acc_ref[...] = sum(
        contract(g[0:rows, :], w_ref[lax.rem(along + 4 - k, 4)], ((1,), (0,))) for k, g in enumerate(gathered)
    )
    for k, out in enumerate((o0_ref, o1_ref, o2_ref, o3_ref)):
        at = lax.rem(across + k, 4)
        out[0:block, :] = acc_ref[pl.ds(pl.multiple_of(at * block, block), block), :].astype(BF16)
        line = jnp.concatenate(pieces(sq_ref[pl.ds(at, 1), :]) + [jnp.zeros((1, width - 3 * block), F32)], axis=1)
        out[block : block + 16, :] = jnp.broadcast_to(line, (16, width)).astype(BF16)


def out_blocks(m, at, gathered, w, after=()):
    rows = gathered[0].shape[0] - 16
    width = w.shape[2]
    block = rows // 4
    vm = pl.BlockSpec(memory_space=pltpu.VMEM)
    return pl.pallas_call(
        drop(functools.partial(out_kernel, m), 6, len(after)),
        in_specs=[pl.BlockSpec(memory_space=pltpu.SMEM)] + [vm] * 5 + [ANYWHERE] * len(after),
        out_specs=[vm] * 4,
        out_shape=[jax.ShapeDtypeStruct((block + 16, width), BF16)] * 4,
        scratch_shapes=[pltpu.VMEM((rows, width), F32), pltpu.VMEM((4, block), F32)],
        cost_estimate=pl.CostEstimate(flops=10**9, bytes_accessed=10**7, transcendentals=0),
        compiler_params=pltpu.CompilerParams(vmem_limit_bytes=14 * 2**20),
        name="out_blocks",
    )(at, *gathered, w, *after)


def residual_kernel(m, units, at_ref, o0_ref, o1_ref, o2_ref, o3_ref, hid_ref, gain_ref, out_ref):
    block, width = hid_ref.shape
    total = sum(o[...].astype(F32) for o in (o0_ref, o1_ref, o2_ref, o3_ref))
    line = total[block : block + 1, :]
    square = line[:, 0:block] + line[:, block : 2 * block] + line[:, 2 * block : 3 * block]
    scale = to_column(lax.rsqrt(square / units + NORM_EPS))
    res = hid_ref[...].astype(F32) + total[0:block, :] * scale
    out_ref[0:block, :] = (res * gain_ref[m : m + 1, :]).astype(BF16)
    line = jnp.concatenate(
        pieces(to_row(jnp.sum(res * res, axis=1, keepdims=True))) + [jnp.zeros((1, width - 3 * block), F32)], axis=1
    )
    out_ref[block : block + 16, :] = jnp.broadcast_to(line, (16, width)).astype(BF16)


def residual_block(m, at, parts, hidden, gain, units, after=()):
    block, width = parts[0].shape[0] - 16, parts[0].shape[1]
    whole = pl.BlockSpec((block + 16, width), lambda g, at: (0, 0))
    return pl.pallas_call(
        drop(functools.partial(residual_kernel, m, float(units)), 7, len(after)),
        grid_spec=pltpu.PrefetchScalarGridSpec(
            num_scalar_prefetch=1,
            grid=(1,),
            in_specs=[whole] * 4
            + [
                pl.BlockSpec((block, width), lambda g, at: (0, 0)),
                pl.BlockSpec((2, width), lambda g, at: (0, at[m])),
            ]
            + [ANYWHERE] * len(after),
            out_specs=whole,
        ),
        out_shape=jax.ShapeDtypeStruct((block + 16, width), BF16),
        cost_estimate=pl.CostEstimate(flops=10**6, bytes_accessed=9 * 10**6, transcendentals=100),
        compiler_params=pltpu.CompilerParams(vmem_limit_bytes=8 * 2**20),
        name="residual_block",
    )(at, *parts, hidden, gain, *after)


def join_kernel(m, at_ref, u0_ref, u1_ref, u2_ref, u3_ref, out_ref):
    block, width = u0_ref.shape[0] - 16, u0_ref.shape[1]
    square = jnp.zeros((1, block), F32)
    half = block // 2
    for k, u in enumerate((u0_ref, u1_ref, u2_ref, u3_ref)):
        at = pl.multiple_of(lax.rem(at_ref[m] + 4 - k, 4) * width, width)
        for n in range(2):
            out_ref[n * (half + 8) + 8 : (n + 1) * (half + 8), pl.ds(at, width)] = u[n * half : (n + 1) * half, :]
        line = u[block : block + 16, :].astype(F32)[0:1, :]
        square = square + line[:, 0:block] + line[:, block : 2 * block] + line[:, 2 * block : 3 * block]
    parts = pieces(lax.rsqrt(square / out_ref.shape[1] + NORM_EPS))
    for n in range(2):
        line = jnp.concatenate(
            [p[:, n * half : (n + 1) * half] for p in parts] + [jnp.zeros((1, 256 - 3 * half), F32)], axis=1
        )
        out_ref[n * (half + 8) : n * (half + 8) + 8, 0:256] = jnp.broadcast_to(line, (8, 256)).astype(BF16)
        out_ref[n * (half + 8) : n * (half + 8) + 8, 256:] = jnp.zeros((8, out_ref.shape[1] - 256), BF16)


def join_columns(m, at, parts, after=()):
    tall, width = parts[0].shape
    vm = pl.BlockSpec(memory_space=pltpu.VMEM)
    return pl.pallas_call(
        drop(functools.partial(join_kernel, m), 5, len(after)),
        in_specs=[pl.BlockSpec(memory_space=pltpu.SMEM)] + [vm] * 4 + [ANYWHERE] * len(after),
        out_specs=vm,
        out_shape=jax.ShapeDtypeStruct((tall, 4 * width), BF16),
        cost_estimate=pl.CostEstimate(flops=10**5, bytes_accessed=6 * 10**6, transcendentals=100),
        compiler_params=pltpu.CompilerParams(vmem_limit_bytes=8 * 2**20),
        name="join_columns",
    )(at, *parts, *after)


def fetch_kernel(w_ref, out_ref, sems):
    depth = w_ref.shape[1]
    half = depth // 2
    copies = [
        pltpu.make_async_copy(
            w_ref.at[m, pl.ds(n * half, half), :], out_ref.at[m, pl.ds(n * half, half), :], sems.at[2 * m + n]
        )
        for m in range(2)
        for n in range(2)
    ]
    for copy in copies:
        copy.start()
    for copy in copies:
        copy.wait()


def fetched(head, after):
    return pl.pallas_call(
        drop(fetch_kernel, 1, len(after)),
        in_specs=[ANYWHERE] + [ANYWHERE] * len(after),
        out_specs=pl.BlockSpec(memory_space=pltpu.VMEM),
        out_shape=pltpu.VMEM(head.shape, head.dtype),
        scratch_shapes=[pltpu.SemaphoreType.DMA((4,))],
        compiler_params=pltpu.CompilerParams(vmem_limit_bytes=40 * 2**20),
        cost_estimate=pl.CostEstimate(flops=0, bytes_accessed=3 * 10**7, transcendentals=0),
        name="fetched",
    )(head, *after)


def score_rows(m, halves, places, base, w_ref, tgt_ref, acc_ref, put):
    half = halves[0].shape[0] - 8
    block = 2 * half
    rows = jnp.concatenate([x[8 : half + 8, :] for x in halves], axis=0)
    acc_ref[0 : rows.shape[0], :] = contract(rows, w_ref[m], ((1,), (0,)))
    for k, at in enumerate(places):
        lines = [x[0:8, 0:256].astype(F32)[0:1, :] for x in halves[2 * k : 2 * k + 2]]
        scale = to_column(
            jnp.concatenate(
                [v[:, 0:half] + v[:, half : 2 * half] + v[:, 2 * half : 3 * half] for v in lines], axis=1
            )
        )
        raw = acc_ref[k * block : (k + 1) * block, :]
        top = jnp.max(raw, axis=1, keepdims=True)
        total = jnp.sum(jnp.exp2((raw - top) * (scale * LOG2E)), axis=1, keepdims=True)
        target = to_column((tgt_ref[pl.ds(at, 1), :] - base).astype(F32)).astype(jnp.int32)
        column = lax.broadcasted_iota(jnp.int32, raw.shape, 1)
        chosen = jnp.sum(jnp.where(column == target, raw, 0.0), axis=1, keepdims=True) * scale
        put(m * 8 + at, to_row(top * scale + jnp.log(total)))
        put(m * 8 + 4 + at, to_row(chosen))


def near_kernel(place_ref, at_ref, *refs):
    w_ref, tgt_ref, out_ref, acc_ref = refs[6:]
    half = refs[0].shape[0] // 2
    base = place_ref[0] * w_ref.shape[2]

    def put(row, value):
        out_ref[pl.ds(row, 1), :] = value

    for m in range(2):
        tiles = refs[3 * m : 3 * m + 3]
        halves = [x.at[pl.ds(n * half, half), :] for x in tiles for n in range(2)]
        places = [lax.rem(at_ref[1 - m] + 4 - k, 4) for k in (0, 1, 3)]
        score_rows(m, halves, places, base, w_ref, tgt_ref, acc_ref, put)


def far_kernel(place_ref, at_ref, *refs):
    w_ref, tgt_ref, near_ref, out_ref, acc_ref = refs[4:]
    base = place_ref[0] * w_ref.shape[2]
    out_ref[...] = jnp.broadcast_to(near_ref[...][None], out_ref.shape)

    def put(row, value):
        out_ref[:, pl.ds(row, 1), :] = jnp.broadcast_to(value[None], (out_ref.shape[0], 1, value.shape[1]))

    for m in range(2):
        places = [lax.rem(at_ref[1 - m] + 2, 4)]
        score_rows(m, refs[2 * m : 2 * m + 2], places, base, w_ref, tgt_ref, acc_ref, put)


def head_stats(place, at, near, cut, head, tgt, group):
    tall, depth = near[0][0].shape
    block = tall - 16
    vocab = head.shape[2]
    vm = pl.BlockSpec(memory_space=pltpu.VMEM)
    sm = pl.BlockSpec(memory_space=pltpu.SMEM)
    common = dict(out_specs=vm, compiler_params=pltpu.CompilerParams(vmem_limit_bytes=24 * 2**20))
    cost = lambda blocks: pl.CostEstimate(
        flops=4 * blocks * block * depth * vocab, bytes_accessed=10**7, transcendentals=2 * blocks * block * vocab
    )
    first = pl.pallas_call(
        near_kernel,
        in_specs=[sm] * 2 + [vm] * 8,
        scratch_shapes=[pltpu.VMEM((3 * block, vocab), F32)],
        out_shape=jax.ShapeDtypeStruct((16, block), F32),
        cost_estimate=cost(3),
        name="head_near",
        **common,
    )(place, at, *near[0], *near[1], head, tgt)
    return pl.pallas_call(
        far_kernel,
        in_specs=[sm] * 2 + [vm] * 7,
        scratch_shapes=[pltpu.VMEM((block, vocab), F32)],
        out_shape=jax.ShapeDtypeStruct((group, 16, block), F32),
        cost_estimate=cost(1),
        name="head_far",
        **common,
    )(place, at, *cut[0], *cut[1], head, tgt, first)


def cut_kernel(a_ref, b_ref, c_ref, d_ref, oa_ref, ob_ref, oc_ref, od_ref):
    oa_ref[...] = a_ref[...]
    ob_ref[...] = b_ref[...]
    oc_ref[...] = c_ref[...]
    od_ref[...] = d_ref[...]


def cut_halves(pairs, after):
    tall, depth = pairs[0][0].shape
    low = pl.BlockSpec((tall // 2, depth), lambda g: (0, 0))
    high = pl.BlockSpec((tall // 2, depth), lambda g: (1, 0))
    return pl.pallas_call(
        drop(cut_kernel, 4, len(after)),
        grid=(1,),
        in_specs=[low, high] * 2 + [ANYWHERE] * len(after),
        out_specs=[low] * 4,
        out_shape=[jax.ShapeDtypeStruct((tall // 2, depth), BF16)] * 4,
        compiler_params=pltpu.CompilerParams(vmem_limit_bytes=8 * 2**20),
        cost_estimate=pl.CostEstimate(flops=0, bytes_accessed=2 * 10**6, transcendentals=0),
        name="cut_halves",
    )(*pairs[0], *pairs[1], *after)


def diff_kernel(stat_ref, live_ref, seg_ref, diff_ref, sums_ref):
    scores = []
    for m in range(2):
        part = stat_ref[:, 8 * m : 8 * m + 8, :]
        lse = part[:, 0:4, :]
        top = jnp.max(lse, axis=0)
        total = top + jnp.log(jnp.sum(jnp.exp(lse - top[None]), axis=0))
        scores.append(jnp.sum(part[:, 4:8, :], axis=0) - total)
    lines = lax.broadcasted_iota(jnp.int32, (4, 128), 0)
    alive = jnp.where(lines < 2, live_ref[0].astype(F32), live_ref[1].astype(F32))
    diff = alive * (scores[0] - scores[1])
    diff_ref[...] = diff
    which = lax.broadcasted_iota(jnp.int32, (8, 128), 0)
    sums = jnp.zeros((8, 128), F32)
    for j in range(4):
        mine = jnp.sum(jnp.where(seg_ref[...] == j, diff, 0.0), axis=1, keepdims=True)
        sums = jnp.where(which == j, jnp.sum(mine, axis=0, keepdims=True), sums)
    sums_ref[...] = sums


def token_diffs(stats, live, seg):
    vm = pl.BlockSpec(memory_space=pltpu.VMEM)
    return pl.pallas_call(
        diff_kernel,
        in_specs=[vm, pl.BlockSpec(memory_space=pltpu.SMEM), vm],
        out_shape=(jax.ShapeDtypeStruct((4, 128), F32), jax.ShapeDtypeStruct((8, 128), F32)),
        name="token_diffs",
    )(stats, live, seg)


def turn_kernel(at_ref, w_ref, hid_ref, w0_ref, w1_ref, h0_ref, h1_ref):
    width = w0_ref.shape[2]
    for m, (out, mine) in enumerate(((w0_ref, h0_ref), (w1_ref, h1_ref))):

        @pl.when(pl.program_id(0) == m)
        def _():
            for j in range(4):
                out[j] = w_ref[:, j * width : (j + 1) * width]
            mine[...] = hid_ref[...]


def turned(at, w_out, hidden):
    models, inner, depth = w_out.shape
    width = depth // 4
    block = hidden.shape[1] // 4
    return pl.pallas_call(
        turn_kernel,
        grid_spec=pltpu.PrefetchScalarGridSpec(
            num_scalar_prefetch=1,
            grid=(models,),
            in_specs=[
                pl.BlockSpec((None, inner, depth), lambda m, at: (m, 0, 0)),
                pl.BlockSpec((None, block, width), lambda m, at: (m, at[1 - m], at[m])),
            ],
            out_specs=[pl.BlockSpec((4, inner, width), lambda m, at: (0, 0, 0))] * 2
            + [pl.BlockSpec((block, width), lambda m, at: (0, 0))] * 2,
        ),
        out_shape=[jax.ShapeDtypeStruct((4, inner, width), w_out.dtype)] * 2
        + [jax.ShapeDtypeStruct((block, width), hidden.dtype)] * 2,
        cost_estimate=pl.CostEstimate(flops=0, bytes_accessed=10**7, transcendentals=0),
        name="turned",
    )(at, w_out, hidden)


def ring(value, axis, by):
    return lax.ppermute(value, axis, [(i, (i + by) % 4) for i in range(4)])


def gathered(value, axis):
    return [value] + [ring(value, axis, k) for k in (1, 2, 3)]


def per_device(
    hidden, w_inner, w_state, w_step, step_bias, rate, skip_gain, norm_gain, w_out, final_gain, head, pool,
    targets, segment_ids, flags, pages, live, owners,
):
    rows = targets.shape[0]
    depth = hidden.shape[2]
    inner = w_inner.shape[3]
    group = lax.axis_size(VOC)
    devices = lax.axis_size(SEQ)
    place = lax.axis_index(VOC).astype(jnp.int32).reshape(1)
    seg = segment_ids.reshape(1, rows)
    tgt = targets.reshape(4, rows // 4)
    w_inner = jnp.swapaxes(w_inner, 1, 2)
    w_state = jnp.swapaxes(w_state, 1, 2)
    w_step = jnp.swapaxes(w_step, 1, 2)
    ways = (("x", "z"), ("z", "x"))
    both = range(2)
    at = jnp.stack([lax.axis_index("x"), lax.axis_index("z")]).astype(jnp.int32)
    turns = turned(at, w_out, hidden)
    weights = [lax.all_to_all(turns[m], ways[m][0], 0, 0) for m in both]
    y, gate, c, e, pay = mix_local(hidden, w_inner, w_state, w_step, step_bias, rate, skip_gain, seg)
    recv = [lax.ppermute(pay, SEQ, [(i, i + k) for i in range(devices - k)]) for k in range(1, REACH + 1)]
    parts, res, full = [], [], []
    gated = gate_out(pages, flags, y, gate, c, e, recv, pool, norm_gain)
    for m in both:
        out = out_blocks(m, at, gathered(gated[m], ways[m][0]), weights[m])
        parts.append([out[0]] + [ring(out[k], ways[m][1], k) for k in (1, 2, 3)])
    for m in both:
        res.append(residual_block(m, at, parts[m], turns[2 + m], final_gain, inner * group, (parts[1][0],)))
    blocks = [gathered(res[m], ways[m][0]) for m in both]
    for m in both:
        full.append(join_columns(m, at, blocks[m], tuple(blocks[1 - m][1:])))
    ready = fetched(head, tuple(full))
    near = [[full[m]] + [ring(full[m], ways[m][1], k) for k in (1, 3)] for m in both]
    halves = cut_halves([near[m][1:] for m in both], (ready,))
    cut = [[ring(halves[2 * m], ways[m][1], 1), ring(halves[2 * m + 1], ways[m][1], 3)] for m in both]
    merged = lax.all_to_all(head_stats(place, at, near, cut, ready, tgt, group), VOC, 0, 0)
    diff, sums = token_diffs(merged, live, segment_ids.reshape(4, 128))
    sums = sums + lax.ppermute(sums, "core", [(0, 1), (1, 0)])
    sums = sum(gathered(sums, "y"))[0:4, 0]
    owned = jnp.where(owners == lax.axis_index(SEQ), sums, 0.0)
    return diff.reshape(rows), owned[None]


def solution(mesh):
    seq, vocab = mesh.devices.shape
    fine = Mesh(mesh.devices.reshape(seq // 2, 2, 4, vocab // 4), ("y", "core", "x", "z"))
    placed = (
        P(None, SEQ, None),
        P(None, None, None, VOC),
        P(),
        P(None, None, VOC),
        P(None, VOC),
        P(None, VOC),
        P(None, VOC),
        P(None, VOC),
        P(None, VOC, None),
        P(),
        P(None, None, VOC),
        P(None, None, VOC, None, None),
        P(SEQ),
        P(SEQ),
        P(),
        P(),
        P(SEQ),
        P(),
    )
    return jax.shard_map(
        per_device, mesh=fine, in_specs=placed, out_specs=(P(SEQ), P(SEQ, None)), check_vma=False
    )
```

```python
import functools

import jax
import jax.numpy as jnp
from jax import lax
from jax.experimental import pallas as pl
from jax.experimental.pallas import tpu as pltpu
from jax.sharding import Mesh
from jax.sharding import PartitionSpec as P

NORM_EPS = 1e-05
SPAN = 256
REACH = 4
SEQ = ("y", "core")
VOC = ("x", "z")
F32 = jnp.float32
BF16 = jnp.bfloat16
LOW = -1e30
LOG2E = 1.4426950408889634


def silu(v):
    return v / (1.0 + jnp.exp(-v))


def contract(a, b, dims):
    return lax.dot_general(a, b, (dims, ((), ())), preferred_element_type=F32)


def drop(kernel, inputs, count):
    def body(*refs):
        return kernel(*refs[:inputs], *refs[inputs + count :])

    return body


ANYWHERE = pl.BlockSpec(memory_space=pl.ANY)


def pieces(value):
    high = value.astype(BF16).astype(F32)
    mid = (value - high).astype(BF16).astype(F32)
    return [high, mid, value - high - mid]


def to_column(row):
    return jnp.transpose(jnp.broadcast_to(row, (8, row.shape[1])))[:, 0:1]


def to_row(column):
    return jnp.transpose(jnp.broadcast_to(column, (column.shape[0], 8)))[0:1, :]


def as_column(row):
    count = row.shape[1]
    spread = jnp.broadcast_to(row, (count, count))
    eye = lax.broadcasted_iota(jnp.int32, spread.shape, 0) == lax.broadcasted_iota(jnp.int32, spread.shape, 1)
    return jnp.sum(jnp.where(eye, spread, 0.0), axis=1, keepdims=True)


def mix_kernel(
    tok_ref, wi_ref, ws_ref, wp_ref, bias_ref, rate_ref, skip_ref, seg_ref,
    y_ref, gate_ref, c_ref, e_ref, pay_ref, val_ref, st_ref, stp_ref,
):
    m = pl.program_id(0)
    k = pl.program_id(1)
    inner = y_ref.shape[1]

    @pl.when(k == 0)
    def _():
        gate_ref[...] = jnp.zeros_like(gate_ref)
        val_ref[...] = jnp.zeros_like(val_ref)
        st_ref[...] = jnp.zeros_like(st_ref)
        stp_ref[...] = jnp.zeros_like(stp_ref)

    tokens = tok_ref[...]
    state = c_ref.shape[1]
    gate_ref[...] += contract(tokens, wi_ref[0], ((1,), (0,)))
    val_ref[...] += contract(tokens, wi_ref[1], ((1,), (0,)))
    st_ref[:, 0:state] += contract(tokens, ws_ref[0], ((1,), (0,)))
    st_ref[:, state:] += contract(tokens, ws_ref[1], ((1,), (0,)))
    stp_ref[...] += contract(tokens, wp_ref[...], ((1,), (1,)))

    @pl.when(k == pl.num_programs(1) - 1)
    def _():
        scan_rows(
            m, bias_ref, rate_ref, skip_ref, seg_ref, y_ref, c_ref, e_ref, pay_ref, val_ref, st_ref, stp_ref
        )


def scan_rows(m, bias_ref, rate_ref, skip_ref, seg_ref, y_ref, c_ref, e_ref, pay_ref, val_ref, st_ref, stp_ref):
    rows, inner = y_ref.shape
    heads = bias_ref.shape[1]
    wide = inner // heads
    state = c_ref.shape[1]
    seg = seg_ref[...]
    raw = jnp.transpose(stp_ref[...])[0:heads, :] + as_column(bias_ref[pl.ds(m, 1), :])
    dt = jnp.maximum(raw, 0.0) + jnp.log1p(jnp.exp(-jnp.abs(raw)))
    la = -dt * as_column(rate_ref[pl.ds(m, 1), :])
    skip = as_column(skip_ref[pl.ds(m, 1), :])
    lane = lax.broadcasted_iota(jnp.int32, la.shape, 1)
    run = la
    step = 1
    while step < rows:
        run = run + jnp.where(lane >= step, pltpu.roll(run, step, 1), 0.0)
        step *= 2
    last = jnp.max(seg, axis=1, keepdims=True)
    base = jnp.zeros_like(la)
    for j in range(4):
        base_j = jnp.sum(jnp.where(seg < j, la, 0.0), axis=1, keepdims=True)
        base = jnp.where(seg == j, base_j, base)
    total = jnp.sum(la, axis=1, keepdims=True)
    grow = jnp.exp(run - base)
    keep = jnp.where(seg == last, jnp.exp(jnp.minimum(total - run, 0.0)) * dt, 0.0)
    tail = jnp.exp(jnp.sum(jnp.where(seg == last, la, 0.0), axis=1, keepdims=True))
    run = run * LOG2E
    cols = jnp.transpose(jnp.concatenate([run, keep, dt, dt], axis=0))
    segf = jnp.broadcast_to(seg.astype(F32), (heads, rows))
    ecol = jnp.transpose(jnp.concatenate([grow, segf], axis=0))
    e_ref[...] = ecol
    values = silu(val_ref[...]).astype(BF16)
    in_map = silu(st_ref[:, 0:state]).astype(BF16)
    out_map = silu(st_ref[:, state:]).astype(BF16)
    c_ref[...] = out_map
    vf = values.astype(F32)
    kept = jnp.concatenate(
        [vf[:, h * wide : (h + 1) * wide] * cols[:, heads + h : heads + h + 1] for h in range(heads)], axis=1
    ).astype(BF16)
    added = contract(kept, in_map, ((0,), (0,)))
    pay_ref[0:inner, :] = added.astype(BF16)
    high = tail.astype(BF16).astype(F32)
    low = tail - high
    meta = jnp.concatenate(
        [
            jnp.broadcast_to(high, (heads, state)),
            jnp.broadcast_to(low, (heads, state)),
            jnp.broadcast_to(last.astype(F32) + 1.0, (8, state)),
        ],
        axis=0,
    )
    pay_ref[inner : inner + 16, :] = meta.astype(BF16)
    timed = jnp.concatenate(
        [vf[:, h * wide : (h + 1) * wide] * cols[:, 2 * heads + h : 2 * heads + h + 1] for h in range(heads)], axis=1
    ).astype(BF16)
    blocks = rows // SPAN
    for i in range(blocks):
        t0 = i * SPAN
        acc = [vf[t0 : t0 + SPAN, h * wide : (h + 1) * wide] * skip[h : h + 1, :] for h in range(heads)]
        for j in range(i + 1):
            s0 = j * SPAN
            scores = contract(out_map[t0 : t0 + SPAN], in_map[s0 : s0 + SPAN], ((1,), (1,)))
            same = ecol[t0 : t0 + SPAN, heads : heads + 1] == segf[0:1, s0 : s0 + SPAN]
            if i == j:
                same = same & (
                    lax.broadcasted_iota(jnp.int32, (SPAN, SPAN), 0)
                    >= lax.broadcasted_iota(jnp.int32, (SPAN, SPAN), 1)
                )
            for h in range(heads):
                gap = cols[t0 : t0 + SPAN, h : h + 1] - run[h : h + 1, s0 : s0 + SPAN]
                weight = jnp.exp2(jnp.where(same, gap, LOW)) * scores
                acc[h] = acc[h] + contract(
                    weight.astype(BF16), timed[s0 : s0 + SPAN, h * wide : (h + 1) * wide], ((1,), (0,))
                )
        y_ref[t0 : t0 + SPAN, :] = jnp.concatenate(acc, axis=1)


def mix_local(hidden, w_inner, w_state, w_step, bias, rate, skip, seg, chunks=1):
    models, rows, depth = hidden.shape
    inner = w_inner.shape[3]
    state = w_state.shape[3]
    heads = bias.shape[1]
    deep = depth // chunks
    whole = lambda a: pl.BlockSpec(a.shape, lambda m, k: (0,) * a.ndim)
    shapes = ((rows, inner), F32), ((rows, inner), F32), ((rows, state), BF16), ((rows, 2 * heads), F32), (
        (inner + 16, state), BF16)
    return pl.pallas_call(
        mix_kernel,
        grid=(models, chunks),
        in_specs=[
            pl.BlockSpec((None, rows, deep), lambda m, k: (m, 0, k)),
            pl.BlockSpec((None, 2, deep, inner), lambda m, k: (m, 0, k, 0)),
            pl.BlockSpec((None, 2, deep, state), lambda m, k: (m, 0, k, 0)),
            pl.BlockSpec((None, heads, deep), lambda m, k: (m, 0, k)),
            whole(bias), whole(rate), whole(skip), whole(seg),
        ],
        out_specs=[pl.BlockSpec((None,) + shape, lambda m, k: (m, 0, 0)) for shape, _ in shapes],
        out_shape=[jax.ShapeDtypeStruct((models,) + shape, kind) for shape, kind in shapes],
        scratch_shapes=[
            pltpu.VMEM((rows, inner), F32), pltpu.VMEM((rows, 2 * state), F32), pltpu.VMEM((rows, heads), F32)
        ],
        cost_estimate=pl.CostEstimate(flops=10**10, bytes_accessed=16 * 10**6, transcendentals=2 * 10**6),
        name="mix_local",
    )(hidden, w_inner, w_state, w_step, bias, rate, skip, seg)


def gate_kernel(
    pages_ref, flags_ref, y_ref, gate_ref, c_ref, e_ref, r1_ref, r2_ref, r3_ref, r4_ref,
    p0_ref, p1_ref, p2_ref, p3_ref, gain_ref, out0_ref, out1_ref, pick_ref,
):
    m = pl.program_id(0)
    rows, inner = y_ref.shape
    heads = p0_ref.shape[0]
    wide = inner // heads
    state = c_ref.shape[1]
    e_col = e_ref[...]
    seg_col = e_col[:, heads : heads + 1]
    seg_first = e_col[0:1, heads : heads + 1]
    init = [
        p.reshape(inner, state)[...].astype(F32) * flags_ref[j].astype(F32)
        for j, p in enumerate((p0_ref, p1_ref, p2_ref, p3_ref))
    ]
    through = jnp.ones((heads, state), F32)
    parts = [jnp.zeros((wide, state), F32) for _ in range(heads)]
    for r in (r1_ref, r2_ref, r3_ref, r4_ref):
        meta = r[inner : inner + 16, :].astype(F32)
        hit = meta[8:9, :] == seg_first + 1.0
        piece = r[0:inner, :].astype(F32)
        weight = jnp.where(hit, through, 0.0)
        for h in range(heads):
            parts[h] = parts[h] + weight[h : h + 1, :] * piece[h * wide : (h + 1) * wide, :]
        through = jnp.where(hit, through * (meta[0:heads] + meta[heads : 2 * heads]), through)
    prior = jnp.concatenate(parts, axis=0)
    through = jnp.concatenate([jnp.broadcast_to(through[h : h + 1, :], (wide, state)) for h in range(heads)], axis=0)
    out_map = c_ref[...]
    low_id, high_id = jnp.min(seg_col), jnp.max(seg_col)
    pick_ref[...] = jnp.zeros_like(pick_ref)
    for j in range(4):

        @pl.when((low_id <= j) & (high_id >= j))
        def _():
            start = jnp.where(seg_first == float(j), prior + through * init[j], init[j])
            high = start.astype(BF16)
            low = (start - high.astype(F32)).astype(BF16)
            from_state = contract(out_map, high, ((1,), (1,))) + contract(out_map, low, ((1,), (1,)))
            pick_ref[...] = jnp.where(seg_col == float(j), from_state, pick_ref[...])

    picked = pick_ref[...]
    spread = jnp.concatenate([jnp.broadcast_to(e_col[:, h : h + 1], (rows, wide)) for h in range(heads)], axis=1)
    gated = (y_ref[...] + picked * spread) * silu(gate_ref[...])
    square = jnp.sum(gated * gated, axis=1, keepdims=True)
    mixed = (gated * gain_ref[pl.ds(m, 1), :]).astype(BF16)
    lines = to_row(square)
    halves = jnp.concatenate([lines[:, 0:inner], lines[:, inner:]], axis=0)
    extra = jnp.concatenate(pieces(halves) + [jnp.zeros((10, inner), F32)], axis=0).astype(BF16)
    for n, out in enumerate((out0_ref, out1_ref)):

        @pl.when(m == n)
        def _():
            out[0:rows, :] = mixed
            out[rows : rows + 16, :] = extra


def gate_out(pages, flags, y, gate, c, e, recv, pool, gain):
    models, rows, inner = y.shape
    heads = pool.shape[2]
    state = c.shape[2]
    mine = lambda a: pl.BlockSpec((None,) + a.shape[1:], lambda m, pg, fl: (m, 0, 0))
    page = lambda j: pl.BlockSpec(
        (None, None, heads, pool.shape[3], state), lambda m, pg, fl: (m, pg[j], 0, 0, 0)
    )
    return pl.pallas_call(
        gate_kernel,
        grid_spec=pltpu.PrefetchScalarGridSpec(
            num_scalar_prefetch=2,
            grid=(models,),
            in_specs=[mine(y), mine(gate), mine(c), mine(e)]
            + [mine(r) for r in recv]
            + [page(j) for j in range(4)]
            + [pl.BlockSpec(gain.shape, lambda m, pg, fl: (0, 0))],
            out_specs=[pl.BlockSpec((rows + 16, inner), lambda m, pg, fl: (0, 0))] * models,
            scratch_shapes=[pltpu.VMEM((rows, inner), F32)],
        ),
        out_shape=[jax.ShapeDtypeStruct((rows + 16, inner), BF16)] * models,
        cost_estimate=pl.CostEstimate(flops=2 * 10**9, bytes_accessed=2 * 10**7, transcendentals=10**5),
        name="gate_out",
    )(pages, flags, y, gate, c, e, *recv, pool, pool, pool, pool, gain)


def out_kernel(m, at_ref, g0_ref, g1_ref, g2_ref, g3_ref, w_ref, o0_ref, o1_ref, o2_ref, o3_ref, acc_ref, sq_ref):
    rows, width = acc_ref.shape
    inner = g0_ref.shape[1]
    block = rows // 4
    along, across = at_ref[m], at_ref[1 - m]
    gathered = (g0_ref, g1_ref, g2_ref, g3_ref)
    extra = sum(g[rows : rows + 16, :].astype(F32) for g in gathered)
    square = extra[0:2] + extra[2:4] + extra[4:6]
    for n in range(4):
        sq_ref[n : n + 1, :] = square[n // 2 : n // 2 + 1, (n % 2) * block : (n % 2 + 1) * block]
    acc_ref[...] = sum(
        contract(g[0:rows, :], w_ref[lax.rem(along + 4 - k, 4)], ((1,), (0,))) for k, g in enumerate(gathered)
    )
    for k, out in enumerate((o0_ref, o1_ref, o2_ref, o3_ref)):
        at = lax.rem(across + k, 4)
        out[0:block, :] = acc_ref[pl.ds(pl.multiple_of(at * block, block), block), :].astype(BF16)
        line = jnp.concatenate(pieces(sq_ref[pl.ds(at, 1), :]) + [jnp.zeros((1, width - 3 * block), F32)], axis=1)
        out[block : block + 16, :] = jnp.broadcast_to(line, (16, width)).astype(BF16)


def out_blocks(m, at, gathered, w, after=()):
    rows = gathered[0].shape[0] - 16
    width = w.shape[2]
    block = rows // 4
    vm = pl.BlockSpec(memory_space=pltpu.VMEM)
    return pl.pallas_call(
        drop(functools.partial(out_kernel, m), 6, len(after)),
        in_specs=[pl.BlockSpec(memory_space=pltpu.SMEM)] + [vm] * 5 + [ANYWHERE] * len(after),
        out_specs=[vm] * 4,
        out_shape=[jax.ShapeDtypeStruct((block + 16, width), BF16)] * 4,
        scratch_shapes=[pltpu.VMEM((rows, width), F32), pltpu.VMEM((4, block), F32)],
        cost_estimate=pl.CostEstimate(flops=10**9, bytes_accessed=10**7, transcendentals=0),
        compiler_params=pltpu.CompilerParams(vmem_limit_bytes=14 * 2**20),
        name="out_blocks",
    )(at, *gathered, w, *after)


def residual_kernel(m, units, at_ref, o0_ref, o1_ref, o2_ref, o3_ref, hid_ref, gain_ref, out_ref):
    block, width = hid_ref.shape
    total = sum(o[...].astype(F32) for o in (o0_ref, o1_ref, o2_ref, o3_ref))
    line = total[block : block + 1, :]
    square = line[:, 0:block] + line[:, block : 2 * block] + line[:, 2 * block : 3 * block]
    scale = to_column(lax.rsqrt(square / units + NORM_EPS))
    res = hid_ref[...].astype(F32) + total[0:block, :] * scale
    out_ref[0:block, :] = (res * gain_ref[m : m + 1, :]).astype(BF16)
    line = jnp.concatenate(
        pieces(to_row(jnp.sum(res * res, axis=1, keepdims=True))) + [jnp.zeros((1, width - 3 * block), F32)], axis=1
    )
    out_ref[block : block + 16, :] = jnp.broadcast_to(line, (16, width)).astype(BF16)


def residual_block(m, at, parts, hidden, gain, units, after=()):
    block, width = parts[0].shape[0] - 16, parts[0].shape[1]
    whole = pl.BlockSpec((block + 16, width), lambda g, at: (0, 0))
    return pl.pallas_call(
        drop(functools.partial(residual_kernel, m, float(units)), 7, len(after)),
        grid_spec=pltpu.PrefetchScalarGridSpec(
            num_scalar_prefetch=1,
            grid=(1,),
            in_specs=[whole] * 4
            + [
                pl.BlockSpec((block, width), lambda g, at: (0, 0)),
                pl.BlockSpec((2, width), lambda g, at: (0, at[m])),
            ]
            + [ANYWHERE] * len(after),
            out_specs=whole,
        ),
        out_shape=jax.ShapeDtypeStruct((block + 16, width), BF16),
        cost_estimate=pl.CostEstimate(flops=10**6, bytes_accessed=9 * 10**6, transcendentals=100),
        compiler_params=pltpu.CompilerParams(vmem_limit_bytes=8 * 2**20),
        name="residual_block",
    )(at, *parts, hidden, gain, *after)


def join_kernel(m, at_ref, u0_ref, u1_ref, u2_ref, u3_ref, out_ref):
    block, width = u0_ref.shape[0] - 16, u0_ref.shape[1]
    square = jnp.zeros((1, block), F32)
    half = block // 2
    for k, u in enumerate((u0_ref, u1_ref, u2_ref, u3_ref)):
        at = pl.multiple_of(lax.rem(at_ref[m] + 4 - k, 4) * width, width)
        for n in range(2):
            out_ref[n * (half + 8) + 8 : (n + 1) * (half + 8), pl.ds(at, width)] = u[n * half : (n + 1) * half, :]
        line = u[block : block + 16, :].astype(F32)[0:1, :]
        square = square + line[:, 0:block] + line[:, block : 2 * block] + line[:, 2 * block : 3 * block]
    parts = pieces(lax.rsqrt(square / out_ref.shape[1] + NORM_EPS))
    for n in range(2):
        line = jnp.concatenate(
            [p[:, n * half : (n + 1) * half] for p in parts] + [jnp.zeros((1, 256 - 3 * half), F32)], axis=1
        )
        out_ref[n * (half + 8) : n * (half + 8) + 8, 0:256] = jnp.broadcast_to(line, (8, 256)).astype(BF16)
        out_ref[n * (half + 8) : n * (half + 8) + 8, 256:] = jnp.zeros((8, out_ref.shape[1] - 256), BF16)


def join_columns(m, at, parts, after=()):
    tall, width = parts[0].shape
    vm = pl.BlockSpec(memory_space=pltpu.VMEM)
    return pl.pallas_call(
        drop(functools.partial(join_kernel, m), 5, len(after)),
        in_specs=[pl.BlockSpec(memory_space=pltpu.SMEM)] + [vm] * 4 + [ANYWHERE] * len(after),
        out_specs=vm,
        out_shape=jax.ShapeDtypeStruct((tall, 4 * width), BF16),
        cost_estimate=pl.CostEstimate(flops=10**5, bytes_accessed=6 * 10**6, transcendentals=100),
        compiler_params=pltpu.CompilerParams(vmem_limit_bytes=8 * 2**20),
        name="join_columns",
    )(at, *parts, *after)


def fetch_kernel(w_ref, out_ref, sems):
    depth = w_ref.shape[1]
    half = depth // 2
    copies = [
        pltpu.make_async_copy(
            w_ref.at[m, pl.ds(n * half, half), :], out_ref.at[m, pl.ds(n * half, half), :], sems.at[2 * m + n]
        )
        for m in range(2)
        for n in range(2)
    ]
    for copy in copies:
        copy.start()
    for copy in copies:
        copy.wait()


def fetched(head, after):
    return pl.pallas_call(
        drop(fetch_kernel, 1, len(after)),
        in_specs=[ANYWHERE] + [ANYWHERE] * len(after),
        out_specs=pl.BlockSpec(memory_space=pltpu.VMEM),
        out_shape=pltpu.VMEM(head.shape, head.dtype),
        scratch_shapes=[pltpu.SemaphoreType.DMA((4,))],
        compiler_params=pltpu.CompilerParams(vmem_limit_bytes=40 * 2**20),
        cost_estimate=pl.CostEstimate(flops=0, bytes_accessed=3 * 10**7, transcendentals=0),
        name="fetched",
    )(head, *after)


def score_rows(m, halves, places, base, w_ref, tgt_ref, acc_ref, put):
    half = halves[0].shape[0] - 8
    block = 2 * half
    rows = jnp.concatenate([x[8 : half + 8, :] for x in halves], axis=0)
    acc_ref[0 : rows.shape[0], :] = contract(rows, w_ref[m], ((1,), (0,)))
    for k, at in enumerate(places):
        lines = [x[0:8, 0:256].astype(F32)[0:1, :] for x in halves[2 * k : 2 * k + 2]]
        scale = to_column(
            jnp.concatenate(
                [v[:, 0:half] + v[:, half : 2 * half] + v[:, 2 * half : 3 * half] for v in lines], axis=1
            )
        )
        raw = acc_ref[k * block : (k + 1) * block, :]
        top = jnp.max(raw, axis=1, keepdims=True)
        total = jnp.sum(jnp.exp2((raw - top) * (scale * LOG2E)), axis=1, keepdims=True)
        target = to_column((tgt_ref[pl.ds(at, 1), :] - base).astype(F32)).astype(jnp.int32)
        column = lax.broadcasted_iota(jnp.int32, raw.shape, 1)
        chosen = jnp.sum(jnp.where(column == target, raw, 0.0), axis=1, keepdims=True) * scale
        put(m * 8 + at, to_row(top * scale + jnp.log(total)))
        put(m * 8 + 4 + at, to_row(chosen))


def own_kernel(place_ref, at_ref, x0_ref, x1_ref, w_ref, tgt_ref, out_ref, acc_ref):
    half = x0_ref.shape[0] // 2
    base = place_ref[0] * w_ref.shape[2]
    out_ref[...] = jnp.zeros_like(out_ref)

    def put(row, value):
        out_ref[pl.ds(row, 1), :] = value

    for m, x in enumerate((x0_ref, x1_ref)):
        halves = [x.at[pl.ds(n * half, half), :] for n in range(2)]
        score_rows(m, halves, [at_ref[1 - m]], base, w_ref, tgt_ref, acc_ref, put)


def near_kernel(place_ref, at_ref, *refs):
    w_ref, tgt_ref, own_ref, out_ref, acc_ref = refs[4:]
    half = refs[0].shape[0] // 2
    base = place_ref[0] * w_ref.shape[2]
    out_ref[...] = own_ref[...]

    def put(row, value):
        out_ref[pl.ds(row, 1), :] = value

    for m in range(2):
        tiles = refs[2 * m : 2 * m + 2]
        halves = [x.at[pl.ds(n * half, half), :] for x in tiles for n in range(2)]
        places = [lax.rem(at_ref[1 - m] + 4 - k, 4) for k in (1, 3)]
        score_rows(m, halves, places, base, w_ref, tgt_ref, acc_ref, put)


def far_kernel(place_ref, at_ref, *refs):
    w_ref, tgt_ref, near_ref, out_ref, acc_ref = refs[4:]
    base = place_ref[0] * w_ref.shape[2]
    out_ref[...] = jnp.broadcast_to(near_ref[...][None], out_ref.shape)

    def put(row, value):
        out_ref[:, pl.ds(row, 1), :] = jnp.broadcast_to(value[None], (out_ref.shape[0], 1, value.shape[1]))

    for m in range(2):
        places = [lax.rem(at_ref[1 - m] + 2, 4)]
        score_rows(m, refs[2 * m : 2 * m + 2], places, base, w_ref, tgt_ref, acc_ref, put)


def head_stats(place, at, near, cut, head, tgt, group):
    tall, depth = near[0][0].shape
    block = tall - 16
    vocab = head.shape[2]
    vm = pl.BlockSpec(memory_space=pltpu.VMEM)
    sm = pl.BlockSpec(memory_space=pltpu.SMEM)
    common = dict(out_specs=vm, compiler_params=pltpu.CompilerParams(vmem_limit_bytes=24 * 2**20))
    cost = lambda blocks: pl.CostEstimate(
        flops=4 * blocks * block * depth * vocab, bytes_accessed=10**7, transcendentals=2 * blocks * block * vocab
    )
    own = pl.pallas_call(
        own_kernel,
        in_specs=[sm] * 2 + [vm] * 4,
        scratch_shapes=[pltpu.VMEM((block, vocab), F32)],
        out_shape=jax.ShapeDtypeStruct((16, block), F32),
        cost_estimate=cost(1),
        name="head_own",
        **common,
    )(place, at, near[0][0], near[1][0], head, tgt)
    first = pl.pallas_call(
        near_kernel,
        in_specs=[sm] * 2 + [vm] * 7,
        scratch_shapes=[pltpu.VMEM((2 * block, vocab), F32)],
        out_shape=jax.ShapeDtypeStruct((16, block), F32),
        cost_estimate=cost(2),
        name="head_near",
        **common,
    )(place, at, *near[0][1:], *near[1][1:], head, tgt, own)
    return pl.pallas_call(
        far_kernel,
        in_specs=[sm] * 2 + [vm] * 7,
        scratch_shapes=[pltpu.VMEM((block, vocab), F32)],
        out_shape=jax.ShapeDtypeStruct((group, 16, block), F32),
        cost_estimate=cost(1),
        name="head_far",
        **common,
    )(place, at, *cut[0], *cut[1], head, tgt, first)


def cut_kernel(a_ref, b_ref, c_ref, d_ref, oa_ref, ob_ref, oc_ref, od_ref):
    oa_ref[...] = a_ref[...]
    ob_ref[...] = b_ref[...]
    oc_ref[...] = c_ref[...]
    od_ref[...] = d_ref[...]


def cut_halves(pairs, after):
    tall, depth = pairs[0][0].shape
    low = pl.BlockSpec((tall // 2, depth), lambda g: (0, 0))
    high = pl.BlockSpec((tall // 2, depth), lambda g: (1, 0))
    return pl.pallas_call(
        drop(cut_kernel, 4, len(after)),
        grid=(1,),
        in_specs=[low, high] * 2 + [ANYWHERE] * len(after),
        out_specs=[low] * 4,
        out_shape=[jax.ShapeDtypeStruct((tall // 2, depth), BF16)] * 4,
        compiler_params=pltpu.CompilerParams(vmem_limit_bytes=8 * 2**20),
        cost_estimate=pl.CostEstimate(flops=0, bytes_accessed=2 * 10**6, transcendentals=0),
        name="cut_halves",
    )(*pairs[0], *pairs[1], *after)


def diff_kernel(stat_ref, live_ref, seg_ref, diff_ref, sums_ref):
    scores = []
    for m in range(2):
        part = stat_ref[:, 8 * m : 8 * m + 8, :]
        lse = part[:, 0:4, :]
        top = jnp.max(lse, axis=0)
        total = top + jnp.log(jnp.sum(jnp.exp(lse - top[None]), axis=0))
        scores.append(jnp.sum(part[:, 4:8, :], axis=0) - total)
    lines = lax.broadcasted_iota(jnp.int32, (4, 128), 0)
    alive = jnp.where(lines < 2, live_ref[0].astype(F32), live_ref[1].astype(F32))
    diff = alive * (scores[0] - scores[1])
    diff_ref[...] = diff
    which = lax.broadcasted_iota(jnp.int32, (8, 128), 0)
    sums = jnp.zeros((8, 128), F32)
    for j in range(4):
        mine = jnp.sum(jnp.where(seg_ref[...] == j, diff, 0.0), axis=1, keepdims=True)
        sums = jnp.where(which == j, jnp.sum(mine, axis=0, keepdims=True), sums)
    sums_ref[...] = sums


def token_diffs(stats, live, seg):
    vm = pl.BlockSpec(memory_space=pltpu.VMEM)
    return pl.pallas_call(
        diff_kernel,
        in_specs=[vm, pl.BlockSpec(memory_space=pltpu.SMEM), vm],
        out_shape=(jax.ShapeDtypeStruct((4, 128), F32), jax.ShapeDtypeStruct((8, 128), F32)),
        name="token_diffs",
    )(stats, live, seg)


def turn_kernel(at_ref, w_ref, hid_ref, w0_ref, w1_ref, h0_ref, h1_ref):
    width = w0_ref.shape[2]
    for m, (out, mine) in enumerate(((w0_ref, h0_ref), (w1_ref, h1_ref))):

        @pl.when(pl.program_id(0) == m)
        def _():
            for j in range(4):
                out[j] = w_ref[:, j * width : (j + 1) * width]
            mine[...] = hid_ref[...]


def turned(at, w_out, hidden):
    models, inner, depth = w_out.shape
    width = depth // 4
    block = hidden.shape[1] // 4
    return pl.pallas_call(
        turn_kernel,
        grid_spec=pltpu.PrefetchScalarGridSpec(
            num_scalar_prefetch=1,
            grid=(models,),
            in_specs=[
                pl.BlockSpec((None, inner, depth), lambda m, at: (m, 0, 0)),
                pl.BlockSpec((None, block, width), lambda m, at: (m, at[1 - m], at[m])),
            ],
            out_specs=[pl.BlockSpec((4, inner, width), lambda m, at: (0, 0, 0))] * 2
            + [pl.BlockSpec((block, width), lambda m, at: (0, 0))] * 2,
        ),
        out_shape=[jax.ShapeDtypeStruct((4, inner, width), w_out.dtype)] * 2
        + [jax.ShapeDtypeStruct((block, width), hidden.dtype)] * 2,
        cost_estimate=pl.CostEstimate(flops=0, bytes_accessed=10**7, transcendentals=0),
        name="turned",
    )(at, w_out, hidden)


def ring(value, axis, by):
    return lax.ppermute(value, axis, [(i, (i + by) % 4) for i in range(4)])


def gathered(value, axis):
    return [value] + [ring(value, axis, k) for k in (1, 2, 3)]


def per_device(
    hidden, w_inner, w_state, w_step, step_bias, rate, skip_gain, norm_gain, w_out, final_gain, head, pool,
    targets, segment_ids, flags, pages, live, owners,
):
    rows = targets.shape[0]
    depth = hidden.shape[2]
    inner = w_inner.shape[3]
    group = lax.axis_size(VOC)
    devices = lax.axis_size(SEQ)
    place = lax.axis_index(VOC).astype(jnp.int32).reshape(1)
    seg = segment_ids.reshape(1, rows)
    tgt = targets.reshape(4, rows // 4)
    w_inner = jnp.swapaxes(w_inner, 1, 2)
    w_state = jnp.swapaxes(w_state, 1, 2)
    w_step = jnp.swapaxes(w_step, 1, 2)
    ways = (("x", "z"), ("z", "x"))
    both = range(2)
    at = jnp.stack([lax.axis_index("x"), lax.axis_index("z")]).astype(jnp.int32)
    turns = turned(at, w_out, hidden)
    weights = [lax.all_to_all(turns[m], ways[m][0], 0, 0) for m in both]
    y, gate, c, e, pay = mix_local(hidden, w_inner, w_state, w_step, step_bias, rate, skip_gain, seg)
    recv = [lax.ppermute(pay, SEQ, [(i, i + k) for i in range(devices - k)]) for k in range(1, REACH + 1)]
    parts, res, full = [], [], []
    gated = gate_out(pages, flags, y, gate, c, e, recv, pool, norm_gain)
    for m in both:
        out = out_blocks(m, at, gathered(gated[m], ways[m][0]), weights[m])
        parts.append([out[0]] + [ring(out[k], ways[m][1], k) for k in (1, 2, 3)])
    for m in both:
        res.append(residual_block(m, at, parts[m], turns[2 + m], final_gain, inner * group, (parts[1][0],)))
    blocks = [gathered(res[m], ways[m][0]) for m in both]
    for m in both:
        full.append(join_columns(m, at, blocks[m], tuple(blocks[1 - m][1:])))
    ready = fetched(head, tuple(full))
    near = [[full[m]] + [ring(full[m], ways[m][1], k) for k in (1, 3)] for m in both]
    halves = cut_halves([near[m][1:] for m in both], (ready,))
    cut = [[ring(halves[2 * m], ways[m][1], 1), ring(halves[2 * m + 1], ways[m][1], 3)] for m in both]
    merged = lax.all_to_all(head_stats(place, at, near, cut, ready, tgt, group), VOC, 0, 0)
    diff, sums = token_diffs(merged, live, segment_ids.reshape(4, 128))
    sums = sums + lax.ppermute(sums, "core", [(0, 1), (1, 0)])
    sums = sum(gathered(sums, "y"))[0:4, 0]
    owned = jnp.where(owners == lax.axis_index(SEQ), sums, 0.0)
    return diff.reshape(rows), owned[None]


def solution(mesh):
    seq, vocab = mesh.devices.shape
    fine = Mesh(mesh.devices.reshape(seq // 2, 2, 4, vocab // 4), ("y", "core", "x", "z"))
    placed = (
        P(None, SEQ, None),
        P(None, None, None, VOC),
        P(),
        P(None, None, VOC),
        P(None, VOC),
        P(None, VOC),
        P(None, VOC),
        P(None, VOC),
        P(None, VOC, None),
        P(),
        P(None, None, VOC),
        P(None, None, VOC, None, None),
        P(SEQ),
        P(SEQ),
        P(),
        P(),
        P(SEQ),
        P(),
    )
    return jax.shard_map(
        per_device, mesh=fine, in_specs=placed, out_specs=(P(SEQ), P(SEQ, None)), check_vma=False
    )
```
